256 devices in a mesh: mem: 64 (over z, x_lo, y), band: 4 (over x_hi, core).
Axes of the slice: x: 4 (x_hi: 2, x_lo: 2; x = x_hi * 2 + x_lo), y: 4, z: 8, core: 2. Of those that a mesh axis runs over, the one named last changes fastest.
Arguments:
- alpha: bfloat16 [128, 4, 320, 720], P('mem', None, 'band'), may hold values from -6 to 6
- static_ctl: bfloat16 [4, 320, 720], P(None, 'band'), may hold values from -6 to 6
- perturbations: bfloat16 [128, 4, 320, 720], P('mem', None, None, 'band'), may hold values from -16 to 16
- static_std: float32 [4, 320, 720], P(None, None, 'band'), may hold values from 0.5 to 2
- lon_root: bfloat16 [720, 720], replicated, may hold values from -0.11 to 1.11
- lat_root: bfloat16 [320, 320], replicated, may hold values from -0.11 to 1.11
- jacobian: bfloat16 [32, 4, 320, 720], P(None, None, 'mem', 'band'), may hold values from -3 to 3
- obs_count: int32 [320, 720], P('mem', 'band'), may hold values from 1 to 6
- channel_mask: int32 [32, 320, 720], P(None, 'mem', 'band'), may hold values 0 or 1
- channel_error: float32 [32], replicated, may hold values from 1 to 2
- member_weight: int32 [128], replicated, may hold values from 1 to 4
Outputs:
- grad_alpha: float32 [128, 4, 320, 720], P('mem', None, 'band')
- grad_static: float32 [4, 320, 720], P(None, 'band')
The draws below stay inside these ranges and needn't reach their ends.
All inputs are finite; a program needn't handle non-finite values. No bound on the sum of `channel_mask` on one device may be relied on, other than what follows from the above.
Results may differ from the reference program's by a relative error of at most 0.0055.
Values may be sent and summed in bfloat16 or wider, within the bound.
A program may use at most 64 MiB of HBM per device.

```python
import math
import jax
import jax.numpy as jnp
from jax import lax

S = 4
CH = 32
LAT = 320
LON = 720
MEM = 128


def root_matrix(key, count, periodic):
    index = jnp.arange(count)
    gap = jnp.abs(index[:, None] - index[None, :])
    if periodic:
        gap = jnp.minimum(gap, count - gap)
    reach = count / 2.0
    shape = jnp.exp(-(gap.astype(jnp.float32) / reach) ** 2)
    rough = jax.random.uniform(key, (count, count), jnp.float32, -1.0, 1.0)
    matrix = jnp.eye(count, dtype=jnp.float32) + 0.8 / math.sqrt(count) * shape * rough
    return matrix.astype(jnp.bfloat16)


def draw_lon_root(key, part):
    return root_matrix(jax.random.fold_in(key, 11), LON, True)


def draw_lat_root(key, part):
    return root_matrix(jax.random.fold_in(key, 23), LAT, False)


def touch_ends(array, key, smallest, high):
    spot = [jax.random.randint(jax.random.fold_in(key, axis), (), 0, length) for axis, length in enumerate(array.shape)]
    widest = array.shape.index(max(array.shape))
    next_to = spot[:widest] + [(spot[widest] + 1) % array.shape[widest]] + spot[widest + 1:]
    return array.at[tuple(spot)].set(smallest).at[tuple(next_to)].set(high)


def raised(array, stream_key, source, target, blocks, factor):
    owner, partner = [(jnp.arange(array.shape[axis_at]) // (array.shape[axis_at] // blocks)).reshape([-1 if axis == axis_at else 1 for axis in range(array.ndim)]) for axis_at in (source, target)]
    chosen = jax.random.permutation(stream_key, blocks)[partner]
    strong = (owner == chosen) | (owner == (partner + blocks // 2) % blocks)
    return jnp.where(strong, factor * array, array)


def block_scale(rng, shape, shards, smallest, high):
    gain, own = 1.0, jax.random.fold_in(rng, 6)
    for position, shards_of in shards:
        steps = jnp.exp(jax.random.uniform(jax.random.fold_in(own, position), (shards_of,), jnp.float32, smallest / len(shards), high / len(shards)))
        gain = gain * jnp.repeat(steps, shape[position] // shards_of).reshape([-1 if axis == position else 1 for axis in range(len(shape))])
    return gain


def gaussian(rng, shape, scale, most, split=(), kind=jnp.bfloat16):
    values = scale * jax.random.normal(rng, shape, jnp.float32)
    if split:
        values = values * block_scale(rng, shape, split, -0.22, 0.18)
    return jnp.clip(values, -most, most).astype(kind)


def heavy_noise(own_key, extent, scale, bound, shards, heavy, held_as=jnp.bfloat16):
    result = scale * jax.random.normal(own_key, extent, jnp.float32)
    if shards:
        result = result * block_scale(own_key, extent, shards, -0.22, 0.18)
    return jnp.clip(raised(result, jax.random.fold_in(own_key, 3), *heavy), -bound, bound).astype(held_as)


def setup_inputs(seed: int = 0) -> dict:
    key_of = jax.random.split(jax.random.key(seed), 12)
    alpha = gaussian(key_of[0], (MEM, S, LAT, LON), 1.0, 6.0, ((0, 64), (2, 4)))
    static_ctl = gaussian(key_of[1], (S, LAT, LON), 1.0, 6.0, ((1, 4),))
    perturbations = heavy_noise(key_of[2], (MEM, S, LAT, LON), 1.0, 16.0, ((0, 64), (3, 4)), (0, 2, 64, 4.0))
    static_std = jnp.clip(jnp.exp(math.log(2.0) - 1.3862944 * jax.random.uniform(key_of[3], (S, LAT, LON), jnp.float32) ** block_scale(key_of[3], (S, LAT, LON), ((2, 4),), -0.2, 0.2)), 0.5, 2.0)
    lon_root = draw_lon_root(jax.random.fold_in(key_of[11], 71), 0)
    lat_root = draw_lat_root(jax.random.fold_in(key_of[11], 71), 0)
    jacobian = gaussian(key_of[6], (CH, S, LAT, LON), S ** -0.5, 3.0, ((2, 64), (3, 4)))
    obs_count = touch_ends(jax.random.randint(key_of[7], (LAT, LON), 1, 7), jax.random.fold_in(key_of[7], 1), 1, 6).astype(jnp.int32)
    channel_mask = touch_ends((jax.random.randint(key_of[8], (CH, LAT, LON), 0, 4) < 3).astype(jnp.int32), jax.random.fold_in(key_of[8], 1), 0, 1)
    channel_error = jnp.clip(jnp.exp(jax.random.uniform(key_of[9], (CH,), jnp.float32, math.log(1.0), math.log(2.0))), 1.0, 2.0)
    member_weight = touch_ends(jax.random.randint(key_of[10], (MEM,), 1, 5), jax.random.fold_in(key_of[10], 1), 1, 4).astype(jnp.int32)
    return {"alpha": alpha, "static_ctl": static_ctl, "perturbations": perturbations, "static_std": static_std, "lon_root": lon_root, "lat_root": lat_root, "jacobian": jacobian, "obs_count": obs_count, "channel_mask": channel_mask, "channel_error": channel_error, "member_weight": member_weight}


def correlate(field, lon_root, lat_root):
    along_lon = jnp.dot(field, lon_root, preferred_element_type=jnp.float32).astype(jnp.bfloat16)
    return jnp.einsum('ij,sjk->sik', lat_root.astype(jnp.float32), along_lon.astype(jnp.float32))

def correlate_adjoint(field, lon_root, lat_root):
    back_lat = jnp.einsum('ji,sjk->sik', lat_root.astype(jnp.float32), field.astype(jnp.float32)).astype(jnp.bfloat16)
    return jnp.einsum('sil,jl->sij', back_lat.astype(jnp.float32), lon_root.astype(jnp.float32))

def reference(alpha, static_ctl, perturbations, static_std, lon_root, lat_root, jacobian, obs_count, channel_mask, channel_error, member_weight):
    weights = member_weight.astype(jnp.float32)
    coef = weights / jnp.sqrt(jnp.sum(weights * weights))

    def add_member(total, item):
        field, spread, factor = item
        term = 0.8 * factor * spread.astype(jnp.float32) * correlate(field, lon_root, lat_root)
        return (total + term, None)
    start = jnp.zeros((S, LAT, LON), jnp.float32)
    ensemble_sum, _ = lax.scan(add_member, start, (alpha, perturbations, coef))
    increment = ensemble_sum + 0.6 * static_std * correlate(static_ctl, lon_root, lat_root)
    obs_weight = channel_mask.astype(jnp.float32) * obs_count.astype(jnp.float32)[None] / (channel_error * channel_error)[:, None, None]
    jac_full = jacobian.astype(jnp.float32)
    radiance = lax.optimization_barrier(jnp.sum(jac_full * increment[None], axis=1))
    obs_gradient = lax.optimization_barrier(jnp.sum(jac_full * (obs_weight * radiance)[:, None], axis=0)).astype(jnp.bfloat16)
    gradient_full = obs_gradient.astype(jnp.float32)

    def member_grad(item):
        field, spread, factor = item
        adjoint_field = (0.8 * factor * spread.astype(jnp.float32) * gradient_full).astype(jnp.bfloat16)
        return field.astype(jnp.float32) + correlate_adjoint(adjoint_field, lon_root, lat_root)
    grad_alpha = lax.map(member_grad, (alpha, perturbations, coef))
    static_adjoint = (0.6 * static_std * gradient_full).astype(jnp.bfloat16)
    grad_static = static_ctl.astype(jnp.float32) + correlate_adjoint(static_adjoint, lon_root, lat_root)
    return (grad_alpha, grad_static)
```

```python
import functools

import jax
import jax.numpy as jnp
import numpy as np
from jax import lax
from jax.experimental import pallas as pl
from jax.experimental.pallas import tpu as pltpu
from jax.sharding import PartitionSpec as P

MESH = pl.DeviceIdType.MESH
F32, BF16 = jnp.float32, jnp.bfloat16

S, CH, MEMB, FIELDS = 4, 32, 2, 3
ROWS, LAT, LON, COLS = 80, 320, 720, 180
REM = COLS - 128
QN, ZN, OWN, PAD = 8, 8, 5, 48
PERM = QN * PAD
PAIR, WIDE = 384, 768


def row_order():
    order = np.zeros((PERM, LAT), np.float32)
    for q in range(QN):
        for z in range(ZN):
            for k in range(OWN):
                order[q * PAD + z * OWN + k, 40 * z + 5 * q + k] = 1.0
    return order


def low_half(shape):
    return lax.broadcasted_iota(jnp.int32, shape, len(shape) - 1) < 64


def joined(even, odd):
    return jnp.where(low_half(even.shape), even, pltpu.roll(odd, 64, 1))


def joined_high(even, odd):
    return jnp.where(low_half(even.shape), pltpu.roll(even, 64, 1), odd)


def kernel(
    alpha_hbm, static_hbm, pert_hbm, std_hbm, w_hbm, lat_hbm, jac_hbm, count_hbm, mask_hbm, order_hbm, order_t_hbm,
    error_ref, weight_ref,
    ga_hbm, gs_hbm,
    alpha, static, pert, std, w, lat, jac, count, mask, order, order_t,
    fs, xr, ss, sr, rs, r1, s2, r2, gz, gzr, cbuf, ag, bs, br, lhs, out,
    spread, packed, rem, latp, latpt, incs, gu,
    load_sem, store_sem, f_send, f_recv, t_send, t_recv, a_send, a_recv, b_send, b_recv, c_send, c_recv, d_send, d_recv,
    e_send, e_recv,
):
    mem, band = lax.axis_index("mem"), lax.axis_index("band")
    z, q = mem // QN, lax.rem(mem, QN)

    bands = [lax.rem(band + k, 4) for k in range(1, 4)]
    to_band = [{"mem": mem, "band": b} for b in bands]
    qs = [lax.rem(q + k, QN) for k in range(1, QN)]
    to_q = [{"mem": z * QN + t, "band": band} for t in qs]
    zs = [lax.rem(z + k, ZN) for k in range(1, ZN)]
    to_z = [{"mem": t * QN + q, "band": band} for t in zs]

    staged = [(alpha_hbm, alpha), (w_hbm, w), (static_hbm, static), (lat_hbm, lat), (order_hbm, order),
              (order_t_hbm, order_t), (pert_hbm, pert), (std_hbm, std), (jac_hbm, jac), (count_hbm, count), (mask_hbm, mask)]
    loads = [pltpu.make_async_copy(src, dst, load_sem.at[i]) for i, (src, dst) in enumerate(staged)]
    for load in loads:
        load.start()

    barrier = pltpu.get_barrier_semaphore()
    partners = to_band + to_q + to_z
    for device in partners:
        pl.semaphore_signal(barrier, inc=1, device_id=device, device_id_type=MESH)

    def remote(src, dst, send, recv, device):
        return pltpu.make_async_remote_copy(
            src_ref=src, dst_ref=dst, send_sem=send, recv_sem=recv, device_id=device, device_id_type=MESH)

    sent = []

    forward = []
    loads[0].wait()
    loads[1].wait()
    for p in range(2):
        rows = alpha[:, 2 * p : 2 * p + 2].reshape(4 * ROWS, LON)
        y = jnp.dot(rows, w[...], preferred_element_type=F32).reshape(MEMB, 2, ROWS, WIDE)
        for m in range(MEMB):
            even, odd = y[m, 0], y[m, 1]
            for b in range(4):
                t = 512 + 128 * (b // 2)
                join = joined if b % 2 == 0 else joined_high
                fs[p, b, m, :, 0:128] = even[:, 128 * b : 128 * b + 128].astype(BF16)
                fs[p, b, m, :, 128:256] = odd[:, 128 * b : 128 * b + 128].astype(BF16)
                fs[p, b, m, :, 256:384] = join(even[:, t : t + 128], odd[:, t : t + 128]).astype(BF16)
        if p == 0:
            pl.semaphore_wait(barrier, len(partners))
        copies = [
            remote(fs.at[p, bands[k]], xr.at[p, :, band], f_send.at[p, k], f_recv.at[p, k], to_band[k]) for k in range(3)]
        for copy in copies:
            copy.start()
        forward.append(copies)
        xr[p, :, band] = fs[p, band]

    loads[2].wait()
    loads[3].wait()
    y = jnp.dot(static[...].reshape(S * ROWS, LON), w[...], preferred_element_type=F32).astype(BF16)
    own = (lax.broadcasted_iota(jnp.int32, (16, LAT), 1) == OWN * mem + lax.broadcasted_iota(jnp.int32, (16, LAT), 0)) & (
        lax.broadcasted_iota(jnp.int32, (16, LAT), 0) < OWN)
    own_rows = jnp.dot(jnp.where(own, 1.0, 0.0).astype(BF16), lat[...], preferred_element_type=F32).astype(BF16)
    here = lax.broadcasted_iota(jnp.int32, (LAT, ROWS), 0) == ROWS * band + lax.broadcasted_iota(jnp.int32, (LAT, ROWS), 1)
    own_part = jnp.dot(own_rows, jnp.where(here, 1.0, 0.0).astype(BF16), preferred_element_type=F32).astype(BF16)
    parts = [jnp.dot(own_part, y[ROWS * s : ROWS * s + ROWS], preferred_element_type=F32)[0:8] for s in range(S)]
    for b in range(4):
        t = 512 + 128 * (b // 2)
        join = joined if b % 2 == 0 else joined_high
        for p in range(2):
            for s in range(2):
                ss[b, :, PAIR * p + 128 * s : PAIR * p + 128 * s + 128] = parts[2 * p + s][:, 128 * b : 128 * b + 128]
            ss[b, :, PAIR * p + 256 : PAIR * p + 384] = join(parts[2 * p][:, t : t + 128], parts[2 * p + 1][:, t : t + 128])
    static_copies = [
        remote(ss.at[bands[k]], sr.at[band], t_send.at[k], t_recv.at[k], to_band[k]) for k in range(3)]
    for copy in static_copies:
        copy.start()
    sr[band] = ss[band]

    loads[4].wait()
    loads[5].wait()
    latp[...] = jnp.dot(order[...], lat[...], preferred_element_type=F32).astype(BF16)
    lat_t = jnp.transpose(lat[...].astype(F32)).astype(BF16)
    latpt[...] = jnp.dot(lat_t, order_t[...], preferred_element_type=F32).astype(BF16)
    weights = weight_ref[...].astype(F32)
    coef = weights / jnp.sqrt(jnp.sum(weights * weights, axis=1, keepdims=True))
    lane = lax.broadcasted_iota(jnp.int32, coef.shape, 1)
    rem[...] = jnp.zeros_like(rem)

    def pack(source):
        for p in range(2):
            for s in range(2):
                packed[:, PAIR * p + 128 * s : PAIR * p + 128 * s + 128] = source(2 * p + s, 0, 128).astype(F32)
                rem[s, :, 0:REM] = source(2 * p + s, 128, COLS).astype(F32)
            packed[:, PAIR * p + 256 : PAIR * p + 384] = joined(rem[0], rem[1])

    loads[6].wait()
    for m in range(MEMB):
        pack(lambda s, lo, hi: pert[m, s, :, lo:hi])
        factor = 0.8 * jnp.sum(jnp.where(lane == MEMB * mem + m, coef, 0.0), axis=1, keepdims=True)
        spread[m] = factor * jnp.dot(order[...], packed[...].astype(BF16), preferred_element_type=F32)
    loads[7].wait()
    pack(lambda s, lo, hi: std[s, :, lo:hi])
    spread[MEMB] = 0.6 * jnp.dot(
        order[...].astype(F32), packed[...], preferred_element_type=F32, precision=lax.Precision.HIGHEST)
    own_std = 0.6 * jnp.dot(
        jnp.where(own, 1.0, 0.0), packed[...], preferred_element_type=F32, precision=lax.Precision.HIGHEST)[0:8]

    first = []
    for p in range(2):
        for copy in forward[p]:
            copy.wait_recv()
        total = None
        for m in range(MEMB):
            field = jnp.dot(latp[...], xr[p, m].reshape(LAT, PAIR), preferred_element_type=F32)
            term = spread[m, :, PAIR * p : PAIR * p + PAIR] * field
            total = term if total is None else total + term
        rs[p] = total.astype(BF16).reshape(QN, PAD, PAIR)
        copies = [
            remote(rs.at[p, qs[k]], r1.at[p, k], a_send.at[p, k], a_recv.at[p, k], to_q[k]) for k in range(QN - 1)]
        for copy in copies:
            copy.start()
        first.append(copies)
        sent += forward[p]

    second = []
    for p in range(2):
        for copy in first[p]:
            copy.wait_recv()
        total = rs[p, q].astype(F32)
        for k in range(QN - 1):
            total = total + r1[p, k].astype(F32)
        for t in range(ZN):
            s2[p, t, 0:OWN, :] = total[OWN * t : OWN * t + OWN, :]
            s2[p, t, OWN:8, :] = jnp.zeros((8 - OWN, PAIR), F32)
        copies = [
            remote(s2.at[p, zs[k]], r2.at[p, k], b_send.at[p, k], b_recv.at[p, k], to_z[k]) for k in range(ZN - 1)]
        for copy in copies:
            copy.start()
        second.append(copies)
        sent += first[p]

    for copy in static_copies:
        copy.wait_recv()
    sent += static_copies
    own_static = sr[0] + sr[1] + sr[2] + sr[3]
    static_term = own_std * own_static
    loads[8].wait()
    loads[9].wait()
    loads[10].wait()
    for p in range(2):
        for copy in second[p]:
            copy.wait_recv()
        sent += second[p]
        total = s2[p, z]
        for k in range(ZN - 1):
            total = total + r2[p, k]
        total = total + static_term[:, PAIR * p : PAIR * p + PAIR]
        for s in range(2):
            incs[2 * p + s, :, 0:128] = total[:, 128 * s : 128 * s + 128]
            rest = total[:, 256:384]
            incs[2 * p + s, :, 128:256] = rest if s == 0 else pltpu.roll(rest, 64, 1)
    inc = [incs[s, 0:OWN, 0:COLS] for s in range(S)]
    counts = count[...].astype(F32)

    def channel(c, grads):
        jac_c = [jac[c, s].astype(F32) for s in range(S)]
        radiance = (jac_c[0] * inc[0] + jac_c[1] * inc[1]) + (jac_c[2] * inc[2] + jac_c[3] * inc[3])
        error = jnp.full((OWN, COLS), error_ref[c], F32)
        weighted = mask[c].astype(F32) * counts / (error * error) * radiance
        return tuple(grads[s] + jac_c[s] * weighted for s in range(S))

    grads = lax.fori_loop(0, CH, channel, tuple(jnp.zeros((OWN, COLS), F32) for _ in range(S)))
    gu[...] = jnp.zeros_like(gu)
    for s in range(S):
        gu[s, 0:OWN, 0:COLS] = grads[s].astype(BF16).astype(F32)
    for p in range(2):
        for s in range(2):
            gz[:, PAIR * p + 128 * s : PAIR * p + 128 * s + 128] = gu[2 * p + s, :, 0:128]
        gz[:, PAIR * p + 256 : PAIR * p + 384] = joined(gu[2 * p, :, 128:256], gu[2 * p + 1, :, 128:256])

    third = [remote(gz, gzr.at[z], c_send.at[k], c_recv.at[k], to_z[k]) for k in range(ZN - 1)]
    for copy in third:
        copy.start()
    gzr[z] = gz[...]
    for copy in third:
        copy.wait_recv()
    sent += third
    for t in range(ZN):
        cbuf[OWN * t : OWN * t + OWN, :] = gzr[t, 0:OWN, :]
    cbuf[OWN * ZN : PAD, :] = jnp.zeros((PAD - OWN * ZN, WIDE), F32)
    ag[q] = cbuf[...].astype(BF16)
    fourth = [remote(ag.at[q], ag.at[q], d_send.at[k], d_recv.at[k], to_q[k]) for k in range(QN - 1)]
    for copy in fourth:
        copy.start()
    for copy in fourth:
        copy.wait_recv()
    sent += fourth

    gradient = ag[...].reshape(PERM, WIDE).astype(F32)
    back = []
    for m in range(FIELDS):
        adjoint = (spread[m] * gradient).astype(BF16)
        bs[m] = jnp.dot(latpt[...], adjoint, preferred_element_type=F32).astype(BF16).reshape(4, ROWS, WIDE)
        copies = [
            remote(bs.at[m, bands[k]], br.at[m, band], e_send.at[m, k], e_recv.at[m, k], to_band[k]) for k in range(3)]
        for copy in copies:
            copy.start()
        back.append(copies)
        br[m, band] = bs[m, band]

    stores = []
    for m in range(FIELDS):
        for copy in back[m]:
            copy.wait_recv()
        sent += back[m]
        for p in range(2):
            tiles = [br[m, b, :, PAIR * p + 256 : PAIR * p + 384].astype(F32) for b in range(4)]
            for s in range(2):
                rows = pl.ds((2 * p + s) * ROWS, ROWS)
                for b in range(4):
                    lhs[rows, 128 * b : 128 * b + 128] = br[m, b, :, PAIR * p + 128 * s : PAIR * p + 128 * s + 128]
                join = joined if s == 0 else joined_high
                for t in range(2):
                    lhs[rows, 512 + 128 * t : 640 + 128 * t] = join(tiles[2 * t], tiles[2 * t + 1]).astype(BF16)
        y = lax.dot_general(lhs[...], w[...], (((1,), (1,)), ((), ())), preferred_element_type=F32)
        base = alpha[m] if m < MEMB else static[...]
        out[m] = base.astype(F32) + y.reshape(S, ROWS, LON)
        store = pltpu.make_async_copy(out.at[m], ga_hbm.at[m] if m < MEMB else gs_hbm, store_sem.at[m])
        store.start()
        stores.append(store)
    for store in stores:
        store.wait()
    for copy in sent:
        copy.wait_send()


def shards(alpha, static_ctl, perturbations, static_std, lon_root, lat_root, jacobian, obs_count, channel_mask,
           channel_error, member_weight):
    pieces = [lon_root[:, COLS * b : COLS * b + 128] for b in range(4)]
    for b in range(4):
        pieces += [lon_root[:, COLS * b + 128 : COLS * b + COLS], jnp.zeros((LON, 64 - REM), BF16)]
    w = jnp.concatenate(pieces, axis=1)
    order = row_order()
    any_space = pl.BlockSpec(memory_space=pl.ANY)
    inputs = [alpha, static_ctl, perturbations, static_std, w, lat_root, jacobian, obs_count, channel_mask,
              jnp.asarray(order, BF16), jnp.asarray(order.T, BF16)]
    dma = pltpu.SemaphoreType.DMA
    vmem = pltpu.VMEM
    scratch = [vmem(x.shape, x.dtype) for x in inputs] + [
        vmem((2, 4, MEMB, ROWS, PAIR), BF16),
        vmem((2, MEMB, 4, ROWS, PAIR), BF16),
        vmem((4, 8, WIDE), F32),
        vmem((4, 8, WIDE), F32),
        vmem((2, QN, PAD, PAIR), BF16),
        vmem((2, QN - 1, PAD, PAIR), BF16),
        vmem((2, ZN, 8, PAIR), F32),
        vmem((2, ZN - 1, 8, PAIR), F32),
        vmem((8, WIDE), F32),
        vmem((ZN, 8, WIDE), F32),
        vmem((PAD, WIDE), F32),
        vmem((QN, PAD, WIDE), BF16),
        vmem((FIELDS, 4, ROWS, WIDE), BF16),
        vmem((FIELDS, 4, ROWS, WIDE), BF16),
        vmem((S * ROWS, WIDE), BF16),
        vmem((FIELDS, S, ROWS, LON), F32),
        vmem((FIELDS, PERM, WIDE), F32),
        vmem((LAT, WIDE), F32),
        vmem((2, LAT, 128), F32),
        vmem((PERM, LAT), BF16),
        vmem((LAT, PERM), BF16),
        vmem((S, 8, 256), F32),
        vmem((S, 8, 256), F32),
        dma((len(inputs),)), dma((FIELDS,)),
        dma((2, 3)), dma((2, 3)), dma((3,)), dma((3,)),
        dma((2, QN - 1)), dma((2, QN - 1)), dma((2, ZN - 1)), dma((2, ZN - 1)),
        dma((ZN - 1,)), dma((ZN - 1,)), dma((QN - 1,)), dma((QN - 1,)),
        dma((FIELDS, 3)), dma((FIELDS, 3)),
    ]
    return pl.pallas_call(
        kernel,
        out_shape=(jax.ShapeDtypeStruct((MEMB, S, ROWS, LON), F32), jax.ShapeDtypeStruct((S, ROWS, LON), F32)),
        in_specs=[any_space] * len(inputs)
        + [pl.BlockSpec(memory_space=pltpu.SMEM), pl.BlockSpec(memory_space=pltpu.VMEM)],
        out_specs=(any_space, any_space),
        scratch_shapes=scratch,
        compiler_params=pltpu.CompilerParams(collective_id=0, has_side_effects=True, vmem_limit_bytes=48 << 20),
        name="hessian",
    )(*inputs, channel_error, member_weight.reshape(1, -1))


def solution(mesh):
    in_specs = (
        P("mem", None, "band", None),
        P(None, "band", None),
        P("mem", None, None, "band"),
        P(None, None, "band"),
        P(),
        P(),
        P(None, None, "mem", "band"),
        P("mem", "band"),
        P(None, "mem", "band"),
        P(),
        P(),
    )
    out_specs = (P("mem", None, "band", None), P(None, "band", None))
    return jax.shard_map(shards, mesh=mesh, in_specs=in_specs, out_specs=out_specs, check_vma=False)
```

```python
import functools

import jax
import jax.numpy as jnp
from jax import lax
from jax.experimental import pallas as pl
from jax.experimental.pallas import tpu as pltpu
from jax.sharding import PartitionSpec as P

MESH = pl.DeviceIdType.MESH
F32, BF16, I32 = jnp.float32, jnp.bfloat16, jnp.int32

S, CH, MEMB, FIELDS = 4, 32, 2, 3
ROWS, LAT, LON, COLS = 80, 320, 720, 180
REM = COLS - 128
YN, TN, OWN = 4, 16, 5
PAIR, WIDE = 384, 768
PIECE = 16


def iota(shape, dim):
    return lax.broadcasted_iota(I32, shape, dim)


def one_hot(rows, columns, column_of_row):
    return jnp.where(iota((rows, columns), 1) == column_of_row(iota((rows, columns), 0)), 1.0, 0.0).astype(BF16)


def fifth(x):
    return (x * 205) // 1024


def grid_row(p):
    y = p // ROWS
    t = fifth(p - ROWS * y)
    return OWN * (8 * (t // 2) + 4 * (t % 2) + y) + p - ROWS * y - OWN * t


def packed_lane(row):
    j, s = row // 4, row % 4
    tail = jnp.where(j < 128, 128 * (s % 2) + j, 256 + 64 * (s % 2) + j - 128)
    return PAIR * (s // 2) + tail


def piece_row(a):
    t, r = a // PIECE, a % PIECE
    tile = fifth(r)
    return jnp.where(r < 3 * OWN, ROWS * tile + OWN * t + r - OWN * tile, -1)


def low_half(shape):
    return iota(shape, len(shape) - 1) < 64


def joined(even, odd):
    return jnp.where(low_half(even.shape), even, pltpu.roll(odd, 64, 1))


def joined_high(even, odd):
    return jnp.where(low_half(even.shape), pltpu.roll(even, 64, 1), odd)


def dot(a, b, contract=(1, 0)):
    return lax.dot_general(a, b, (((contract[0],), (contract[1],)), ((), ())), preferred_element_type=F32)


def kernel(
    alpha_hbm, static_hbm, pert_hbm, std_hbm, lon_hbm, lat_hbm, jac_hbm, count_hbm, mask_hbm, error_ref, weight_ref,
    ga_hbm, gs_hbm,
    alpha, static, pert, std, lon, lat, jac, count, mask,
    w, fs, rl, xr, ss, sr, rs, r1, s2, r2, gp, gzr, ag, bs, bl, br, lhs, out,
    spread, packed, rem, order, latp, latpt, spreader, to_piece, from_piece, squares, terms, isc, gsc, incs,
    load_sem, std_sem, store_sem, f_send, f_recv, t_send, t_recv, a_send, a_recv, b_send, b_recv, c_send, c_recv,
    d_send, d_recv, e_send, e_recv,
):
    mem, band = lax.axis_index("mem"), lax.axis_index("band")
    z, x, y = mem // 8, (mem // 4) % 2, mem % 4
    t = 2 * z + x
    chip, core = band // 2, band % 2
    sib, far, cross = 2 * chip + 1 - core, 2 * (1 - chip) + core, 3 - band

    def at_band(b):
        return {"mem": mem, "band": b}

    ys = [lax.rem(y + k, YN) for k in range(1, YN)]
    to_y = [{"mem": 8 * z + 4 * x + v, "band": band} for v in ys]
    ts = [lax.rem(t + k, TN) for k in range(1, TN)]
    to_t = [{"mem": 8 * (v // 2) + 4 * (v % 2) + y, "band": band} for v in ts]

    staged = [(lon_hbm, lon), (alpha_hbm, alpha), (static_hbm, static), (lat_hbm, lat),
              (pert_hbm.reshape(MEMB, S * COLS, LAT), pert), (jac_hbm, jac), (count_hbm, count), (mask_hbm, mask)]
    loads = [pltpu.make_async_copy(src, dst, load_sem.at[i]) for i, (src, dst) in enumerate(staged)]
    loads += [pltpu.make_async_copy(std_hbm.at[:, s, :], std.at[s], std_sem.at[s]) for s in range(S)]
    for load in loads:
        load.start()

    barrier = pltpu.get_barrier_semaphore()
    partners = [at_band(sib), at_band(far)] + to_y + to_t
    for device in partners:
        pl.semaphore_signal(barrier, inc=1, device_id=device, device_id_type=MESH)

    def remote(src, dst, send, recv, device):
        return pltpu.make_async_remote_copy(
            src_ref=src, dst_ref=dst, send_sem=send, recv_sem=recv, device_id=device, device_id_type=MESH)

    sent = []

    loads[0].wait()
    for b in range(4):
        w[:, 128 * b : 128 * b + 128] = lon[:, COLS * b : COLS * b + 128]
        w[:, 512 + 64 * b : 512 + 64 * b + REM] = lon[:, COLS * b + 128 : COLS * b + COLS]
        w[:, 512 + 64 * b + REM : 576 + 64 * b] = jnp.zeros((LON, 64 - REM), BF16)

    forward = []
    loads[1].wait()
    for p in range(2):
        rows = alpha[:, 2 * p : 2 * p + 2].reshape(4 * ROWS, LON)
        v = dot(rows, w[...]).reshape(MEMB, 2, ROWS, WIDE)
        for m in range(MEMB):
            even, odd = v[m, 0], v[m, 1]
            for b in range(4):
                tile = 512 + 128 * (b // 2)
                join = joined if b % 2 == 0 else joined_high
                fs[p, b, m, :, 0:128] = even[:, 128 * b : 128 * b + 128].astype(BF16)
                fs[p, b, m, :, 128:256] = odd[:, 128 * b : 128 * b + 128].astype(BF16)
                fs[p, b, m, :, 256:384] = join(even[:, tile : tile + 128], odd[:, tile : tile + 128]).astype(BF16)
        copies = [
            remote(fs.at[p, far], xr.at[p, :, band], f_send.at[p, 0], f_recv.at[p, 0], at_band(far)),
            remote(fs.at[p, cross], rl.at[p], f_send.at[p, 1], f_recv.at[p, 1], at_band(sib)),
            remote(fs.at[p, sib], xr.at[p, :, band], f_send.at[p, 2], f_recv.at[p, 2], at_band(sib)),
            remote(rl.at[p], xr.at[p, :, sib], f_send.at[p, 3], f_recv.at[p, 3], at_band(far)),
        ]
        if p == 0:
            pl.semaphore_wait(barrier, len(partners))
        else:
            forward[0][1].wait_recv()
            forward[0][3].start()
        for copy in copies[:3]:
            copy.start()
        forward.append(copies)
        xr[p, :, band] = fs[p, band]

    loads[2].wait()
    loads[3].wait()
    v = dot(static[...].reshape(S * ROWS, LON), w[...]).astype(BF16)
    forward[1][1].wait_recv()
    forward[1][3].start()
    own_rows = dot(one_hot(16, LAT, lambda k: jnp.where(k < OWN, OWN * mem + k, -1)), lat[...]).astype(BF16)
    here = jnp.where(iota((LAT, ROWS), 0) == ROWS * band + iota((LAT, ROWS), 1), 1.0, 0.0).astype(BF16)
    own_part = dot(own_rows, here).astype(BF16)
    parts = [dot(own_part, v[ROWS * s : ROWS * s + ROWS])[0:8] for s in range(S)]
    for b in range(4):
        tile = 512 + 128 * (b // 2)
        join = joined if b % 2 == 0 else joined_high
        for p in range(2):
            for s in range(2):
                ss[b, :, PAIR * p + 128 * s : PAIR * p + 128 * s + 128] = parts[2 * p + s][:, 128 * b : 128 * b + 128]
            ss[b, :, PAIR * p + 256 : PAIR * p + 384] = join(
                parts[2 * p][:, tile : tile + 128], parts[2 * p + 1][:, tile : tile + 128])
    static_copies = [
        remote(ss.at[far], sr.at[band], t_send.at[0], t_recv.at[0], at_band(far)),
        remote(ss.at[sib], sr.at[band], t_send.at[1], t_recv.at[1], at_band(sib)),
        remote(ss.at[cross], sr.at[4], t_send.at[2], t_recv.at[2], at_band(sib)),
        remote(sr.at[4], sr.at[sib], t_send.at[3], t_recv.at[3], at_band(far)),
    ]
    for copy in static_copies[:3]:
        copy.start()
    sr[band] = ss[band]

    order[...] = one_hot(LAT, LAT, grid_row)
    latp[...] = dot(order[...], lat[...]).astype(BF16)
    spreader[...] = one_hot(S * COLS, WIDE, packed_lane)
    weights = weight_ref[...].astype(F32)
    coef = weights / jnp.sqrt(jnp.sum(weights * weights, axis=1, keepdims=True))
    loads[4].wait()
    for m in range(MEMB):
        factor = 0.8 * jnp.sum(jnp.where(iota(coef.shape, 1) == MEMB * mem + m, coef, 0.0), axis=1, keepdims=True)
        ordered = dot(order[...], pert[m], (1, 1)).astype(BF16)
        spread[m, 0:LAT] = factor * dot(ordered, spreader[...])
    to_piece[...] = one_hot(TN * PIECE, 3 * ROWS, piece_row)
    static_copies[2].wait_recv()
    static_copies[3].start()

    first = []
    for p in range(2):
        for k in (0, 2, 3):
            forward[p][k].wait_recv()
        total = None
        for m in range(MEMB):
            term = spread[m, 0:LAT, PAIR * p : PAIR * p + PAIR] * dot(latp[...], xr[p, m].reshape(LAT, PAIR))
            total = term if total is None else total + term
        rs[p] = total.astype(BF16).reshape(YN, ROWS, PAIR)
        copies = [
            remote(rs.at[p, ys[k]], r1.at[p, k], a_send.at[p, k], a_recv.at[p, k], to_y[k]) for k in range(YN - 1)]
        for copy in copies:
            copy.start()
        first.append(copies)
        sent += forward[p]

    for load in loads[8:]:
        load.wait()
    rem[...] = jnp.zeros_like(rem)
    for p in range(2):
        for s in range(2):
            value = std[2 * p + s]
            ordered = None
            for _ in range(3):
                head = value.astype(BF16)
                term = dot(order[...], head, (1, 1))
                ordered = term if ordered is None else ordered + term
                value = value - head.astype(F32)
            ordered = 0.6 * ordered
            spread[MEMB, 0:LAT, PAIR * p + 128 * s : PAIR * p + 128 * s + 128] = ordered[:, 0:128]
            rem[s, :, 0:REM] = ordered[:, 128:COLS]
        spread[MEMB, 0:LAT, PAIR * p + 256 : PAIR * p + 384] = joined(rem[0], rem[1])
    latpt[...] = dot(jnp.transpose(lat[...].astype(F32)).astype(BF16), order[...], (1, 1)).astype(BF16)
    hot = iota((3 * ROWS, TN * PIECE), 0) == piece_row(iota((3 * ROWS, TN * PIECE), 1))
    from_piece[...] = jnp.where(hot, 1.0, 0.0).astype(BF16)
    error = jnp.sum(jnp.where(iota((CH, CH), 0) == iota((CH, CH), 1), error_ref[...], 0.0), axis=1, keepdims=True)
    squares[...] = jnp.broadcast_to(error * error, squares.shape)
    spread[:, LAT:] = jnp.zeros((FIELDS, 8, WIDE), F32)
    first_row = ROWS * y + OWN * t
    shift = first_row % 8
    own_std = spread[MEMB, pl.ds(pl.multiple_of(first_row - shift, 8), 16), :]
    own_std = pltpu.roll(own_std, (16 - shift) % 16, 0)[0:8]
    for k in (0, 1, 3):
        static_copies[k].wait_recv()
    sent += static_copies
    static_term = own_std * (sr[0] + sr[1] + sr[2] + sr[3])
    terms[...] = jnp.zeros_like(terms)
    for p in range(2):
        for l in range(3):
            terms[p, OWN * l : OWN * l + OWN] = static_term[0:OWN, PAIR * p + 128 * l : PAIR * p + 128 * l + 128]

    second = []
    for p in range(2):
        for copy in first[p]:
            copy.wait_recv()
        total = rs[p, y].astype(F32)
        for k in range(YN - 1):
            total = total + r1[p, k].astype(F32)
        total = total.astype(BF16)
        tall = jnp.concatenate([total[:, 0:128], total[:, 128:256], total[:, 256:384]], axis=0)
        s2[p] = dot(to_piece[...], tall).astype(BF16).reshape(TN, PIECE, 128)
        copies = [
            remote(s2.at[p, ts[k]], r2.at[p, k], b_send.at[p, k], b_recv.at[p, k], to_t[k]) for k in range(TN - 1)]
        for copy in copies:
            copy.start()
        second.append(copies)
        sent += first[p]

    for load in loads[5:8]:
        load.wait()
    for p in range(2):
        for copy in second[p]:
            copy.wait_recv()
        sent += second[p]
        total = terms[p] + s2[p, t].astype(F32)
        for k in range(TN - 1):
            total = total + r2[p, k].astype(F32)
        isc[2 * p, 0:OWN, 0:128] = total[0:OWN]
        isc[2 * p + 1, 0:OWN, 0:128] = total[OWN : 2 * OWN]
        isc[2 * p, 0:OWN, 128:256] = total[2 * OWN : 3 * OWN]
        isc[2 * p + 1, 0:OWN, 128:256] = pltpu.roll(total, 64, 1)[2 * OWN : 3 * OWN]
    for i in range(OWN):
        for s in range(S):
            incs[i, s : s + 1, :] = isc[s, i : i + 1, :]
    inc = [incs[i, 0:S, 0:COLS] for i in range(OWN)]
    counts = count[...].astype(F32)

    def channels(step, grads):
        base = pl.multiple_of(8 * step, 8)
        square = squares[pl.ds(base, 8), 0:1]
        grads = list(grads)
        for i in range(OWN):
            weight = mask[i, pl.ds(base, 8), :].astype(F32) * counts[i : i + 1, :] / square
            for c in range(8):
                jac_c = jac[base + c, i].astype(F32)
                radiance = jnp.sum(jac_c * inc[i], axis=0, keepdims=True)
                grads[i] = grads[i] + jac_c * (weight[c : c + 1, :] * radiance)
        return tuple(grads)

    grads = lax.fori_loop(0, CH // 8, channels, tuple(jnp.zeros((S, COLS), F32) for _ in range(OWN)))
    gsc[...] = jnp.zeros_like(gsc)
    for i in range(OWN):
        for s in range(S):
            gsc[s, i : i + 1, 0:COLS] = grads[i][s : s + 1, :].astype(BF16).astype(F32)
    for p in range(2):
        both = joined(gsc[2 * p, :, 128:256], gsc[2 * p + 1, :, 128:256])
        piece = [gsc[2 * p, 0:OWN, 0:128], gsc[2 * p + 1, 0:OWN, 0:128], both[0:OWN], jnp.zeros((1, 128), F32)]
        gp[p] = jnp.concatenate(piece, axis=0).astype(BF16)

    third = [remote(gp, gzr.at[:, t], c_send.at[k], c_recv.at[k], to_t[k]) for k in range(TN - 1)]
    for copy in third:
        copy.start()
    for p in range(2):
        gzr[p, t] = gp[p]
    for copy in third:
        copy.wait_recv()
    sent += third
    for p in range(2):
        tall = dot(from_piece[...], gzr[p].reshape(TN * PIECE, 128)).astype(BF16)
        for l in range(3):
            ag[y, :, PAIR * p + 128 * l : PAIR * p + 128 * l + 128] = tall[ROWS * l : ROWS * l + ROWS]
    fourth = [remote(ag.at[y], ag.at[y], d_send.at[k], d_recv.at[k], to_y[k]) for k in range(YN - 1)]
    for copy in fourth:
        copy.start()
    for copy in fourth:
        copy.wait_recv()
    sent += fourth

    gradient = ag[...].reshape(LAT, WIDE).astype(F32)
    back = []
    for m in range(FIELDS):
        adjoint = (spread[m, 0:LAT] * gradient).astype(BF16)
        bs[m] = dot(latpt[...], adjoint).astype(BF16).reshape(4, ROWS, WIDE)
        copies = [
            remote(bs.at[m, far], br.at[m, band], e_send.at[m, 0], e_recv.at[m, 0], at_band(far)),
            remote(bs.at[m, cross], bl.at[m], e_send.at[m, 1], e_recv.at[m, 1], at_band(sib)),
            remote(bs.at[m, sib], br.at[m, band], e_send.at[m, 2], e_recv.at[m, 2], at_band(sib)),
            remote(bl.at[m], br.at[m, sib], e_send.at[m, 3], e_recv.at[m, 3], at_band(far)),
        ]
        if m > 0:
            back[m - 1][1].wait_recv()
            back[m - 1][3].start()
        for copy in copies[:3]:
            copy.start()
        back.append(copies)
        br[m, band] = bs[m, band]
    back[FIELDS - 1][1].wait_recv()
    back[FIELDS - 1][3].start()

    stores = []
    for m in range(FIELDS):
        for k in (0, 2, 3):
            back[m][k].wait_recv()
        sent += back[m]
        for p in range(2):
            tiles = [br[m, b, :, PAIR * p + 256 : PAIR * p + 384].astype(F32) for b in range(4)]
            for s in range(2):
                rows = pl.ds((2 * p + s) * ROWS, ROWS)
                for b in range(4):
                    lhs[rows, 128 * b : 128 * b + 128] = br[m, b, :, PAIR * p + 128 * s : PAIR * p + 128 * s + 128]
                join = joined if s == 0 else joined_high
                for h in range(2):
                    lhs[rows, 512 + 128 * h : 640 + 128 * h] = join(tiles[2 * h], tiles[2 * h + 1]).astype(BF16)
        v = dot(lhs[...], w[...], (1, 1))
        base = alpha[m] if m < MEMB else static[...]
        out[m] = base.astype(F32) + v.reshape(S, ROWS, LON)
        store = pltpu.make_async_copy(out.at[m], ga_hbm.at[m] if m < MEMB else gs_hbm, store_sem.at[m])
        store.start()
        stores.append(store)
    for store in stores:
        store.wait()
    for copy in sent:
        copy.wait_send()


def shards(alpha, static_ctl, perturbations, static_std, lon_root, lat_root, jacobian, obs_count, channel_mask,
           channel_error, member_weight):
    inputs = [alpha, static_ctl, jnp.transpose(perturbations, (0, 3, 1, 2)), jnp.transpose(static_std, (2, 0, 1)),
              lon_root, lat_root, jnp.transpose(jacobian, (0, 2, 1, 3)), obs_count, jnp.transpose(channel_mask, (1, 0, 2))]
    dma, vmem = pltpu.SemaphoreType.DMA, pltpu.VMEM
    scratch = [
        vmem((MEMB, S, ROWS, LON), BF16),
        vmem((S, ROWS, LON), BF16),
        vmem((MEMB, S * COLS, LAT), BF16),
        vmem((S, COLS, LAT), F32),
        vmem((LON, LON), BF16),
        vmem((LAT, LAT), BF16),
        vmem((CH, OWN, S, COLS), BF16),
        vmem((OWN, COLS), I32),
        vmem((OWN, CH, COLS), I32),
        vmem((LON, WIDE), BF16),
        vmem((2, 4, MEMB, ROWS, PAIR), BF16),
        vmem((2, MEMB, ROWS, PAIR), BF16),
        vmem((2, MEMB, 4, ROWS, PAIR), BF16),
        vmem((4, 8, WIDE), F32),
        vmem((5, 8, WIDE), F32),
        vmem((2, YN, ROWS, PAIR), BF16),
        vmem((2, YN - 1, ROWS, PAIR), BF16),
        vmem((2, TN, PIECE, 128), BF16),
        vmem((2, TN - 1, PIECE, 128), BF16),
        vmem((2, PIECE, 128), BF16),
        vmem((2, TN, PIECE, 128), BF16),
        vmem((YN, ROWS, WIDE), BF16),
        vmem((FIELDS, 4, ROWS, WIDE), BF16),
        vmem((FIELDS, ROWS, WIDE), BF16),
        vmem((FIELDS, 4, ROWS, WIDE), BF16),
        vmem((S * ROWS, WIDE), BF16),
        vmem((FIELDS, S, ROWS, LON), F32),
        vmem((FIELDS, LAT + 8, WIDE), F32),
        vmem((LAT, WIDE), F32),
        vmem((2, LAT, 128), F32),
        vmem((LAT, LAT), BF16),
        vmem((LAT, LAT), BF16),
        vmem((LAT, LAT), BF16),
        vmem((S * COLS, WIDE), BF16),
        vmem((TN * PIECE, 3 * ROWS), BF16),
        vmem((3 * ROWS, TN * PIECE), BF16),
        vmem((CH, 128), F32),
        vmem((2, PIECE, 128), F32),
        vmem((S, 8, 256), F32),
        vmem((S, 8, 256), F32),
        vmem((OWN, 8, 256), F32),
        dma((8,)), dma((S,)), dma((FIELDS,)),
        dma((2, 4)), dma((2, 4)), dma((4,)), dma((4,)),
        dma((2, YN - 1)), dma((2, YN - 1)), dma((2, TN - 1)), dma((2, TN - 1)),
        dma((TN - 1,)), dma((TN - 1,)), dma((YN - 1,)), dma((YN - 1,)),
        dma((FIELDS, 4)), dma((FIELDS, 4)),
    ]
    in_hbm = pl.BlockSpec(memory_space=pl.ANY)
    in_vmem = pl.BlockSpec(memory_space=pltpu.VMEM)
    return pl.pallas_call(
        kernel,
        out_shape=(jax.ShapeDtypeStruct((MEMB, S, ROWS, LON), F32), jax.ShapeDtypeStruct((S, ROWS, LON), F32)),
        in_specs=[in_hbm] * len(inputs) + [in_vmem, in_vmem],
        out_specs=(in_hbm, in_hbm),
        scratch_shapes=scratch,
        compiler_params=pltpu.CompilerParams(collective_id=0, has_side_effects=True, vmem_limit_bytes=60 << 20),
        name="hessian",
    )(*inputs, channel_error.reshape(1, CH), member_weight.reshape(1, -1))


def solution(mesh):
    in_specs = (
        P("mem", None, "band", None),
        P(None, "band", None),
        P("mem", None, None, "band"),
        P(None, None, "band"),
        P(),
        P(),
        P(None, None, "mem", "band"),
        P("mem", "band"),
        P(None, "mem", "band"),
        P(),
        P(),
    )
    out_specs = (P("mem", None, "band", None), P(None, "band", None))
    return jax.shard_map(shards, mesh=mesh, in_specs=in_specs, out_specs=out_specs, check_vma=False)
```

```python
import functools

import jax
import jax.numpy as jnp
from jax import lax
from jax.experimental import pallas as pl
from jax.experimental.pallas import tpu as pltpu
from jax.sharding import PartitionSpec as P

MESH = pl.DeviceIdType.MESH
F32, BF16, I32 = jnp.float32, jnp.bfloat16, jnp.int32

S, CH, MEMB, FIELDS = 4, 32, 2, 3
ROWS, LAT, LON, COLS = 80, 320, 720, 180
REM = COLS - 128
YN, TN, OWN = 4, 16, 5
WIDE = 768
CHUNKS = 2
TILES = (2, 4)
BASE = (512, 0)
PIECE = (16, 32)
SPAN = ((128, COLS), (0, 128))


def iota(shape, dim):
    return lax.broadcasted_iota(I32, shape, dim)


def one_hot(rows, columns, column_of_row):
    return jnp.where(iota((rows, columns), 1) == column_of_row(iota((rows, columns), 0)), 1.0, 0.0).astype(BF16)


def fifth(x):
    return (x * 205) // 1024


def grid_row(p):
    y = p // ROWS
    t = fifth(p - ROWS * y)
    return OWN * (8 * (t // 2) + 4 * (t % 2) + y) + p - ROWS * y - OWN * t


def packed_lane(row):
    j, s = row // 4, row % 4
    return jnp.where(j < 128, 128 * s + j, 512 + 128 * (s // 2) + 64 * (s % 2) + j - 128)


def piece_row(c, a):
    t, r = a // PIECE[c], a % PIECE[c]
    tile = fifth(r)
    return jnp.where(r < TILES[c] * OWN, ROWS * tile + OWN * t + r - OWN * tile, -1)


def low_half(shape):
    return iota(shape, len(shape) - 1) < 64


def joined(even, odd):
    return jnp.where(low_half(even.shape), even, pltpu.roll(odd, 64, 1))


def joined_high(even, odd):
    return jnp.where(low_half(even.shape), pltpu.roll(even, 64, 1), odd)


def dot(a, b, contract=(1, 0)):
    return lax.dot_general(a, b, (((contract[0],), (contract[1],)), ((), ())), preferred_element_type=F32)


def kernel(
    alpha_hbm, static_hbm, pert_hbm, std_hbm, lon_hbm, lat_hbm, jac_hbm, count_hbm, mask_hbm, error_ref, weight_ref,
    ga_hbm, gs_hbm,
    alpha, static, pert, std, lon, lat, jac, count, mask,
    w, ss, sr, out, spread, rem, order, latp, latpt, spreader, squares, incs, gr,
    fs0, fs1, rl0, rl1, xr0, xr1, rs0, rs1, r10, r11, s20, s21, r20, r21, terms0, terms1, gp0, gp1, gz0, gz1, ag0, ag1,
    bs0, bs1, bl0, bl1, br0, br1, bss0, bss1, brs0, brs1, to0, to1, from0, from1, lhs0, lhs1,
    load_sem, std_sem, store_sem, f_send, f_recv, t_send, t_recv, a_send, a_recv, b_send, b_recv, c_send, c_recv,
    d_send, d_recv, e_send, e_recv, g_send, g_recv,
):
    fs, rl, xr, rs, r1, s2, r2 = (fs0, fs1), (rl0, rl1), (xr0, xr1), (rs0, rs1), (r10, r11), (s20, s21), (r20, r21)
    terms, gp, gz, ag, bs, bl, br = (terms0, terms1), (gp0, gp1), (gz0, gz1), (ag0, ag1), (bs0, bs1), (bl0, bl1), (br0, br1)
    bss, brs, to_piece, from_piece, lhs = (bss0, bss1), (brs0, brs1), (to0, to1), (from0, from1), (lhs0, lhs1)
    lanes = [slice(BASE[c], BASE[c] + 128 * TILES[c]) for c in range(CHUNKS)]

    mem, band = lax.axis_index("mem"), lax.axis_index("band")
    z, x, y = mem // 8, (mem // 4) % 2, mem % 4
    t = 2 * z + x
    chip, core = band // 2, band % 2
    sib, far, cross = 2 * chip + 1 - core, 2 * (1 - chip) + core, 3 - band

    def at_band(b):
        return {"mem": mem, "band": b}

    ys = [lax.rem(y + k, YN) for k in range(1, YN)]
    to_y = [{"mem": 8 * z + 4 * x + v, "band": band} for v in ys]
    ts = [lax.rem(t + k, TN) for k in range(1, TN)]
    to_t = [{"mem": 8 * (v // 2) + 4 * (v % 2) + y, "band": band} for v in ts]

    staged = [(lon_hbm, lon), (alpha_hbm, alpha), (static_hbm, static), (lat_hbm, lat),
              (pert_hbm.reshape(MEMB, S * COLS, LAT), pert), (jac_hbm, jac), (count_hbm, count), (mask_hbm, mask)]
    loads = [pltpu.make_async_copy(src, dst, load_sem.at[i]) for i, (src, dst) in enumerate(staged)]
    loads += [pltpu.make_async_copy(std_hbm.at[:, s, :], std.at[s], std_sem.at[s]) for s in range(S)]
    for load in loads:
        load.start()

    barrier = pltpu.get_barrier_semaphore()
    partners = [at_band(far), at_band(cross)] + to_t + to_y + [at_band(sib)]
    for device in partners:
        pl.semaphore_signal(barrier, inc=1, device_id=device, device_id_type=MESH)

    def remote(src, dst, send, recv, device):
        return pltpu.make_async_remote_copy(
            src_ref=src, dst_ref=dst, send_sem=send, recv_sem=recv, device_id=device, device_id_type=MESH)

    sent = []

    loads[0].wait()
    for b in range(4):
        w[:, 512 + 64 * b : 512 + 64 * b + REM] = lon[:, COLS * b + 128 : COLS * b + COLS]
        w[:, 512 + 64 * b + REM : 576 + 64 * b] = jnp.zeros((LON, 64 - REM), BF16)
        w[:, 128 * b : 128 * b + 128] = lon[:, COLS * b : COLS * b + 128]

    forward = []
    loads[1].wait()
    for c in range(CHUNKS):
        v = dot(alpha[...].reshape(MEMB * S * ROWS, LON), w[:, lanes[c]])
        v = v.reshape(MEMB, S, ROWS, 128 * TILES[c])
        for m in range(MEMB):
            for b in range(4):
                if c == 0:
                    tile = 128 * (b // 2)
                    join = joined if b % 2 == 0 else joined_high
                    for h in range(2):
                        pair = join(v[m, 2 * h][:, tile : tile + 128], v[m, 2 * h + 1][:, tile : tile + 128])
                        fs[c][b, m, :, 128 * h : 128 * h + 128] = pair.astype(BF16)
                else:
                    for s in range(S):
                        fs[c][b, m, :, 128 * s : 128 * s + 128] = v[m, s][:, 128 * b : 128 * b + 128].astype(BF16)
        copies = [
            remote(fs[c].at[far], xr[c].at[band], f_send.at[c, 0], f_recv.at[c, 0], at_band(far)),
            remote(fs[c].at[cross], rl[c], f_send.at[c, 1], f_recv.at[c, 1], at_band(sib)),
            remote(fs[c].at[sib], xr[c].at[band], f_send.at[c, 2], f_recv.at[c, 2], at_band(sib)),
            remote(rl[c], xr[c].at[sib], f_send.at[c, 3], f_recv.at[c, 3], at_band(far)),
        ]
        if c == 0:
            pl.semaphore_wait(barrier, len(partners))
        else:
            forward[0][1].wait_recv()
            forward[0][3].start()
        for copy in copies[:3]:
            copy.start()
        forward.append(copies)
        xr[c][band] = fs[c][band]

    loads[2].wait()
    loads[3].wait()
    v = dot(static[...].reshape(S * ROWS, LON), w[...]).astype(BF16)
    forward[1][1].wait_recv()
    forward[1][3].start()
    own_rows = dot(one_hot(16, LAT, lambda k: jnp.where(k < OWN, OWN * mem + k, -1)), lat[...]).astype(BF16)
    here = jnp.where(iota((LAT, ROWS), 0) == ROWS * band + iota((LAT, ROWS), 1), 1.0, 0.0).astype(BF16)
    own_part = dot(own_rows, here).astype(BF16)
    parts = [dot(own_part, v[ROWS * s : ROWS * s + ROWS])[0:8] for s in range(S)]
    for b in range(4):
        tile = 512 + 128 * (b // 2)
        join = joined if b % 2 == 0 else joined_high
        for s in range(S):
            ss[b, :, 128 * s : 128 * s + 128] = parts[s][:, 128 * b : 128 * b + 128]
        for h in range(2):
            ss[b, :, 512 + 128 * h : 640 + 128 * h] = join(
                parts[2 * h][:, tile : tile + 128], parts[2 * h + 1][:, tile : tile + 128])
    others = (far, cross, sib)
    static_copies = [remote(ss.at[b], sr.at[band], t_send.at[k], t_recv.at[k], at_band(b)) for k, b in enumerate(others)]
    for copy in static_copies:
        copy.start()
    sr[band] = ss[band]

    order[...] = one_hot(LAT, LAT, grid_row)
    latp[...] = dot(order[...], lat[...]).astype(BF16)
    spreader[...] = one_hot(S * COLS, WIDE, packed_lane)
    weights = weight_ref[...].astype(F32)
    coef = weights / jnp.sqrt(jnp.sum(weights * weights, axis=1, keepdims=True))
    loads[4].wait()
    for m in range(MEMB):
        factor = 0.8 * jnp.sum(jnp.where(iota(coef.shape, 1) == MEMB * mem + m, coef, 0.0), axis=1, keepdims=True)
        ordered = dot(order[...], pert[m], (1, 1)).astype(BF16)
        spread[m, 0:LAT] = factor * dot(ordered, spreader[...])
    for c in range(CHUNKS):
        rows, height = TN * PIECE[c], ROWS * TILES[c]
        to_piece[c][...] = one_hot(rows, height, lambda a: piece_row(c, a))

    def sum_first(c):
        for k in (0, 2, 3):
            forward[c][k].wait_recv()
        total = None
        for m in range(MEMB):
            field = dot(latp[...], xr[c][:, m].reshape(LAT, 128 * TILES[c]))
            term = spread[m, 0:LAT, lanes[c]] * field
            total = term if total is None else total + term
        rs[c][...] = total.astype(BF16).reshape(YN, ROWS, 128 * TILES[c])
        copies = [
            remote(rs[c].at[ys[k]], r1[c].at[k], a_send.at[c, k], a_recv.at[c, k], to_y[k]) for k in range(YN - 1)]
        for copy in copies:
            copy.start()
        sent.extend(forward[c])
        return copies

    def sum_second(c, first):
        for copy in first:
            copy.wait_recv()
        total = rs[c][y].astype(F32)
        for k in range(YN - 1):
            total = total + r1[c][k].astype(F32)
        total = total.astype(BF16)
        tall = jnp.concatenate([total[:, 128 * l : 128 * l + 128] for l in range(TILES[c])], axis=0)
        s2[c][...] = dot(to_piece[c][...], tall).astype(BF16).reshape(TN, PIECE[c], 128)
        copies = [
            remote(s2[c].at[ts[k]], r2[c].at[k], b_send.at[c, k], b_recv.at[c, k], to_t[k]) for k in range(TN - 1)]
        for copy in copies:
            copy.start()
        sent.extend(first)
        return copies

    def pixels(c, second):
        for copy in second:
            copy.wait_recv()
        sent.extend(second)
        total = terms[c][...] + s2[c][t].astype(F32)
        for k in range(TN - 1):
            total = total + r2[c][k].astype(F32)
        lo, hi = SPAN[c]
        turned = pltpu.roll(total, 64, 1) if c == 0 else None
        for i in range(OWN):
            for s in range(S):
                row = OWN * s + i if c else OWN * (s // 2) + i
                source = total if c or s % 2 == 0 else turned
                incs[i, s : s + 1, :] = source[row : row + 1, :]
        inc = [incs[i, 0:S, 0 : hi - lo] for i in range(OWN)]
        counts = count[:, lo:hi].astype(F32)

        def channels(step, grads):
            base = pl.multiple_of(8 * step, 8)
            square = squares[pl.ds(base, 8), 0:1]
            grads = list(grads)
            for i in range(OWN):
                weight = mask[i, pl.ds(base, 8), lo:hi].astype(F32) * counts[i : i + 1, :] / square
                for n in range(8):
                    jac_n = jac[base + n, i, :, lo:hi].astype(F32)
                    radiance = jnp.sum(jac_n * inc[i], axis=0, keepdims=True)
                    grads[i] = grads[i] + jac_n * (weight[n : n + 1, :] * radiance)
            return tuple(grads)

        grads = lax.fori_loop(0, CH // 8, channels, tuple(jnp.zeros((S, hi - lo), F32) for _ in range(OWN)))
        gr[...] = jnp.zeros_like(gr)
        for i in range(OWN):
            for s in range(S):
                row = OWN * s + i if c else OWN * (s // 2) + i
                half = 0 if c else s % 2
                gr[half, row : row + 1, 0 : hi - lo] = grads[i][s : s + 1, :].astype(BF16).astype(F32)
        gp[c][...] = (gr[0] if c else joined(gr[0, 0 : PIECE[0]], gr[1, 0 : PIECE[0]])).astype(BF16)
        copies = [remote(gp[c], gz[c].at[t], c_send.at[c, k], c_recv.at[c, k], to_t[k]) for k in range(TN - 1)]
        for copy in copies:
            copy.start()
        gz[c][t] = gp[c][...]
        return copies

    def gather(c, third):
        for copy in third:
            copy.wait_recv()
        sent.extend(third)
        tall = dot(from_piece[c][...], gz[c][...].reshape(TN * PIECE[c], 128)).astype(BF16)
        for l in range(TILES[c]):
            ag[c][y, :, 128 * l : 128 * l + 128] = tall[ROWS * l : ROWS * l + ROWS]
        copies = [remote(ag[c].at[y], ag[c].at[y], d_send.at[c, k], d_recv.at[c, k], to_y[k]) for k in range(YN - 1)]
        for copy in copies:
            copy.start()
        return copies

    source, half = far + (cross - far) * (y // 2), y % 2

    def adjoint(c, fourth):
        for copy in fourth:
            copy.wait_recv()
        sent.extend(fourth)
        gradient = ag[c][...].reshape(LAT, 128 * TILES[c]).astype(F32)
        width = 64 * TILES[c]
        back = dot(latpt[...], (spread[MEMB, 0:LAT, lanes[c]] * gradient).astype(BF16)).astype(BF16)
        back = back.reshape(4, ROWS, 128 * TILES[c])
        for h in range(2):
            bss[c][h] = back[:, :, width * h : width * h + width]
        fixed = [
            remote(bss[c].at[half, source], brs[c].at[half, band], g_send.at[c, 0], g_recv.at[c, 0], at_band(source)),
            remote(bss[c].at[:, sib], brs[c].at[:, band], g_send.at[c, 1], g_recv.at[c, 1], at_band(sib)),
        ] + [
            remote(brs[c].at[half, source], brs[c].at[half, source], g_send.at[c, 2 + k], g_recv.at[c, 2 + k], to_y[k])
            for k in range(YN - 1)]
        for copy in fixed[:2]:
            copy.start()
        for m in range(MEMB):
            back = dot(latpt[...], (spread[m, 0:LAT, lanes[c]] * gradient).astype(BF16)).astype(BF16)
            bs[c][:, m] = back.reshape(4, ROWS, 128 * TILES[c])
        copies = [
            remote(bs[c].at[far], br[c].at[band], e_send.at[c, 0], e_recv.at[c, 0], at_band(far)),
            remote(bs[c].at[cross], bl[c], e_send.at[c, 1], e_recv.at[c, 1], at_band(sib)),
            remote(bs[c].at[sib], br[c].at[band], e_send.at[c, 2], e_recv.at[c, 2], at_band(sib)),
            remote(bl[c], br[c].at[sib], e_send.at[c, 3], e_recv.at[c, 3], at_band(far)),
        ]
        for copy in copies[:3]:
            copy.start()
        br[c][band] = bs[c][band]
        for h in range(2):
            brs[c][h, band] = bss[c][h, band]
        return copies, fixed

    def pass_on(c, copies, fixed):
        copies[1].wait_recv()
        copies[3].start()
        fixed[0].wait_recv()
        for copy in fixed[2:]:
            copy.start()

    first = [sum_first(0)]

    for load in loads[8:]:
        load.wait()
    rem[...] = jnp.zeros_like(rem)
    for h in range(2):
        for s in range(2):
            value = std[2 * h + s]
            ordered = None
            for _ in range(3):
                top = value.astype(BF16)
                term = dot(order[...], top, (1, 1))
                ordered = term if ordered is None else ordered + term
                value = value - top.astype(F32)
            ordered = 0.6 * ordered
            spread[MEMB, 0:LAT, 128 * (2 * h + s) : 128 * (2 * h + s) + 128] = ordered[:, 0:128]
            rem[s, :, 0:REM] = ordered[:, 128:COLS]
        spread[MEMB, 0:LAT, 512 + 128 * h : 640 + 128 * h] = joined(rem[0], rem[1])

    first.append(sum_first(1))
    spread[:, LAT:] = jnp.zeros((FIELDS, 8, WIDE), F32)
    first_row = ROWS * y + OWN * t
    shift = first_row % 8
    own_std = spread[MEMB, pl.ds(pl.multiple_of(first_row - shift, 8), 16), :]
    own_std = pltpu.roll(own_std, (16 - shift) % 16, 0)[0:8]
    for copy in static_copies:
        copy.wait_recv()
    sent.extend(static_copies)
    static_term = own_std * (sr[0] + sr[1] + sr[2] + sr[3])
    for c in range(CHUNKS):
        terms[c][...] = jnp.zeros_like(terms[c])
        for l in range(TILES[c]):
            terms[c][OWN * l : OWN * l + OWN] = static_term[0:OWN, BASE[c] + 128 * l : BASE[c] + 128 * l + 128]

    second = [sum_second(0, first[0])]
    latpt[...] = dot(jnp.transpose(lat[...].astype(F32)).astype(BF16), order[...], (1, 1)).astype(BF16)
    for c in range(CHUNKS):
        rows, height = TN * PIECE[c], ROWS * TILES[c]
        hot = iota((height, rows), 0) == piece_row(c, iota((height, rows), 1))
        from_piece[c][...] = jnp.where(hot, 1.0, 0.0).astype(BF16)
    error = jnp.sum(jnp.where(iota((CH, CH), 0) == iota((CH, CH), 1), error_ref[...], 0.0), axis=1, keepdims=True)
    squares[...] = jnp.broadcast_to(error * error, squares.shape)
    for load in loads[5:8]:
        load.wait()

    second.append(sum_second(1, first[1]))

    third = [pixels(0, second[0])]

    third.append(pixels(1, second[1]))

    fourth = [gather(0, third[0])]

    fourth.append(gather(1, third[1]))

    ways = [adjoint(0, fourth[0])]
    pass_on(0, *ways[0])

    ways.append(adjoint(1, fourth[1]))

    copies, fixed = ways[0]
    for copy in copies[:1] + copies[2:] + fixed[1:]:
        copy.wait_recv()
    for f in range(FIELDS):
        for h in range(2):
            if f < MEMB:
                tiles = [br[0][b, f, :, 128 * h : 128 * h + 128].astype(F32) for b in range(4)]
            else:
                tiles = [brs[0][h, b].astype(F32) for b in range(4)]
            for s in range(2):
                join = joined if s == 0 else joined_high
                for g in range(2):
                    pair = join(tiles[2 * g], tiles[2 * g + 1]).astype(BF16)
                    lhs[0][pl.ds((2 * h + s) * ROWS, ROWS), 128 * g : 128 * g + 128] = pair
        base = alpha[f] if f < MEMB else static[...]
        out[f] = base.astype(F32) + dot(lhs[0][...], w[:, lanes[0]], (1, 1)).reshape(S, ROWS, LON)
        if f == 0:
            ways[1][0][1].wait_recv()
            ways[1][0][3].start()
    ways[1][1][0].wait_recv()
    for copy in ways[1][1][2:]:
        copy.start()

    stores = []
    copies, fixed = ways[1]
    for f in range(FIELDS):
        if f == 0:
            for copy in copies[:1] + copies[2:]:
                copy.wait_recv()
        if f == MEMB:
            for copy in fixed[1:]:
                copy.wait_recv()
        for s in range(S):
            for b in range(4):
                if f < MEMB:
                    tile = br[1][b, f, :, 128 * s : 128 * s + 128]
                else:
                    tile = brs[1][s // 2, b, :, 128 * (s % 2) : 128 * (s % 2) + 128]
                lhs[1][ROWS * s : ROWS * s + ROWS, 128 * b : 128 * b + 128] = tile
        out[f] = out[f] + dot(lhs[1][...], w[:, lanes[1]], (1, 1)).reshape(S, ROWS, LON)
        store = pltpu.make_async_copy(out.at[f], ga_hbm.at[f] if f < MEMB else gs_hbm, store_sem.at[f])
        store.start()
        stores.append(store)
    for copies, fixed in ways:
        sent.extend(copies)
        sent.extend(fixed)
    for store in stores:
        store.wait()
    for copy in sent:
        copy.wait_send()


def shards(alpha, static_ctl, perturbations, static_std, lon_root, lat_root, jacobian, obs_count, channel_mask,
           channel_error, member_weight):
    inputs = [alpha, static_ctl, jnp.transpose(perturbations, (0, 3, 1, 2)), jnp.transpose(static_std, (2, 0, 1)),
              lon_root, lat_root, jnp.transpose(jacobian, (0, 2, 1, 3)), obs_count, jnp.transpose(channel_mask, (1, 0, 2))]
    dma, vmem = pltpu.SemaphoreType.DMA, pltpu.VMEM
    scratch = [
        vmem((MEMB, S, ROWS, LON), BF16),
        vmem((S, ROWS, LON), BF16),
        vmem((MEMB, S * COLS, LAT), BF16),
        vmem((S, COLS, LAT), F32),
        vmem((LON, LON), BF16),
        vmem((LAT, LAT), BF16),
        vmem((CH, OWN, S, COLS), BF16),
        vmem((OWN, COLS), I32),
        vmem((OWN, CH, COLS), I32),
        vmem((LON, WIDE), BF16),
        vmem((4, 8, WIDE), F32),
        vmem((4, 8, WIDE), F32),
        vmem((FIELDS, S, ROWS, LON), F32),
        vmem((FIELDS, LAT + 8, WIDE), F32),
        vmem((2, LAT, 128), F32),
        vmem((LAT, LAT), BF16),
        vmem((LAT, LAT), BF16),
        vmem((LAT, LAT), BF16),
        vmem((S * COLS, WIDE), BF16),
        vmem((CH, 128), F32),
        vmem((OWN, 8, 128), F32),
        vmem((2, 32, 128), F32),
    ]

    def both(shape, kind):
        return [vmem(shape(128 * TILES[c], PIECE[c], ROWS * TILES[c]), kind) for c in range(CHUNKS)]

    scratch += both(lambda n, r, h: (4, MEMB, ROWS, n), BF16)
    scratch += both(lambda n, r, h: (MEMB, ROWS, n), BF16)
    scratch += both(lambda n, r, h: (4, MEMB, ROWS, n), BF16)
    scratch += both(lambda n, r, h: (YN, ROWS, n), BF16)
    scratch += both(lambda n, r, h: (YN - 1, ROWS, n), BF16)
    scratch += both(lambda n, r, h: (TN, r, 128), BF16)
    scratch += both(lambda n, r, h: (TN - 1, r, 128), BF16)
    scratch += both(lambda n, r, h: (r, 128), F32)
    scratch += both(lambda n, r, h: (r, 128), BF16)
    scratch += both(lambda n, r, h: (TN, r, 128), BF16)
    scratch += both(lambda n, r, h: (YN, ROWS, n), BF16)
    scratch += both(lambda n, r, h: (4, MEMB, ROWS, n), BF16)
    scratch += both(lambda n, r, h: (MEMB, ROWS, n), BF16)
    scratch += both(lambda n, r, h: (4, MEMB, ROWS, n), BF16)
    scratch += both(lambda n, r, h: (2, 4, ROWS, n // 2), BF16)
    scratch += both(lambda n, r, h: (2, 4, ROWS, n // 2), BF16)
    scratch += both(lambda n, r, h: (TN * r, h), BF16)
    scratch += both(lambda n, r, h: (h, TN * r), BF16)
    scratch += both(lambda n, r, h: (S * ROWS, n), BF16)
    scratch += [
        dma((8,)), dma((S,)), dma((FIELDS,)),
        dma((2, 4)), dma((2, 4)), dma((3,)), dma((3,)),
        dma((2, YN - 1)), dma((2, YN - 1)), dma((2, TN - 1)), dma((2, TN - 1)),
        dma((2, TN - 1)), dma((2, TN - 1)), dma((2, YN - 1)), dma((2, YN - 1)),
        dma((2, 4)), dma((2, 4)), dma((2, YN + 1)), dma((2, YN + 1)),
    ]
    in_hbm = pl.BlockSpec(memory_space=pl.ANY)
    in_vmem = pl.BlockSpec(memory_space=pltpu.VMEM)
    return pl.pallas_call(
        kernel,
        out_shape=(jax.ShapeDtypeStruct((MEMB, S, ROWS, LON), F32), jax.ShapeDtypeStruct((S, ROWS, LON), F32)),
        in_specs=[in_hbm] * len(inputs) + [in_vmem, in_vmem],
        out_specs=(in_hbm, in_hbm),
        scratch_shapes=scratch,
        compiler_params=pltpu.CompilerParams(collective_id=0, has_side_effects=True, vmem_limit_bytes=60 << 20),
        name="hessian",
    )(*inputs, channel_error.reshape(1, CH), member_weight.reshape(1, -1))


def solution(mesh):
    in_specs = (
        P("mem", None, "band", None),
        P(None, "band", None),
        P("mem", None, None, "band"),
        P(None, None, "band"),
        P(),
        P(),
        P(None, None, "mem", "band"),
        P("mem", "band"),
        P(None, "mem", "band"),
        P(),
        P(),
    )
    out_specs = (P("mem", None, "band", None), P(None, "band", None))
    return jax.shard_map(shards, mesh=mesh, in_specs=in_specs, out_specs=out_specs, check_vma=False)
```

```python
import functools

import jax
import jax.numpy as jnp
from jax import lax
from jax.experimental import pallas as pl
from jax.experimental.pallas import tpu as pltpu
from jax.sharding import PartitionSpec as P

MESH = pl.DeviceIdType.MESH
F32, BF16, I32 = jnp.float32, jnp.bfloat16, jnp.int32

S, CH, MEM, MEMB, FIELDS = 4, 32, 128, 2, 3
ROWS, LAT, LON, COLS = 80, 320, 720, 180
REM = COLS - 128
YN, TN, OWN = 4, 16, 5
WIDE = 768
CHUNKS = 2
TILES = (2, 4)
BASE = (512, 0)
PIECE, ALL = 32, 6


def iota(shape, dim):
    return lax.broadcasted_iota(I32, shape, dim)


def one_hot(rows, columns, column_of_row):
    return jnp.where(iota((rows, columns), 1) == column_of_row(iota((rows, columns), 0)), 1.0, 0.0).astype(BF16)


def fifth(x):
    return (x * 205) // 1024


def grid_row(p):
    y = p // ROWS
    t = fifth(p - ROWS * y)
    return OWN * (8 * (t // 2) + 4 * (t % 2) + y) + p - ROWS * y - OWN * t


def packed_lane(row):
    j, s = row // 4, row % 4
    return jnp.where(j < 128, 128 * s + j, 512 + 128 * (s // 2) + 64 * (s % 2) + j - 128)


def piece_row(a):
    t, r = a // PIECE, a % PIECE
    tile = fifth(r)
    return jnp.where(r < ALL * OWN, ROWS * tile + OWN * t + r - OWN * tile, -1)


def low_half(shape):
    return iota(shape, len(shape) - 1) < 64


def joined(even, odd):
    return jnp.where(low_half(even.shape), even, pltpu.roll(odd, 64, 1))


def joined_high(even, odd):
    return jnp.where(low_half(even.shape), pltpu.roll(even, 64, 1), odd)


def dot(a, b, contract=(1, 0)):
    return lax.dot_general(a, b, (((contract[0],), (contract[1],)), ((), ())), preferred_element_type=F32)


def kernel(
    alpha_hbm, static_hbm, pert_hbm, std_hbm, lon_hbm, lat_hbm, jac_hbm, count_hbm, mask_hbm, error_hbm, weight_hbm,
    ga_hbm, gs_hbm,
    alpha, static, pert, std, lon, lat, jac, count, mask, error_row, weight_row,
    w, ss, sr, out, spread, rem, order, latp, latpt, spreader, squares, incs, isc, gsc, s2, r2, terms, gp, gz, to_piece,
    from_piece,
    fs0, fs1, rl0, rl1, xr0, xr1, rs0, rs1, r10, r11, ag0, ag1,
    bs0, bs1, bl0, bl1, br0, br1, bss0, bss1, brs0, brs1, lhs0, lhs1,
    load_sem, std_sem, store_sem, f_send, f_recv, t_send, t_recv, a_send, a_recv, b_send, b_recv, c_send, c_recv,
    d_send, d_recv, e_send, e_recv, g_send, g_recv,
):
    fs, rl, xr, rs, r1, ag = (fs0, fs1), (rl0, rl1), (xr0, xr1), (rs0, rs1), (r10, r11), (ag0, ag1)
    bs, bl, br, bss, brs, lhs = (bs0, bs1), (bl0, bl1), (br0, br1), (bss0, bss1), (brs0, brs1), (lhs0, lhs1)
    lanes = [slice(BASE[c], BASE[c] + 128 * TILES[c]) for c in range(CHUNKS)]

    mem, band = lax.axis_index("mem"), lax.axis_index("band")
    z, x, y = mem // 8, (mem // 4) % 2, mem % 4
    t = 2 * z + x
    chip, core = band // 2, band % 2
    sib, far, cross = 2 * chip + 1 - core, 2 * (1 - chip) + core, 3 - band

    def at_band(b):
        return {"mem": mem, "band": b}

    ys = [lax.rem(y + k, YN) for k in range(1, YN)]
    to_y = [{"mem": 8 * z + 4 * x + v, "band": band} for v in ys]
    ts = [lax.rem(t + k, TN) for k in range(1, TN)]
    to_t = [{"mem": 8 * (v // 2) + 4 * (v % 2) + y, "band": band} for v in ts]

    staged = [(lon_hbm, lon), (alpha_hbm, alpha), (static_hbm, static), (lat_hbm, lat),
              (pert_hbm.reshape(MEMB, S * COLS, LAT), pert), (jac_hbm, jac), (count_hbm, count), (mask_hbm, mask),
              (error_hbm, error_row), (weight_hbm, weight_row)]
    loads = [pltpu.make_async_copy(src, dst, load_sem.at[i]) for i, (src, dst) in enumerate(staged)]
    loads += [pltpu.make_async_copy(std_hbm.at[:, s, :], std.at[s], std_sem.at[s]) for s in range(S)]
    for load in loads:
        load.start()

    barrier = pltpu.get_barrier_semaphore()
    partners = [at_band(far), at_band(cross)] + to_t + to_y + [at_band(sib)]
    for device in partners:
        pl.semaphore_signal(barrier, inc=1, device_id=device, device_id_type=MESH)

    def remote(src, dst, send, recv, device):
        return pltpu.make_async_remote_copy(
            src_ref=src, dst_ref=dst, send_sem=send, recv_sem=recv, device_id=device, device_id_type=MESH)

    sent = []

    loads[0].wait()
    for b in range(4):
        w[:, 512 + 64 * b : 512 + 64 * b + REM] = lon[:, COLS * b + 128 : COLS * b + COLS]
        w[:, 512 + 64 * b + REM : 576 + 64 * b] = jnp.zeros((LON, 64 - REM), BF16)
        w[:, 128 * b : 128 * b + 128] = lon[:, COLS * b : COLS * b + 128]

    forward = []
    loads[1].wait()
    for c in range(CHUNKS):
        v = dot(alpha[...].reshape(MEMB * S * ROWS, LON), w[:, lanes[c]])
        v = v.reshape(MEMB, S, ROWS, 128 * TILES[c])
        for m in range(MEMB):
            for b in range(4):
                if c == 0:
                    tile = 128 * (b // 2)
                    join = joined if b % 2 == 0 else joined_high
                    for h in range(2):
                        pair = join(v[m, 2 * h][:, tile : tile + 128], v[m, 2 * h + 1][:, tile : tile + 128])
                        fs[c][b, m, :, 128 * h : 128 * h + 128] = pair.astype(BF16)
                else:
                    for s in range(S):
                        fs[c][b, m, :, 128 * s : 128 * s + 128] = v[m, s][:, 128 * b : 128 * b + 128].astype(BF16)
        copies = [
            remote(fs[c].at[far], xr[c].at[band], f_send.at[c, 0], f_recv.at[c, 0], at_band(far)),
            remote(fs[c].at[cross], rl[c], f_send.at[c, 1], f_recv.at[c, 1], at_band(sib)),
            remote(fs[c].at[sib], xr[c].at[band], f_send.at[c, 2], f_recv.at[c, 2], at_band(sib)),
            remote(rl[c], xr[c].at[sib], f_send.at[c, 3], f_recv.at[c, 3], at_band(far)),
        ]
        forward.append(copies)
        xr[c][band] = fs[c][band]

    loads[2].wait()
    loads[3].wait()
    v = dot(static[...].reshape(S * ROWS, LON), w[...]).astype(BF16)
    own_rows = dot(one_hot(16, LAT, lambda k: jnp.where(k < OWN, OWN * mem + k, -1)), lat[...]).astype(BF16)
    here = jnp.where(iota((LAT, ROWS), 0) == ROWS * band + iota((LAT, ROWS), 1), 1.0, 0.0).astype(BF16)
    own_part = dot(own_rows, here).astype(BF16)
    parts = [dot(own_part, v[ROWS * s : ROWS * s + ROWS])[0:8] for s in range(S)]
    for b in range(4):
        tile = 512 + 128 * (b // 2)
        join = joined if b % 2 == 0 else joined_high
        for s in range(S):
            ss[b, :, 128 * s : 128 * s + 128] = parts[s][:, 128 * b : 128 * b + 128]
        for h in range(2):
            ss[b, :, 512 + 128 * h : 640 + 128 * h] = join(
                parts[2 * h][:, tile : tile + 128], parts[2 * h + 1][:, tile : tile + 128])
    others = (far, cross, sib)
    static_copies = [remote(ss.at[b], sr.at[band], t_send.at[k], t_recv.at[k], at_band(b)) for k, b in enumerate(others)]
    sr[band] = ss[band]
    order[...] = one_hot(LAT, LAT, grid_row)
    latp[...] = dot(order[...], lat[...]).astype(BF16)
    pl.semaphore_wait(barrier, len(partners))
    for c, k in ((0, 0), (0, 1), (1, 1)):
        forward[c][k].start()
    forward[0][1].wait_recv()
    forward[0][3].start()
    forward[1][0].start()
    forward[1][1].wait_recv()
    forward[1][3].start()
    for copy in [forward[0][2], forward[1][2]] + static_copies:
        copy.start()

    spreader[...] = one_hot(S * COLS, WIDE, packed_lane)
    loads[9].wait()
    weights = weight_row[...].astype(F32)
    coef = weights / jnp.sqrt(jnp.sum(weights * weights, axis=1, keepdims=True))
    loads[4].wait()
    for m in range(MEMB):
        factor = 0.8 * jnp.sum(jnp.where(iota(coef.shape, 1) == MEMB * mem + m, coef, 0.0), axis=1, keepdims=True)
        ordered = dot(order[...], pert[m], (1, 1)).astype(BF16)
        spread[m, 0:LAT] = factor * dot(ordered, spreader[...])
    to_piece[...] = one_hot(TN * PIECE, ALL * ROWS, piece_row)

    def sum_first(c):
        for k in (0, 2, 3):
            forward[c][k].wait_recv()
        total = None
        for m in range(MEMB):
            field = dot(latp[...], xr[c][:, m].reshape(LAT, 128 * TILES[c]))
            term = spread[m, 0:LAT, lanes[c]] * field
            total = term if total is None else total + term
        rs[c][...] = total.astype(BF16).reshape(YN, ROWS, 128 * TILES[c])
        copies = [
            remote(rs[c].at[ys[k]], r1[c].at[k], a_send.at[c, k], a_recv.at[c, k], to_y[k]) for k in range(YN - 1)]
        for copy in copies:
            copy.start()
        sent.extend(forward[c])
        return copies

    source, half = far + (cross - far) * (y // 2), y % 2

    def adjoint(c, fourth):
        for copy in fourth:
            copy.wait_recv()
        sent.extend(fourth)
        gradient = ag[c][...].reshape(LAT, 128 * TILES[c]).astype(F32)
        width = 64 * TILES[c]
        back = dot(latpt[...], (spread[MEMB, 0:LAT, lanes[c]] * gradient).astype(BF16)).astype(BF16)
        back = back.reshape(4, ROWS, 128 * TILES[c])
        for h in range(2):
            bss[c][h] = back[:, :, width * h : width * h + width]
        fixed = [
            remote(bss[c].at[half, source], brs[c].at[half, band], g_send.at[c, 0], g_recv.at[c, 0], at_band(source)),
            remote(bss[c].at[:, sib], brs[c].at[:, band], g_send.at[c, 1], g_recv.at[c, 1], at_band(sib)),
        ] + [
            remote(brs[c].at[half, source], brs[c].at[half, source], g_send.at[c, 2 + k], g_recv.at[c, 2 + k], to_y[k])
            for k in range(YN - 1)]
        for copy in fixed[:2]:
            copy.start()
        for m in range(MEMB):
            back = dot(latpt[...], (spread[m, 0:LAT, lanes[c]] * gradient).astype(BF16)).astype(BF16)
            bs[c][:, m] = back.reshape(4, ROWS, 128 * TILES[c])
        copies = [
            remote(bs[c].at[far], br[c].at[band], e_send.at[c, 0], e_recv.at[c, 0], at_band(far)),
            remote(bs[c].at[cross], bl[c], e_send.at[c, 1], e_recv.at[c, 1], at_band(sib)),
            remote(bs[c].at[sib], br[c].at[band], e_send.at[c, 2], e_recv.at[c, 2], at_band(sib)),
            remote(bl[c], br[c].at[sib], e_send.at[c, 3], e_recv.at[c, 3], at_band(far)),
        ]
        for copy in copies[:3]:
            copy.start()
        br[c][band] = bs[c][band]
        for h in range(2):
            brs[c][h, band] = bss[c][h, band]
        return copies, fixed

    def pass_on(c, copies, fixed):
        copies[1].wait_recv()
        copies[3].start()
        fixed[0].wait_recv()
        for copy in fixed[2:]:
            copy.start()

    first = [sum_first(0)]

    for load in loads[10:]:
        load.wait()
    rem[...] = jnp.zeros_like(rem)
    for h in range(2):
        for s in range(2):
            value = std[2 * h + s]
            ordered = None
            for _ in range(3):
                top = value.astype(BF16)
                term = dot(order[...], top, (1, 1))
                ordered = term if ordered is None else ordered + term
                value = value - top.astype(F32)
            ordered = 0.6 * ordered
            spread[MEMB, 0:LAT, 128 * (2 * h + s) : 128 * (2 * h + s) + 128] = ordered[:, 0:128]
            rem[s, :, 0:REM] = ordered[:, 128:COLS]
        spread[MEMB, 0:LAT, 512 + 128 * h : 640 + 128 * h] = joined(rem[0], rem[1])

    first.append(sum_first(1))
    spread[:, LAT:] = jnp.zeros((FIELDS, 8, WIDE), F32)
    first_row = ROWS * y + OWN * t
    shift = first_row % 8
    own_std = spread[MEMB, pl.ds(pl.multiple_of(first_row - shift, 8), 16), :]
    own_std = pltpu.roll(own_std, (16 - shift) % 16, 0)[0:8]
    for copy in static_copies:
        copy.wait_recv()
    sent.extend(static_copies)
    static_term = own_std * (sr[0] + sr[1] + sr[2] + sr[3])
    terms[...] = jnp.zeros_like(terms)
    for l in range(ALL):
        terms[OWN * l : OWN * l + OWN] = static_term[0:OWN, 128 * l : 128 * l + 128]

    tiles = [None] * ALL
    for c in range(CHUNKS):
        for copy in first[c]:
            copy.wait_recv()
        sent.extend(first[c])
        total = rs[c][y].astype(F32)
        for k in range(YN - 1):
            total = total + r1[c][k].astype(F32)
        for l in range(TILES[c]):
            tiles[BASE[c] // 128 + l] = total[:, 128 * l : 128 * l + 128].astype(BF16)
    s2[...] = dot(to_piece[...], jnp.concatenate(tiles, axis=0)).astype(BF16).reshape(TN, PIECE, 128)
    second = [remote(s2.at[ts[k]], r2.at[k], b_send.at[k], b_recv.at[k], to_t[k]) for k in range(TN - 1)]
    for copy in second:
        copy.start()
    latpt[...] = dot(jnp.transpose(lat[...].astype(F32)).astype(BF16), order[...], (1, 1)).astype(BF16)
    hot = iota((ALL * ROWS, TN * PIECE), 0) == piece_row(iota((ALL * ROWS, TN * PIECE), 1))
    from_piece[...] = jnp.where(hot, 1.0, 0.0).astype(BF16)
    for load in loads[5:9]:
        load.wait()
    error = jnp.sum(jnp.where(iota((CH, CH), 0) == iota((CH, CH), 1), error_row[...], 0.0), axis=1, keepdims=True)
    squares[...] = jnp.broadcast_to(error * error, squares.shape)

    for copy in second:
        copy.wait_recv()
    sent.extend(second)
    total = terms[...] + s2[t].astype(F32)
    for k in range(TN - 1):
        total = total + r2[k].astype(F32)
    turned = pltpu.roll(total, 64, 1)
    for s in range(S):
        row = OWN * (4 + s // 2)
        isc[s, 0:OWN, 0:128] = total[OWN * s : OWN * s + OWN]
        isc[s, 0:OWN, 128:256] = (total if s % 2 == 0 else turned)[row : row + OWN]
    for i in range(OWN):
        for s in range(S):
            incs[i, s : s + 1, :] = isc[s, i : i + 1, :]
    inc = [incs[i, 0:S, 0:COLS] for i in range(OWN)]
    counts = count[...].astype(F32)

    def channels(step, grads):
        base = pl.multiple_of(8 * step, 8)
        square = squares[pl.ds(base, 8), 0:1]
        grads = list(grads)
        for i in range(OWN):
            weight = mask[i, pl.ds(base, 8), :].astype(F32) * counts[i : i + 1, :] / square
            for n in range(8):
                jac_n = jac[base + n, i].astype(F32)
                radiance = jnp.sum(jac_n * inc[i], axis=0, keepdims=True)
                grads[i] = grads[i] + jac_n * (weight[n : n + 1, :] * radiance)
        return tuple(grads)

    grads = lax.fori_loop(0, CH // 8, channels, tuple(jnp.zeros((S, COLS), F32) for _ in range(OWN)))
    gsc[...] = jnp.zeros_like(gsc)
    for i in range(OWN):
        for s in range(S):
            gsc[s, i : i + 1, 0:COLS] = grads[i][s : s + 1, :].astype(BF16).astype(F32)
    piece = [gsc[s, 0:OWN, 0:128] for s in range(S)]
    piece += [joined(gsc[2 * h, :, 128:256], gsc[2 * h + 1, :, 128:256])[0:OWN] for h in range(2)]
    gp[...] = jnp.concatenate(piece + [jnp.zeros((PIECE - ALL * OWN, 128), F32)], axis=0).astype(BF16)

    third = [remote(gp, gz.at[t], c_send.at[k], c_recv.at[k], to_t[k]) for k in range(TN - 1)]
    for copy in third:
        copy.start()
    gz[t] = gp[...]
    for copy in third:
        copy.wait_recv()
    sent.extend(third)
    tall = dot(from_piece[...], gz[...].reshape(TN * PIECE, 128)).astype(BF16)
    fourth = []
    for c in range(CHUNKS):
        for l in range(TILES[c]):
            row = ROWS * (BASE[c] // 128 + l)
            ag[c][y, :, 128 * l : 128 * l + 128] = tall[row : row + ROWS]
        copies = [remote(ag[c].at[y], ag[c].at[y], d_send.at[c, k], d_recv.at[c, k], to_y[k]) for k in range(YN - 1)]
        for copy in copies:
            copy.start()
        fourth.append(copies)

    ways = [adjoint(0, fourth[0])]
    pass_on(0, *ways[0])

    ways.append(adjoint(1, fourth[1]))

    copies, fixed = ways[0]
    for copy in copies[:1] + copies[2:] + fixed[1:]:
        copy.wait_recv()
    for f in range(FIELDS):
        for h in range(2):
            if f < MEMB:
                tiles = [br[0][b, f, :, 128 * h : 128 * h + 128].astype(F32) for b in range(4)]
            else:
                tiles = [brs[0][h, b].astype(F32) for b in range(4)]
            for s in range(2):
                join = joined if s == 0 else joined_high
                for g in range(2):
                    pair = join(tiles[2 * g], tiles[2 * g + 1]).astype(BF16)
                    lhs[0][pl.ds((2 * h + s) * ROWS, ROWS), 128 * g : 128 * g + 128] = pair
        base = alpha[f] if f < MEMB else static[...]
        out[f] = base.astype(F32) + dot(lhs[0][...], w[:, lanes[0]], (1, 1)).reshape(S, ROWS, LON)
        if f == 0:
            ways[1][0][1].wait_recv()
            ways[1][0][3].start()
    ways[1][1][0].wait_recv()
    for copy in ways[1][1][2:]:
        copy.start()

    stores = []
    copies, fixed = ways[1]
    for f in range(FIELDS):
        if f == 0:
            for copy in copies[:1] + copies[2:]:
                copy.wait_recv()
        if f == MEMB:
            for copy in fixed[1:]:
                copy.wait_recv()
        for s in range(S):
            for b in range(4):
                if f < MEMB:
                    tile = br[1][b, f, :, 128 * s : 128 * s + 128]
                else:
                    tile = brs[1][s // 2, b, :, 128 * (s % 2) : 128 * (s % 2) + 128]
                lhs[1][ROWS * s : ROWS * s + ROWS, 128 * b : 128 * b + 128] = tile
        out[f] = out[f] + dot(lhs[1][...], w[:, lanes[1]], (1, 1)).reshape(S, ROWS, LON)
        store = pltpu.make_async_copy(out.at[f], ga_hbm.at[f] if f < MEMB else gs_hbm, store_sem.at[f])
        store.start()
        stores.append(store)
    for copies, fixed in ways:
        sent.extend(copies)
        sent.extend(fixed)
    for store in stores:
        store.wait()
    for copy in sent:
        copy.wait_send()


def shards(alpha, static_ctl, perturbations, static_std, lon_root, lat_root, jacobian, obs_count, channel_mask,
           channel_error, member_weight):
    inputs = [alpha, static_ctl, jnp.transpose(perturbations, (0, 3, 1, 2)), jnp.transpose(static_std, (2, 0, 1)),
              lon_root, lat_root, jnp.transpose(jacobian, (0, 2, 1, 3)), obs_count, jnp.transpose(channel_mask, (1, 0, 2)),
              channel_error.reshape(1, CH), member_weight.reshape(1, MEM)]
    dma, vmem = pltpu.SemaphoreType.DMA, pltpu.VMEM
    scratch = [
        vmem((MEMB, S, ROWS, LON), BF16),
        vmem((S, ROWS, LON), BF16),
        vmem((MEMB, S * COLS, LAT), BF16),
        vmem((S, COLS, LAT), F32),
        vmem((LON, LON), BF16),
        vmem((LAT, LAT), BF16),
        vmem((CH, OWN, S, COLS), BF16),
        vmem((OWN, COLS), I32),
        vmem((OWN, CH, COLS), I32),
        vmem((1, CH), F32),
        vmem((1, MEM), I32),
        vmem((LON, WIDE), BF16),
        vmem((4, 8, WIDE), F32),
        vmem((4, 8, WIDE), F32),
        vmem((FIELDS, S, ROWS, LON), F32),
        vmem((FIELDS, LAT + 8, WIDE), F32),
        vmem((2, LAT, 128), F32),
        vmem((LAT, LAT), BF16),
        vmem((LAT, LAT), BF16),
        vmem((LAT, LAT), BF16),
        vmem((S * COLS, WIDE), BF16),
        vmem((CH, 128), F32),
        vmem((OWN, 8, 256), F32),
        vmem((S, 8, 256), F32),
        vmem((S, 8, 256), F32),
        vmem((TN, PIECE, 128), BF16),
        vmem((TN - 1, PIECE, 128), BF16),
        vmem((PIECE, 128), F32),
        vmem((PIECE, 128), BF16),
        vmem((TN, PIECE, 128), BF16),
        vmem((TN * PIECE, ALL * ROWS), BF16),
        vmem((ALL * ROWS, TN * PIECE), BF16),
    ]

    def both(shape, kind):
        return [vmem(shape(128 * TILES[c]), kind) for c in range(CHUNKS)]

    scratch += both(lambda n: (4, MEMB, ROWS, n), BF16)
    scratch += both(lambda n: (MEMB, ROWS, n), BF16)
    scratch += both(lambda n: (4, MEMB, ROWS, n), BF16)
    scratch += both(lambda n: (YN, ROWS, n), BF16)
    scratch += both(lambda n: (YN - 1, ROWS, n), BF16)
    scratch += both(lambda n: (YN, ROWS, n), BF16)
    scratch += both(lambda n: (4, MEMB, ROWS, n), BF16)
    scratch += both(lambda n: (MEMB, ROWS, n), BF16)
    scratch += both(lambda n: (4, MEMB, ROWS, n), BF16)
    scratch += both(lambda n: (2, 4, ROWS, n // 2), BF16)
    scratch += both(lambda n: (2, 4, ROWS, n // 2), BF16)
    scratch += both(lambda n: (S * ROWS, n), BF16)
    scratch += [
        dma((10,)), dma((S,)), dma((FIELDS,)),
        dma((2, 4)), dma((2, 4)), dma((3,)), dma((3,)),
        dma((2, YN - 1)), dma((2, YN - 1)), dma((TN - 1,)), dma((TN - 1,)),
        dma((TN - 1,)), dma((TN - 1,)), dma((2, YN - 1)), dma((2, YN - 1)),
        dma((2, 4)), dma((2, 4)), dma((2, YN + 1)), dma((2, YN + 1)),
    ]
    anywhere = pl.BlockSpec(memory_space=pl.ANY)
    return pl.pallas_call(
        kernel,
        out_shape=(jax.ShapeDtypeStruct((MEMB, S, ROWS, LON), F32), jax.ShapeDtypeStruct((S, ROWS, LON), F32)),
        in_specs=[pl.BlockSpec(memory_space=pltpu.HBM)] * len(inputs),
        out_specs=(anywhere, anywhere),
        scratch_shapes=scratch,
        compiler_params=pltpu.CompilerParams(collective_id=0, has_side_effects=True, vmem_limit_bytes=40 << 20),
        name="hessian",
    )(*[pltpu.with_memory_space_constraint(v, pltpu.HBM) for v in inputs])


def solution(mesh):
    in_specs = (
        P("mem", None, "band", None),
        P(None, "band", None),
        P("mem", None, None, "band"),
        P(None, None, "band"),
        P(),
        P(),
        P(None, None, "mem", "band"),
        P("mem", "band"),
        P(None, "mem", "band"),
        P(),
        P(),
    )
    out_specs = (P("mem", None, "band", None), P(None, "band", None))
    return jax.shard_map(shards, mesh=mesh, in_specs=in_specs, out_specs=out_specs, check_vma=False)
```

```python
import functools

import jax
import jax.numpy as jnp
from jax import lax
from jax.experimental import pallas as pl
from jax.experimental.pallas import tpu as pltpu
from jax.sharding import PartitionSpec as P

MESH = pl.DeviceIdType.MESH
F32, BF16, I32 = jnp.float32, jnp.bfloat16, jnp.int32

S, CH, MEM, MEMB, FIELDS = 4, 32, 128, 2, 3
ROWS, LAT, LON, COLS = 80, 320, 720, 180
REM = COLS - 128
YN, TN, OWN = 4, 16, 5
WIDE = 768
CHUNKS = 2
TILES = (2, 4)
BASE = (512, 0)
PIECE = (16, 32)
SPAN = ((128, COLS), (0, 128))


def iota(shape, dim):
    return lax.broadcasted_iota(I32, shape, dim)


def one_hot(rows, columns, column_of_row):
    return jnp.where(iota((rows, columns), 1) == column_of_row(iota((rows, columns), 0)), 1.0, 0.0).astype(BF16)


def fifth(x):
    return (x * 205) // 1024


def grid_row(p):
    y = p // ROWS
    t = fifth(p - ROWS * y)
    return OWN * (8 * (t // 2) + 4 * (t % 2) + y) + p - ROWS * y - OWN * t


def packed_lane(row):
    j, s = row // 4, row % 4
    return jnp.where(j < 128, 128 * s + j, 512 + 128 * (s // 2) + 64 * (s % 2) + j - 128)


def piece_row(c, a):
    t, r = a // PIECE[c], a % PIECE[c]
    tile = fifth(r)
    return jnp.where(r < TILES[c] * OWN, ROWS * tile + OWN * t + r - OWN * tile, -1)


def low_half(shape):
    return iota(shape, len(shape) - 1) < 64


def joined(even, odd):
    return jnp.where(low_half(even.shape), even, pltpu.roll(odd, 64, 1))


def joined_high(even, odd):
    return jnp.where(low_half(even.shape), pltpu.roll(even, 64, 1), odd)


def dot(a, b, contract=(1, 0)):
    return lax.dot_general(a, b, (((contract[0],), (contract[1],)), ((), ())), preferred_element_type=F32)


def kernel(
    alpha_hbm, static_hbm, pert_hbm, std_hbm, lon_hbm, lat_hbm, jac_hbm, count_hbm, mask_hbm, error_hbm, weight_hbm,
    ga_hbm, gs_hbm,
    alpha, static, pert, std, lon, lat, jac, count, mask, error_row, weight_row,
    w, ss, sr, out, spread, rem, order, latp, latpt, spreader, squares, incs, gr,
    fs0, fs1, rl0, rl1, xr0, xr1, rs0, rs1, r10, r11, s20, s21, r20, r21, terms0, terms1, gp0, gp1, gz0, gz1, ag0, ag1,
    bs0, bs1, bl0, bl1, br0, br1, bss0, bss1, brs0, brs1, to0, to1, from0, from1, lhs0, lhs1,
    load_sem, std_sem, store_sem, f_send, f_recv, t_send, t_recv, a_send, a_recv, b_send, b_recv, c_send, c_recv,
    d_send, d_recv, e_send, e_recv, g_send, g_recv,
):
    fs, rl, xr, rs, r1, s2, r2 = (fs0, fs1), (rl0, rl1), (xr0, xr1), (rs0, rs1), (r10, r11), (s20, s21), (r20, r21)
    terms, gp, gz, ag, bs, bl, br = (terms0, terms1), (gp0, gp1), (gz0, gz1), (ag0, ag1), (bs0, bs1), (bl0, bl1), (br0, br1)
    bss, brs, to_piece, from_piece, lhs = (bss0, bss1), (brs0, brs1), (to0, to1), (from0, from1), (lhs0, lhs1)
    lanes = [slice(BASE[c], BASE[c] + 128 * TILES[c]) for c in range(CHUNKS)]

    mem, band = lax.axis_index("mem"), lax.axis_index("band")
    z, x, y = mem // 8, (mem // 4) % 2, mem % 4
    t = 2 * z + x
    chip, core = band // 2, band % 2
    sib, far, cross = 2 * chip + 1 - core, 2 * (1 - chip) + core, 3 - band

    def at_band(b):
        return {"mem": mem, "band": b}

    ys = [lax.rem(y + k, YN) for k in range(1, YN)]
    to_y = [{"mem": 8 * z + 4 * x + v, "band": band} for v in ys]
    ts = [lax.rem(t + k, TN) for k in range(1, TN)]
    to_t = [{"mem": 8 * (v // 2) + 4 * (v % 2) + y, "band": band} for v in ts]

    staged = [(lon_hbm, lon), (alpha_hbm, alpha), (static_hbm, static), (lat_hbm, lat),
              (pert_hbm.reshape(MEMB, S * COLS, LAT), pert), (jac_hbm, jac), (count_hbm, count), (mask_hbm, mask),
              (error_hbm, error_row), (weight_hbm, weight_row)]
    loads = [pltpu.make_async_copy(src, dst, load_sem.at[i]) for i, (src, dst) in enumerate(staged)]
    loads += [pltpu.make_async_copy(std_hbm.at[:, s, :], std.at[s], std_sem.at[s]) for s in range(S)]
    for load in loads:
        load.start()

    barrier = pltpu.get_barrier_semaphore()
    partners = [at_band(far), at_band(cross)] + to_t + to_y + [at_band(sib)]
    for device in partners:
        pl.semaphore_signal(barrier, inc=1, device_id=device, device_id_type=MESH)

    def remote(src, dst, send, recv, device):
        return pltpu.make_async_remote_copy(
            src_ref=src, dst_ref=dst, send_sem=send, recv_sem=recv, device_id=device, device_id_type=MESH)

    sent = []

    loads[0].wait()
    for b in range(4):
        w[:, 512 + 64 * b : 512 + 64 * b + REM] = lon[:, COLS * b + 128 : COLS * b + COLS]
        w[:, 512 + 64 * b + REM : 576 + 64 * b] = jnp.zeros((LON, 64 - REM), BF16)
        w[:, 128 * b : 128 * b + 128] = lon[:, COLS * b : COLS * b + 128]

    forward = []
    loads[1].wait()
    for c in range(CHUNKS):
        v = dot(alpha[...].reshape(MEMB * S * ROWS, LON), w[:, lanes[c]])
        v = v.reshape(MEMB, S, ROWS, 128 * TILES[c])
        for m in range(MEMB):
            for b in range(4):
                if c == 0:
                    tile = 128 * (b // 2)
                    join = joined if b % 2 == 0 else joined_high
                    for h in range(2):
                        pair = join(v[m, 2 * h][:, tile : tile + 128], v[m, 2 * h + 1][:, tile : tile + 128])
                        fs[c][b, m, :, 128 * h : 128 * h + 128] = pair.astype(BF16)
                else:
                    for s in range(S):
                        fs[c][b, m, :, 128 * s : 128 * s + 128] = v[m, s][:, 128 * b : 128 * b + 128].astype(BF16)
        copies = [
            remote(fs[c].at[far], xr[c].at[band], f_send.at[c, 0], f_recv.at[c, 0], at_band(far)),
            remote(fs[c].at[cross], rl[c], f_send.at[c, 1], f_recv.at[c, 1], at_band(sib)),
            remote(fs[c].at[sib], xr[c].at[band], f_send.at[c, 2], f_recv.at[c, 2], at_band(sib)),
            remote(rl[c], xr[c].at[sib], f_send.at[c, 3], f_recv.at[c, 3], at_band(far)),
        ]
        forward.append(copies)
        xr[c][band] = fs[c][band]

    loads[2].wait()
    loads[3].wait()
    v = dot(static[...].reshape(S * ROWS, LON), w[...]).astype(BF16)
    own_rows = dot(one_hot(16, LAT, lambda k: jnp.where(k < OWN, OWN * mem + k, -1)), lat[...]).astype(BF16)
    here = jnp.where(iota((LAT, ROWS), 0) == ROWS * band + iota((LAT, ROWS), 1), 1.0, 0.0).astype(BF16)
    own_part = dot(own_rows, here).astype(BF16)
    parts = [dot(own_part, v[ROWS * s : ROWS * s + ROWS])[0:8] for s in range(S)]
    for b in range(4):
        tile = 512 + 128 * (b // 2)
        join = joined if b % 2 == 0 else joined_high
        for s in range(S):
            ss[b, :, 128 * s : 128 * s + 128] = parts[s][:, 128 * b : 128 * b + 128]
        for h in range(2):
            ss[b, :, 512 + 128 * h : 640 + 128 * h] = join(
                parts[2 * h][:, tile : tile + 128], parts[2 * h + 1][:, tile : tile + 128])
    others = (far, cross, sib)
    static_copies = [remote(ss.at[b], sr.at[band], t_send.at[k], t_recv.at[k], at_band(b)) for k, b in enumerate(others)]
    sr[band] = ss[band]
    order[...] = one_hot(LAT, LAT, grid_row)
    latp[...] = dot(order[...], lat[...]).astype(BF16)
    pl.semaphore_wait(barrier, len(partners))
    for copy in forward[0][:3] + [forward[1][1]] + static_copies:
        copy.start()
    forward[0][1].wait_recv()
    forward[0][3].start()
    forward[1][0].start()
    forward[1][1].wait_recv()
    forward[1][3].start()
    forward[1][2].start()

    spreader[...] = one_hot(S * COLS, WIDE, packed_lane)
    loads[9].wait()
    weights = weight_row[...].astype(F32)
    coef = weights / jnp.sqrt(jnp.sum(weights * weights, axis=1, keepdims=True))
    loads[4].wait()
    for m in range(MEMB):
        factor = 0.8 * jnp.sum(jnp.where(iota(coef.shape, 1) == MEMB * mem + m, coef, 0.0), axis=1, keepdims=True)
        ordered = dot(order[...], pert[m], (1, 1)).astype(BF16)
        spread[m, 0:LAT] = factor * dot(ordered, spreader[...])
    for c in range(CHUNKS):
        rows, height = TN * PIECE[c], ROWS * TILES[c]
        to_piece[c][...] = one_hot(rows, height, lambda a: piece_row(c, a))

    def sum_first(c):
        for k in (0, 2, 3):
            forward[c][k].wait_recv()
        total = None
        for m in range(MEMB):
            field = dot(latp[...], xr[c][:, m].reshape(LAT, 128 * TILES[c]))
            term = spread[m, 0:LAT, lanes[c]] * field
            total = term if total is None else total + term
        rs[c][...] = total.astype(BF16).reshape(YN, ROWS, 128 * TILES[c])
        copies = [
            remote(rs[c].at[ys[k]], r1[c].at[k], a_send.at[c, k], a_recv.at[c, k], to_y[k]) for k in range(YN - 1)]
        for copy in copies:
            copy.start()
        sent.extend(forward[c])
        return copies

    def sum_second(c, first):
        for copy in first:
            copy.wait_recv()
        total = rs[c][y].astype(F32)
        for k in range(YN - 1):
            total = total + r1[c][k].astype(F32)
        total = total.astype(BF16)
        tall = jnp.concatenate([total[:, 128 * l : 128 * l + 128] for l in range(TILES[c])], axis=0)
        s2[c][...] = dot(to_piece[c][...], tall).astype(BF16).reshape(TN, PIECE[c], 128)
        copies = [
            remote(s2[c].at[ts[k]], r2[c].at[k], b_send.at[c, k], b_recv.at[c, k], to_t[k]) for k in range(TN - 1)]
        for copy in copies:
            copy.start()
        sent.extend(first)
        return copies

    def pixels(c, second):
        for copy in second:
            copy.wait_recv()
        sent.extend(second)
        total = terms[c][...] + s2[c][t].astype(F32)
        for k in range(TN - 1):
            total = total + r2[c][k].astype(F32)
        lo, hi = SPAN[c]
        turned = pltpu.roll(total, 64, 1) if c == 0 else None
        for i in range(OWN):
            for s in range(S):
                row = OWN * s + i if c else OWN * (s // 2) + i
                source = total if c or s % 2 == 0 else turned
                incs[i, s : s + 1, :] = source[row : row + 1, :]
        inc = [incs[i, 0:S, 0 : hi - lo] for i in range(OWN)]
        counts = count[:, lo:hi].astype(F32)

        def channels(step, grads):
            base = pl.multiple_of(8 * step, 8)
            square = squares[pl.ds(base, 8), 0:1]
            grads = list(grads)
            for i in range(OWN):
                weight = mask[i, pl.ds(base, 8), lo:hi].astype(F32) * counts[i : i + 1, :] / square
                for n in range(8):
                    jac_n = jac[base + n, i, :, lo:hi].astype(F32)
                    radiance = jnp.sum(jac_n * inc[i], axis=0, keepdims=True)
                    grads[i] = grads[i] + jac_n * (weight[n : n + 1, :] * radiance)
            return tuple(grads)

        grads = lax.fori_loop(0, CH // 8, channels, tuple(jnp.zeros((S, hi - lo), F32) for _ in range(OWN)))
        gr[...] = jnp.zeros_like(gr)
        for i in range(OWN):
            for s in range(S):
                row = OWN * s + i if c else OWN * (s // 2) + i
                half = 0 if c else s % 2
                gr[half, row : row + 1, 0 : hi - lo] = grads[i][s : s + 1, :].astype(BF16).astype(F32)
        gp[c][...] = (gr[0] if c else joined(gr[0, 0 : PIECE[0]], gr[1, 0 : PIECE[0]])).astype(BF16)
        copies = [remote(gp[c], gz[c].at[t], c_send.at[c, k], c_recv.at[c, k], to_t[k]) for k in range(TN - 1)]
        for copy in copies:
            copy.start()
        gz[c][t] = gp[c][...]
        return copies

    def gather(c, third):
        for copy in third:
            copy.wait_recv()
        sent.extend(third)
        tall = dot(from_piece[c][...], gz[c][...].reshape(TN * PIECE[c], 128)).astype(BF16)
        for l in range(TILES[c]):
            ag[c][y, :, 128 * l : 128 * l + 128] = tall[ROWS * l : ROWS * l + ROWS]
        copies = [remote(ag[c].at[y], ag[c].at[y], d_send.at[c, k], d_recv.at[c, k], to_y[k]) for k in range(YN - 1)]
        for copy in copies:
            copy.start()
        return copies

    source, half = far + (cross - far) * (y // 2), y % 2

    def adjoint(c, fourth):
        for copy in fourth:
            copy.wait_recv()
        sent.extend(fourth)
        gradient = ag[c][...].reshape(LAT, 128 * TILES[c]).astype(F32)
        width = 64 * TILES[c]
        back = dot(latpt[...], (spread[MEMB, 0:LAT, lanes[c]] * gradient).astype(BF16)).astype(BF16)
        back = back.reshape(4, ROWS, 128 * TILES[c])
        for h in range(2):
            bss[c][h] = back[:, :, width * h : width * h + width]
        fixed = [
            remote(bss[c].at[half, source], brs[c].at[half, band], g_send.at[c, 0], g_recv.at[c, 0], at_band(source)),
            remote(bss[c].at[:, sib], brs[c].at[:, band], g_send.at[c, 1], g_recv.at[c, 1], at_band(sib)),
        ] + [
            remote(brs[c].at[half, source], brs[c].at[half, source], g_send.at[c, 2 + k], g_recv.at[c, 2 + k], to_y[k])
            for k in range(YN - 1)]
        for copy in fixed[:2]:
            copy.start()
        for m in range(MEMB):
            back = dot(latpt[...], (spread[m, 0:LAT, lanes[c]] * gradient).astype(BF16)).astype(BF16)
            bs[c][:, m] = back.reshape(4, ROWS, 128 * TILES[c])
        copies = [
            remote(bs[c].at[far], br[c].at[band], e_send.at[c, 0], e_recv.at[c, 0], at_band(far)),
            remote(bs[c].at[cross], bl[c], e_send.at[c, 1], e_recv.at[c, 1], at_band(sib)),
            remote(bs[c].at[sib], br[c].at[band], e_send.at[c, 2], e_recv.at[c, 2], at_band(sib)),
            remote(bl[c], br[c].at[sib], e_send.at[c, 3], e_recv.at[c, 3], at_band(far)),
        ]
        for copy in copies[:3]:
            copy.start()
        br[c][band] = bs[c][band]
        for h in range(2):
            brs[c][h, band] = bss[c][h, band]
        return copies, fixed

    first = [sum_first(0)]

    for load in loads[10:]:
        load.wait()
    rem[...] = jnp.zeros_like(rem)
    for h in range(2):
        for s in range(2):
            value = std[2 * h + s]
            ordered = None
            for _ in range(3):
                top = value.astype(BF16)
                term = dot(order[...], top, (1, 1))
                ordered = term if ordered is None else ordered + term
                value = value - top.astype(F32)
            ordered = 0.6 * ordered
            spread[MEMB, 0:LAT, 128 * (2 * h + s) : 128 * (2 * h + s) + 128] = ordered[:, 0:128]
            rem[s, :, 0:REM] = ordered[:, 128:COLS]
        spread[MEMB, 0:LAT, 512 + 128 * h : 640 + 128 * h] = joined(rem[0], rem[1])

    spread[:, LAT:] = jnp.zeros((FIELDS, 8, WIDE), F32)
    first_row = ROWS * y + OWN * t
    shift = first_row % 8
    own_std = spread[MEMB, pl.ds(pl.multiple_of(first_row - shift, 8), 16), :]
    own_std = pltpu.roll(own_std, (16 - shift) % 16, 0)[0:8]
    for copy in static_copies:
        copy.wait_recv()
    sent.extend(static_copies)
    static_term = own_std * (sr[0] + sr[1] + sr[2] + sr[3])
    for c in range(CHUNKS):
        terms[c][...] = jnp.zeros_like(terms[c])
        for l in range(TILES[c]):
            terms[c][OWN * l : OWN * l + OWN] = static_term[0:OWN, BASE[c] + 128 * l : BASE[c] + 128 * l + 128]
    for load in loads[5:9]:
        load.wait()
    error = jnp.sum(jnp.where(iota((CH, CH), 0) == iota((CH, CH), 1), error_row[...], 0.0), axis=1, keepdims=True)
    squares[...] = jnp.broadcast_to(error * error, squares.shape)

    second = [sum_second(0, first[0])]
    latpt[...] = dot(jnp.transpose(lat[...].astype(F32)).astype(BF16), order[...], (1, 1)).astype(BF16)
    for c in range(CHUNKS):
        rows, height = TN * PIECE[c], ROWS * TILES[c]
        hot = iota((height, rows), 0) == piece_row(c, iota((height, rows), 1))
        from_piece[c][...] = jnp.where(hot, 1.0, 0.0).astype(BF16)

    first.append(sum_first(1))

    third = [pixels(0, second[0])]

    second.append(sum_second(1, first[1]))

    fourth = [gather(0, third[0])]

    third.append(pixels(1, second[1]))

    ways = [adjoint(0, fourth[0])]
    ways[0][0][1].wait_recv()
    ways[0][0][3].start()

    fourth.append(gather(1, third[1]))
    ways[0][1][0].wait_recv()
    for copy in ways[0][1][2:]:
        copy.start()

    ways.append(adjoint(1, fourth[1]))

    copies, fixed = ways[0]
    for copy in copies[:1] + copies[2:] + fixed[1:]:
        copy.wait_recv()
    for f in range(FIELDS):
        for h in range(2):
            if f < MEMB:
                tiles = [br[0][b, f, :, 128 * h : 128 * h + 128].astype(F32) for b in range(4)]
            else:
                tiles = [brs[0][h, b].astype(F32) for b in range(4)]
            for s in range(2):
                join = joined if s == 0 else joined_high
                for g in range(2):
                    pair = join(tiles[2 * g], tiles[2 * g + 1]).astype(BF16)
                    lhs[0][pl.ds((2 * h + s) * ROWS, ROWS), 128 * g : 128 * g + 128] = pair
        base = alpha[f] if f < MEMB else static[...]
        out[f] = base.astype(F32) + dot(lhs[0][...], w[:, lanes[0]], (1, 1)).reshape(S, ROWS, LON)
        if f == 0:
            ways[1][0][1].wait_recv()
            ways[1][0][3].start()
    ways[1][1][0].wait_recv()
    for copy in ways[1][1][2:]:
        copy.start()

    stores = []
    copies, fixed = ways[1]
    for f in range(FIELDS):
        if f == 0:
            for copy in copies[:1] + copies[2:]:
                copy.wait_recv()
        if f == MEMB:
            for copy in fixed[1:]:
                copy.wait_recv()
        for s in range(S):
            for b in range(4):
                if f < MEMB:
                    tile = br[1][b, f, :, 128 * s : 128 * s + 128]
                else:
                    tile = brs[1][s // 2, b, :, 128 * (s % 2) : 128 * (s % 2) + 128]
                lhs[1][ROWS * s : ROWS * s + ROWS, 128 * b : 128 * b + 128] = tile
        out[f] = out[f] + dot(lhs[1][...], w[:, lanes[1]], (1, 1)).reshape(S, ROWS, LON)
        store = pltpu.make_async_copy(out.at[f], ga_hbm.at[f] if f < MEMB else gs_hbm, store_sem.at[f])
        store.start()
        stores.append(store)
    for copies, fixed in ways:
        sent.extend(copies)
        sent.extend(fixed)
    for store in stores:
        store.wait()
    for copy in sent:
        copy.wait_send()


def shards(alpha, static_ctl, perturbations, static_std, lon_root, lat_root, jacobian, obs_count, channel_mask,
           channel_error, member_weight):
    inputs = [alpha, static_ctl, jnp.transpose(perturbations, (0, 3, 1, 2)), jnp.transpose(static_std, (2, 0, 1)),
              lon_root, lat_root, jnp.transpose(jacobian, (0, 2, 1, 3)), obs_count, jnp.transpose(channel_mask, (1, 0, 2)),
              channel_error.reshape(1, CH), member_weight.reshape(1, MEM)]
    dma, vmem = pltpu.SemaphoreType.DMA, pltpu.VMEM
    scratch = [
        vmem((MEMB, S, ROWS, LON), BF16),
        vmem((S, ROWS, LON), BF16),
        vmem((MEMB, S * COLS, LAT), BF16),
        vmem((S, COLS, LAT), F32),
        vmem((LON, LON), BF16),
        vmem((LAT, LAT), BF16),
        vmem((CH, OWN, S, COLS), BF16),
        vmem((OWN, COLS), I32),
        vmem((OWN, CH, COLS), I32),
        vmem((1, CH), F32),
        vmem((1, MEM), I32),
        vmem((LON, WIDE), BF16),
        vmem((4, 8, WIDE), F32),
        vmem((4, 8, WIDE), F32),
        vmem((FIELDS, S, ROWS, LON), F32),
        vmem((FIELDS, LAT + 8, WIDE), F32),
        vmem((2, LAT, 128), F32),
        vmem((LAT, LAT), BF16),
        vmem((LAT, LAT), BF16),
        vmem((LAT, LAT), BF16),
        vmem((S * COLS, WIDE), BF16),
        vmem((CH, 128), F32),
        vmem((OWN, 8, 128), F32),
        vmem((2, 32, 128), F32),
    ]

    def both(shape, kind):
        return [vmem(shape(128 * TILES[c], PIECE[c], ROWS * TILES[c]), kind) for c in range(CHUNKS)]

    scratch += both(lambda n, r, h: (4, MEMB, ROWS, n), BF16)
    scratch += both(lambda n, r, h: (MEMB, ROWS, n), BF16)
    scratch += both(lambda n, r, h: (4, MEMB, ROWS, n), BF16)
    scratch += both(lambda n, r, h: (YN, ROWS, n), BF16)
    scratch += both(lambda n, r, h: (YN - 1, ROWS, n), BF16)
    scratch += both(lambda n, r, h: (TN, r, 128), BF16)
    scratch += both(lambda n, r, h: (TN - 1, r, 128), BF16)
    scratch += both(lambda n, r, h: (r, 128), F32)
    scratch += both(lambda n, r, h: (r, 128), BF16)
    scratch += both(lambda n, r, h: (TN, r, 128), BF16)
    scratch += both(lambda n, r, h: (YN, ROWS, n), BF16)
    scratch += both(lambda n, r, h: (4, MEMB, ROWS, n), BF16)
    scratch += both(lambda n, r, h: (MEMB, ROWS, n), BF16)
    scratch += both(lambda n, r, h: (4, MEMB, ROWS, n), BF16)
    scratch += both(lambda n, r, h: (2, 4, ROWS, n // 2), BF16)
    scratch += both(lambda n, r, h: (2, 4, ROWS, n // 2), BF16)
    scratch += both(lambda n, r, h: (TN * r, h), BF16)
    scratch += both(lambda n, r, h: (h, TN * r), BF16)
    scratch += both(lambda n, r, h: (S * ROWS, n), BF16)
    scratch += [
        dma((10,)), dma((S,)), dma((FIELDS,)),
        dma((2, 4)), dma((2, 4)), dma((3,)), dma((3,)),
        dma((2, YN - 1)), dma((2, YN - 1)), dma((2, TN - 1)), dma((2, TN - 1)),
        dma((2, TN - 1)), dma((2, TN - 1)), dma((2, YN - 1)), dma((2, YN - 1)),
        dma((2, 4)), dma((2, 4)), dma((2, YN + 1)), dma((2, YN + 1)),
    ]
    anywhere = pl.BlockSpec(memory_space=pl.ANY)
    return pl.pallas_call(
        kernel,
        out_shape=(jax.ShapeDtypeStruct((MEMB, S, ROWS, LON), F32), jax.ShapeDtypeStruct((S, ROWS, LON), F32)),
        in_specs=[pl.BlockSpec(memory_space=pltpu.HBM)] * len(inputs),
        out_specs=(anywhere, anywhere),
        scratch_shapes=scratch,
        compiler_params=pltpu.CompilerParams(collective_id=0, has_side_effects=True, vmem_limit_bytes=40 << 20),
        name="hessian",
    )(*[pltpu.with_memory_space_constraint(v, pltpu.HBM) for v in inputs])


def solution(mesh):
    in_specs = (
        P("mem", None, "band", None),
        P(None, "band", None),
        P("mem", None, None, "band"),
        P(None, None, "band"),
        P(),
        P(),
        P(None, None, "mem", "band"),
        P("mem", "band"),
        P(None, "mem", "band"),
        P(),
        P(),
    )
    out_specs = (P("mem", None, "band", None), P(None, "band", None))
    return jax.shard_map(shards, mesh=mesh, in_specs=in_specs, out_specs=out_specs, check_vma=False)
```

```python
import functools

import jax
import jax.numpy as jnp
from jax import lax
from jax.experimental import pallas as pl
from jax.experimental.pallas import tpu as pltpu
from jax.sharding import PartitionSpec as P

MESH = pl.DeviceIdType.MESH
F32, BF16, I32 = jnp.float32, jnp.bfloat16, jnp.int32

S, CH, MEM, MEMB, FIELDS = 4, 32, 128, 2, 3
ROWS, LAT, LON, COLS = 80, 320, 720, 180
REM = COLS - 128
YN, TN, OWN = 4, 16, 5
WIDE = 768
NEXT_Y, NEXT_T = (2, 1, 3), (8, 7, 9, 6, 10, 5, 11, 4, 12, 3, 13, 2, 14, 1, 15)
CHUNKS = 2
TILES = (2, 4)
BASE = (512, 0)
PIECE = (16, 32)
SPAN = ((128, COLS), (0, 128))


def iota(shape, dim):
    return lax.broadcasted_iota(I32, shape, dim)


def one_hot(rows, columns, column_of_row):
    return jnp.where(iota((rows, columns), 1) == column_of_row(iota((rows, columns), 0)), 1.0, 0.0).astype(BF16)


def fifth(x):
    return (x * 205) // 1024


def grid_row(p):
    y = p // ROWS
    t = fifth(p - ROWS * y)
    return OWN * (8 * (t // 2) + 4 * (t % 2) + y) + p - ROWS * y - OWN * t


def packed_lane(row):
    j, s = row // 4, row % 4
    return jnp.where(j < 128, 128 * s + j, 512 + 128 * (s // 2) + 64 * (s % 2) + j - 128)


def piece_row(c, a):
    t, r = a // PIECE[c], a % PIECE[c]
    tile = fifth(r)
    return jnp.where(r < TILES[c] * OWN, ROWS * tile + OWN * t + r - OWN * tile, -1)


def low_half(shape):
    return iota(shape, len(shape) - 1) < 64


def joined(even, odd):
    return jnp.where(low_half(even.shape), even, pltpu.roll(odd, 64, 1))


def joined_high(even, odd):
    return jnp.where(low_half(even.shape), pltpu.roll(even, 64, 1), odd)


def dot(a, b, contract=(1, 0)):
    return lax.dot_general(a, b, (((contract[0],), (contract[1],)), ((), ())), preferred_element_type=F32)


def kernel(
    alpha_hbm, static_hbm, pert_hbm, std_hbm, lon_hbm, lat_hbm, jac_hbm, count_hbm, mask_hbm, error_hbm, weight_hbm,
    ga_hbm, gs_hbm,
    alpha, static, pert, std, lon, lat, jac, count, mask, error_row, weight_row,
    w, ss, sr, out, spread, rem, order, latp, latpt, spreader, squares, incs, gr,
    fs0, fs1, rl0, rl1, xr0, xr1, rs0, rs1, r10, r11, s20, s21, r20, r21, terms0, terms1, gp0, gp1, gz0, gz1, ag0, ag1,
    bs0, bs1, bl0, bl1, br0, br1, bss0, bss1, brs0, brs1, to0, to1, from0, from1, lhs0, lhs1,
    load_sem, std_sem, store_sem, f_send, f_recv, t_send, t_recv, a_send, a_recv, b_send, b_recv, c_send, c_recv,
    d_send, d_recv, e_send, e_recv, g_send, g_recv,
):
    fs, rl, xr, rs, r1, s2, r2 = (fs0, fs1), (rl0, rl1), (xr0, xr1), (rs0, rs1), (r10, r11), (s20, s21), (r20, r21)
    terms, gp, gz, ag, bs, bl, br = (terms0, terms1), (gp0, gp1), (gz0, gz1), (ag0, ag1), (bs0, bs1), (bl0, bl1), (br0, br1)
    bss, brs, to_piece, from_piece, lhs = (bss0, bss1), (brs0, brs1), (to0, to1), (from0, from1), (lhs0, lhs1)
    lanes = [slice(BASE[c], BASE[c] + 128 * TILES[c]) for c in range(CHUNKS)]

    mem, band = lax.axis_index("mem"), lax.axis_index("band")
    z, x, y = mem // 8, (mem // 4) % 2, mem % 4
    t = 2 * z + x
    chip, core = band // 2, band % 2
    sib, far, cross = 2 * chip + 1 - core, 2 * (1 - chip) + core, 3 - band

    def at_band(b):
        return {"mem": mem, "band": b}

    ys = [lax.rem(y + k, YN) for k in NEXT_Y]
    to_y = [{"mem": 8 * z + 4 * x + v, "band": band} for v in ys]
    ts = [lax.rem(t + k, TN) for k in NEXT_T]
    to_t = [{"mem": 8 * (v // 2) + 4 * (v % 2) + y, "band": band} for v in ts]

    staged = [(lon_hbm, lon), (alpha_hbm, alpha), (static_hbm, static), (lat_hbm, lat),
              (pert_hbm.reshape(MEMB, S * COLS, LAT), pert), (jac_hbm, jac), (count_hbm, count), (mask_hbm, mask),
              (error_hbm, error_row), (weight_hbm, weight_row)]
    loads = [pltpu.make_async_copy(src, dst, load_sem.at[i]) for i, (src, dst) in enumerate(staged)]
    loads += [pltpu.make_async_copy(std_hbm.at[:, s, :], std.at[s], std_sem.at[s]) for s in range(S)]
    for load in loads:
        load.start()

    barrier = pltpu.get_barrier_semaphore()
    partners = to_t + to_y + [at_band(far), at_band(cross), at_band(sib)]
    for device in partners:
        pl.semaphore_signal(barrier, inc=1, device_id=device, device_id_type=MESH)

    def remote(src, dst, send, recv, device):
        return pltpu.make_async_remote_copy(
            src_ref=src, dst_ref=dst, send_sem=send, recv_sem=recv, device_id=device, device_id_type=MESH)

    sent = []

    loads[0].wait()
    for b in range(4):
        w[:, 512 + 64 * b : 512 + 64 * b + REM] = lon[:, COLS * b + 128 : COLS * b + COLS]
        w[:, 512 + 64 * b + REM : 576 + 64 * b] = jnp.zeros((LON, 64 - REM), BF16)
        w[:, 128 * b : 128 * b + 128] = lon[:, COLS * b : COLS * b + 128]

    forward = []
    loads[1].wait()
    for c in range(CHUNKS):
        v = dot(alpha[...].reshape(MEMB * S * ROWS, LON), w[:, lanes[c]])
        v = v.reshape(MEMB, S, ROWS, 128 * TILES[c])
        for m in range(MEMB):
            for b in range(4):
                if c == 0:
                    tile = 128 * (b // 2)
                    join = joined if b % 2 == 0 else joined_high
                    for h in range(2):
                        pair = join(v[m, 2 * h][:, tile : tile + 128], v[m, 2 * h + 1][:, tile : tile + 128])
                        fs[c][b, m, :, 128 * h : 128 * h + 128] = pair.astype(BF16)
                else:
                    for s in range(S):
                        fs[c][b, m, :, 128 * s : 128 * s + 128] = v[m, s][:, 128 * b : 128 * b + 128].astype(BF16)
        copies = [
            remote(fs[c].at[far], xr[c].at[band], f_send.at[c, 0], f_recv.at[c, 0], at_band(far)),
            remote(fs[c].at[cross], rl[c], f_send.at[c, 1], f_recv.at[c, 1], at_band(sib)),
            remote(fs[c].at[sib], xr[c].at[band], f_send.at[c, 2], f_recv.at[c, 2], at_band(sib)),
            remote(rl[c], xr[c].at[sib], f_send.at[c, 3], f_recv.at[c, 3], at_band(far)),
        ]
        forward.append(copies)
        xr[c][band] = fs[c][band]

    loads[2].wait()
    loads[3].wait()
    v = dot(static[...].reshape(S * ROWS, LON), w[...]).astype(BF16)
    own_rows = dot(one_hot(16, LAT, lambda k: jnp.where(k < OWN, OWN * mem + k, -1)), lat[...]).astype(BF16)
    here = jnp.where(iota((LAT, ROWS), 0) == ROWS * band + iota((LAT, ROWS), 1), 1.0, 0.0).astype(BF16)
    own_part = dot(own_rows, here).astype(BF16)
    parts = [dot(own_part, v[ROWS * s : ROWS * s + ROWS])[0:8] for s in range(S)]
    for b in range(4):
        tile = 512 + 128 * (b // 2)
        join = joined if b % 2 == 0 else joined_high
        for s in range(S):
            ss[b, :, 128 * s : 128 * s + 128] = parts[s][:, 128 * b : 128 * b + 128]
        for h in range(2):
            ss[b, :, 512 + 128 * h : 640 + 128 * h] = join(
                parts[2 * h][:, tile : tile + 128], parts[2 * h + 1][:, tile : tile + 128])
    others = (far, cross, sib)
    static_copies = [remote(ss.at[b], sr.at[band], t_send.at[k], t_recv.at[k], at_band(b)) for k, b in enumerate(others)]
    sr[band] = ss[band]
    order[...] = one_hot(LAT, LAT, grid_row)
    latp[...] = dot(order[...], lat[...]).astype(BF16)
    pl.semaphore_wait(barrier, len(partners))
    for copy in forward[0][:3] + [forward[1][1]] + static_copies:
        copy.start()
    forward[0][1].wait_recv()
    forward[0][3].start()
    forward[1][0].start()
    forward[1][1].wait_recv()
    forward[1][3].start()
    forward[1][2].start()

    spreader[...] = one_hot(S * COLS, WIDE, packed_lane)
    loads[9].wait()
    weights = weight_row[...].astype(F32)
    coef = weights / jnp.sqrt(jnp.sum(weights * weights, axis=1, keepdims=True))
    loads[4].wait()
    for m in range(MEMB):
        factor = 0.8 * jnp.sum(jnp.where(iota(coef.shape, 1) == MEMB * mem + m, coef, 0.0), axis=1, keepdims=True)
        ordered = dot(order[...], pert[m], (1, 1)).astype(BF16)
        spread[m, 0:LAT] = factor * dot(ordered, spreader[...])
    for c in range(CHUNKS):
        rows, height = TN * PIECE[c], ROWS * TILES[c]
        to_piece[c][...] = one_hot(rows, height, lambda a: piece_row(c, a))

    def sum_first(c):
        for k in (0, 2, 3):
            forward[c][k].wait_recv()
        total = None
        for m in range(MEMB):
            field = dot(latp[...], xr[c][:, m].reshape(LAT, 128 * TILES[c]))
            term = spread[m, 0:LAT, lanes[c]] * field
            total = term if total is None else total + term
        rs[c][...] = total.astype(BF16).reshape(YN, ROWS, 128 * TILES[c])
        copies = [
            remote(rs[c].at[ys[k]], r1[c].at[k], a_send.at[c, k], a_recv.at[c, k], to_y[k]) for k in range(YN - 1)]
        for copy in copies:
            copy.start()
        sent.extend(forward[c])
        return copies

    def sum_second(c, first):
        for copy in first:
            copy.wait_recv()
        total = rs[c][y].astype(F32)
        for k in range(YN - 1):
            total = total + r1[c][k].astype(F32)
        total = total.astype(BF16)
        tall = jnp.concatenate([total[:, 128 * l : 128 * l + 128] for l in range(TILES[c])], axis=0)
        s2[c][...] = dot(to_piece[c][...], tall).astype(BF16).reshape(TN, PIECE[c], 128)
        copies = [
            remote(s2[c].at[ts[k]], r2[c].at[k], b_send.at[c, k], b_recv.at[c, k], to_t[k]) for k in range(TN - 1)]
        for copy in copies:
            copy.start()
        sent.extend(first)
        return copies

    def pixels(c, second):
        for copy in second:
            copy.wait_recv()
        sent.extend(second)
        total = terms[c][...] + s2[c][t].astype(F32)
        for k in range(TN - 1):
            total = total + r2[c][k].astype(F32)
        lo, hi = SPAN[c]
        turned = pltpu.roll(total, 64, 1) if c == 0 else None
        for i in range(OWN):
            for s in range(S):
                row = OWN * s + i if c else OWN * (s // 2) + i
                source = total if c or s % 2 == 0 else turned
                incs[i, s : s + 1, :] = source[row : row + 1, :]
        inc = [incs[i, 0:S, 0 : hi - lo] for i in range(OWN)]
        counts = count[:, lo:hi].astype(F32)

        def channels(step, grads):
            base = pl.multiple_of(8 * step, 8)
            square = squares[pl.ds(base, 8), 0:1]
            grads = list(grads)
            for i in range(OWN):
                weight = mask[i, pl.ds(base, 8), lo:hi].astype(F32) * counts[i : i + 1, :] / square
                for n in range(8):
                    jac_n = jac[base + n, i, :, lo:hi].astype(F32)
                    radiance = jnp.sum(jac_n * inc[i], axis=0, keepdims=True)
                    grads[i] = grads[i] + jac_n * (weight[n : n + 1, :] * radiance)
            return tuple(grads)

        grads = lax.fori_loop(0, CH // 8, channels, tuple(jnp.zeros((S, hi - lo), F32) for _ in range(OWN)))
        gr[...] = jnp.zeros_like(gr)
        for i in range(OWN):
            for s in range(S):
                row = OWN * s + i if c else OWN * (s // 2) + i
                half = 0 if c else s % 2
                gr[half, row : row + 1, 0 : hi - lo] = grads[i][s : s + 1, :].astype(BF16).astype(F32)
        gp[c][...] = (gr[0] if c else joined(gr[0, 0 : PIECE[0]], gr[1, 0 : PIECE[0]])).astype(BF16)
        copies = [remote(gp[c], gz[c].at[t], c_send.at[c, k], c_recv.at[c, k], to_t[k]) for k in range(TN - 1)]
        for copy in copies:
            copy.start()
        gz[c][t] = gp[c][...]
        return copies

    def gather(c, third):
        for copy in third:
            copy.wait_recv()
        sent.extend(third)
        tall = dot(from_piece[c][...], gz[c][...].reshape(TN * PIECE[c], 128)).astype(BF16)
        for l in range(TILES[c]):
            ag[c][y, :, 128 * l : 128 * l + 128] = tall[ROWS * l : ROWS * l + ROWS]
        copies = [remote(ag[c].at[y], ag[c].at[y], d_send.at[c, k], d_recv.at[c, k], to_y[k]) for k in range(YN - 1)]
        for copy in copies:
            copy.start()
        return copies

    source, half = far + (cross - far) * (y // 2), y % 2

    def adjoint(c, fourth):
        for copy in fourth:
            copy.wait_recv()
        sent.extend(fourth)
        gradient = ag[c][...].reshape(LAT, 128 * TILES[c]).astype(F32)
        width = 64 * TILES[c]
        back = dot(latpt[...], (spread[MEMB, 0:LAT, lanes[c]] * gradient).astype(BF16)).astype(BF16)
        back = back.reshape(4, ROWS, 128 * TILES[c])
        for h in range(2):
            bss[c][h] = back[:, :, width * h : width * h + width]
        fixed = [
            remote(bss[c].at[half, source], brs[c].at[half, band], g_send.at[c, 0], g_recv.at[c, 0], at_band(source)),
            remote(bss[c].at[:, sib], brs[c].at[:, band], g_send.at[c, 1], g_recv.at[c, 1], at_band(sib)),
        ] + [
            remote(brs[c].at[half, source], brs[c].at[half, source], g_send.at[c, 2 + k], g_recv.at[c, 2 + k], to_y[k])
            for k in range(YN - 1)]
        for copy in fixed[:2]:
            copy.start()
        for m in range(MEMB):
            back = dot(latpt[...], (spread[m, 0:LAT, lanes[c]] * gradient).astype(BF16)).astype(BF16)
            bs[c][:, m] = back.reshape(4, ROWS, 128 * TILES[c])
        copies = [
            remote(bs[c].at[far], br[c].at[band], e_send.at[c, 0], e_recv.at[c, 0], at_band(far)),
            remote(bs[c].at[cross], bl[c], e_send.at[c, 1], e_recv.at[c, 1], at_band(sib)),
            remote(bs[c].at[sib], br[c].at[band], e_send.at[c, 2], e_recv.at[c, 2], at_band(sib)),
            remote(bl[c], br[c].at[sib], e_send.at[c, 3], e_recv.at[c, 3], at_band(far)),
        ]
        for copy in copies[:3]:
            copy.start()
        br[c][band] = bs[c][band]
        for h in range(2):
            brs[c][h, band] = bss[c][h, band]
        return copies, fixed

    first = [sum_first(0)]

    for load in loads[10:]:
        load.wait()
    rem[...] = jnp.zeros_like(rem)
    for h in range(2):
        for s in range(2):
            value = std[2 * h + s]
            ordered = None
            for _ in range(3):
                top = value.astype(BF16)
                term = dot(order[...], top, (1, 1))
                ordered = term if ordered is None else ordered + term
                value = value - top.astype(F32)
            ordered = 0.6 * ordered
            spread[MEMB, 0:LAT, 128 * (2 * h + s) : 128 * (2 * h + s) + 128] = ordered[:, 0:128]
            rem[s, :, 0:REM] = ordered[:, 128:COLS]
        spread[MEMB, 0:LAT, 512 + 128 * h : 640 + 128 * h] = joined(rem[0], rem[1])

    spread[:, LAT:] = jnp.zeros((FIELDS, 8, WIDE), F32)
    first_row = ROWS * y + OWN * t
    shift = first_row % 8
    own_std = spread[MEMB, pl.ds(pl.multiple_of(first_row - shift, 8), 16), :]
    own_std = pltpu.roll(own_std, (16 - shift) % 16, 0)[0:8]
    for copy in static_copies:
        copy.wait_recv()
    sent.extend(static_copies)
    static_term = own_std * (sr[0] + sr[1] + sr[2] + sr[3])
    for c in range(CHUNKS):
        terms[c][...] = jnp.zeros_like(terms[c])
        for l in range(TILES[c]):
            terms[c][OWN * l : OWN * l + OWN] = static_term[0:OWN, BASE[c] + 128 * l : BASE[c] + 128 * l + 128]
    for load in loads[5:9]:
        load.wait()
    error = jnp.sum(jnp.where(iota((CH, CH), 0) == iota((CH, CH), 1), error_row[...], 0.0), axis=1, keepdims=True)
    squares[...] = jnp.broadcast_to(error * error, squares.shape)

    second = [sum_second(0, first[0])]

    first.append(sum_first(1))
    latpt[...] = dot(jnp.transpose(lat[...].astype(F32)).astype(BF16), order[...], (1, 1)).astype(BF16)
    for c in range(CHUNKS):
        rows, height = TN * PIECE[c], ROWS * TILES[c]
        hot = iota((height, rows), 0) == piece_row(c, iota((height, rows), 1))
        from_piece[c][...] = jnp.where(hot, 1.0, 0.0).astype(BF16)

    third = [pixels(0, second[0])]

    second.append(sum_second(1, first[1]))

    fourth = [gather(0, third[0])]

    third.append(pixels(1, second[1]))

    ways = [adjoint(0, fourth[0])]
    ways[0][0][1].wait_recv()
    ways[0][0][3].start()

    fourth.append(gather(1, third[1]))
    ways[0][1][0].wait_recv()
    for copy in ways[0][1][2:]:
        copy.start()

    ways.append(adjoint(1, fourth[1]))
    ways[1][0][1].wait_recv()
    ways[1][0][3].start()

    copies, fixed = ways[0]
    for copy in copies[:1] + copies[2:]:
        copy.wait_recv()
    for f in range(FIELDS):
        if f == MEMB:
            for copy in fixed[1:]:
                copy.wait_recv()
        for h in range(2):
            if f < MEMB:
                tiles = [br[0][b, f, :, 128 * h : 128 * h + 128].astype(F32) for b in range(4)]
            else:
                tiles = [brs[0][h, b].astype(F32) for b in range(4)]
            for s in range(2):
                join = joined if s == 0 else joined_high
                for g in range(2):
                    pair = join(tiles[2 * g], tiles[2 * g + 1]).astype(BF16)
                    lhs[0][pl.ds((2 * h + s) * ROWS, ROWS), 128 * g : 128 * g + 128] = pair
        base = alpha[f] if f < MEMB else static[...]
        out[f] = base.astype(F32) + dot(lhs[0][...], w[:, lanes[0]], (1, 1)).reshape(S, ROWS, LON)
        if f == MEMB - 1:
            ways[1][1][0].wait_recv()
            for copy in ways[1][1][2:]:
                copy.start()

    stores = []
    copies, fixed = ways[1]
    for f in range(FIELDS):
        if f == 0:
            for copy in copies[:1] + copies[2:]:
                copy.wait_recv()
        if f == MEMB:
            for copy in fixed[1:]:
                copy.wait_recv()
        for s in range(S):
            for b in range(4):
                if f < MEMB:
                    tile = br[1][b, f, :, 128 * s : 128 * s + 128]
                else:
                    tile = brs[1][s // 2, b, :, 128 * (s % 2) : 128 * (s % 2) + 128]
                lhs[1][ROWS * s : ROWS * s + ROWS, 128 * b : 128 * b + 128] = tile
        out[f] = out[f] + dot(lhs[1][...], w[:, lanes[1]], (1, 1)).reshape(S, ROWS, LON)
        store = pltpu.make_async_copy(out.at[f], ga_hbm.at[f] if f < MEMB else gs_hbm, store_sem.at[f])
        store.start()
        stores.append(store)
    for copies, fixed in ways:
        sent.extend(copies)
        sent.extend(fixed)
    for store in stores:
        store.wait()
    for copy in sent:
        copy.wait_send()


def shards(alpha, static_ctl, perturbations, static_std, lon_root, lat_root, jacobian, obs_count, channel_mask,
           channel_error, member_weight):
    inputs = [alpha, static_ctl, jnp.transpose(perturbations, (0, 3, 1, 2)), jnp.transpose(static_std, (2, 0, 1)),
              lon_root, lat_root, jnp.transpose(jacobian, (0, 2, 1, 3)), obs_count, jnp.transpose(channel_mask, (1, 0, 2)),
              channel_error.reshape(1, CH), member_weight.reshape(1, MEM)]
    dma, vmem = pltpu.SemaphoreType.DMA, pltpu.VMEM
    scratch = [
        vmem((MEMB, S, ROWS, LON), BF16),
        vmem((S, ROWS, LON), BF16),
        vmem((MEMB, S * COLS, LAT), BF16),
        vmem((S, COLS, LAT), F32),
        vmem((LON, LON), BF16),
        vmem((LAT, LAT), BF16),
        vmem((CH, OWN, S, COLS), BF16),
        vmem((OWN, COLS), I32),
        vmem((OWN, CH, COLS), I32),
        vmem((1, CH), F32),
        vmem((1, MEM), I32),
        vmem((LON, WIDE), BF16),
        vmem((4, 8, WIDE), F32),
        vmem((4, 8, WIDE), F32),
        vmem((FIELDS, S, ROWS, LON), F32),
        vmem((FIELDS, LAT + 8, WIDE), F32),
        vmem((2, LAT, 128), F32),
        vmem((LAT, LAT), BF16),
        vmem((LAT, LAT), BF16),
        vmem((LAT, LAT), BF16),
        vmem((S * COLS, WIDE), BF16),
        vmem((CH, 128), F32),
        vmem((OWN, 8, 128), F32),
        vmem((2, 32, 128), F32),
    ]

    def both(shape, kind):
        return [vmem(shape(128 * TILES[c], PIECE[c], ROWS * TILES[c]), kind) for c in range(CHUNKS)]

    scratch += both(lambda n, r, h: (4, MEMB, ROWS, n), BF16)
    scratch += both(lambda n, r, h: (MEMB, ROWS, n), BF16)
    scratch += both(lambda n, r, h: (4, MEMB, ROWS, n), BF16)
    scratch += both(lambda n, r, h: (YN, ROWS, n), BF16)
    scratch += both(lambda n, r, h: (YN - 1, ROWS, n), BF16)
    scratch += both(lambda n, r, h: (TN, r, 128), BF16)
    scratch += both(lambda n, r, h: (TN - 1, r, 128), BF16)
    scratch += both(lambda n, r, h: (r, 128), F32)
    scratch += both(lambda n, r, h: (r, 128), BF16)
    scratch += both(lambda n, r, h: (TN, r, 128), BF16)
    scratch += both(lambda n, r, h: (YN, ROWS, n), BF16)
    scratch += both(lambda n, r, h: (4, MEMB, ROWS, n), BF16)
    scratch += both(lambda n, r, h: (MEMB, ROWS, n), BF16)
    scratch += both(lambda n, r, h: (4, MEMB, ROWS, n), BF16)
    scratch += both(lambda n, r, h: (2, 4, ROWS, n // 2), BF16)
    scratch += both(lambda n, r, h: (2, 4, ROWS, n // 2), BF16)
    scratch += both(lambda n, r, h: (TN * r, h), BF16)
    scratch += both(lambda n, r, h: (h, TN * r), BF16)
    scratch += both(lambda n, r, h: (S * ROWS, n), BF16)
    scratch += [
        dma((10,)), dma((S,)), dma((FIELDS,)),
        dma((2, 4)), dma((2, 4)), dma((3,)), dma((3,)),
        dma((2, YN - 1)), dma((2, YN - 1)), dma((2, TN - 1)), dma((2, TN - 1)),
        dma((2, TN - 1)), dma((2, TN - 1)), dma((2, YN - 1)), dma((2, YN - 1)),
        dma((2, 4)), dma((2, 4)), dma((2, YN + 1)), dma((2, YN + 1)),
    ]
    anywhere = pl.BlockSpec(memory_space=pl.ANY)
    return pl.pallas_call(
        kernel,
        out_shape=(jax.ShapeDtypeStruct((MEMB, S, ROWS, LON), F32), jax.ShapeDtypeStruct((S, ROWS, LON), F32)),
        in_specs=[pl.BlockSpec(memory_space=pltpu.HBM)] * len(inputs),
        out_specs=(anywhere, anywhere),
        scratch_shapes=scratch,
        compiler_params=pltpu.CompilerParams(collective_id=0, has_side_effects=True, vmem_limit_bytes=40 << 20),
        name="hessian",
    )(*[pltpu.with_memory_space_constraint(v, pltpu.HBM) for v in inputs])


def solution(mesh):
    in_specs = (
        P("mem", None, "band", None),
        P(None, "band", None),
        P("mem", None, None, "band"),
        P(None, None, "band"),
        P(),
        P(),
        P(None, None, "mem", "band"),
        P("mem", "band"),
        P(None, "mem", "band"),
        P(),
        P(),
    )
    out_specs = (P("mem", None, "band", None), P(None, "band", None))
    return jax.shard_map(shards, mesh=mesh, in_specs=in_specs, out_specs=out_specs, check_vma=False)
```

```python
import functools

import jax
import jax.numpy as jnp
from jax import lax
from jax.experimental import pallas as pl
from jax.experimental.pallas import tpu as pltpu
from jax.sharding import PartitionSpec as P

MESH = pl.DeviceIdType.MESH
F32, BF16, I32 = jnp.float32, jnp.bfloat16, jnp.int32

S, CH, MEM, MEMB, FIELDS = 4, 32, 128, 2, 3
ROWS, LAT, LON, COLS = 80, 320, 720, 180
REM = COLS - 128
YN, TN, OWN = 4, 16, 5
WIDE = 768
NEXT_Y, NEXT_T = (2, 1, 3), (8, 7, 9, 6, 10, 5, 11, 4, 12, 3, 13, 2, 14, 1, 15)
CHUNKS = 2
TILES = (2, 4)
BASE = (512, 0)
PIECE = (16, 32)
SPAN = ((128, COLS), (0, 128))


def iota(shape, dim):
    return lax.broadcasted_iota(I32, shape, dim)


def one_hot(rows, columns, column_of_row):
    return jnp.where(iota((rows, columns), 1) == column_of_row(iota((rows, columns), 0)), 1.0, 0.0).astype(BF16)


def fifth(x):
    return (x * 205) // 1024


def grid_row(p):
    y = p // ROWS
    t = fifth(p - ROWS * y)
    return OWN * (8 * (t // 2) + 4 * (t % 2) + y) + p - ROWS * y - OWN * t


def packed_lane(row):
    j, s = row // 4, row % 4
    return jnp.where(j < 128, 128 * s + j, 512 + 128 * (s // 2) + 64 * (s % 2) + j - 128)


def piece_row(c, a):
    t, r = a // PIECE[c], a % PIECE[c]
    tile = fifth(r)
    return jnp.where(r < TILES[c] * OWN, ROWS * tile + OWN * t + r - OWN * tile, -1)


def low_half(shape):
    return iota(shape, len(shape) - 1) < 64


def joined(even, odd):
    return jnp.where(low_half(even.shape), even, pltpu.roll(odd, 64, 1))


def joined_high(even, odd):
    return jnp.where(low_half(even.shape), pltpu.roll(even, 64, 1), odd)


def dot(a, b, contract=(1, 0)):
    return lax.dot_general(a, b, (((contract[0],), (contract[1],)), ((), ())), preferred_element_type=F32)


def kernel(
    alpha_hbm, static_hbm, pert_hbm, std_hbm, lon_hbm, lat_hbm, jac_hbm, count_hbm, mask_hbm, error_hbm, weight_hbm,
    ga, gs,
    alpha, static, pert, std, lon, lat, jac, count, mask, error_row, weight_row,
    w, ss, sr, spread, rem, order, latp, latpt, spreader, squares, incs, gr,
    fs0, fs1, rl0, rl1, xr0, xr1, rs0, rs1, r10, r11, s20, s21, r20, r21, terms0, terms1, gp0, gp1, gz0, gz1, ag0, ag1,
    bs0, bs1, bl0, bl1, br0, br1, bss0, bss1, brs0, brs1, to0, to1, from0, from1, lhs0, lhs1,
    load_sem, std_sem, f_send, f_recv, t_send, t_recv, a_send, a_recv, b_send, b_recv, c_send, c_recv,
    d_send, d_recv, e_send, e_recv, g_send, g_recv,
):
    fs, rl, xr, rs, r1, s2, r2 = (fs0, fs1), (rl0, rl1), (xr0, xr1), (rs0, rs1), (r10, r11), (s20, s21), (r20, r21)
    terms, gp, gz, ag, bs, bl, br = (terms0, terms1), (gp0, gp1), (gz0, gz1), (ag0, ag1), (bs0, bs1), (bl0, bl1), (br0, br1)
    bss, brs, to_piece, from_piece, lhs = (bss0, bss1), (brs0, brs1), (to0, to1), (from0, from1), (lhs0, lhs1)
    lanes = [slice(BASE[c], BASE[c] + 128 * TILES[c]) for c in range(CHUNKS)]

    mem, band = lax.axis_index("mem"), lax.axis_index("band")
    z, x, y = mem // 8, (mem // 4) % 2, mem % 4
    t = 2 * z + x
    chip, core = band // 2, band % 2
    sib, far, cross = 2 * chip + 1 - core, 2 * (1 - chip) + core, 3 - band

    def at_band(b):
        return {"mem": mem, "band": b}

    ys = [lax.rem(y + k, YN) for k in NEXT_Y]
    to_y = [{"mem": 8 * z + 4 * x + v, "band": band} for v in ys]
    ts = [lax.rem(t + k, TN) for k in NEXT_T]
    to_t = [{"mem": 8 * (v // 2) + 4 * (v % 2) + y, "band": band} for v in ts]

    staged = [(lon_hbm, lon), (alpha_hbm, alpha), (static_hbm, static), (lat_hbm, lat),
              (pert_hbm.reshape(MEMB, S * COLS, LAT), pert), (jac_hbm, jac), (count_hbm, count), (mask_hbm, mask),
              (error_hbm, error_row), (weight_hbm, weight_row)]
    loads = [pltpu.make_async_copy(src, dst, load_sem.at[i]) for i, (src, dst) in enumerate(staged)]
    loads += [pltpu.make_async_copy(std_hbm.at[:, s, :], std.at[s], std_sem.at[s]) for s in range(S)]
    for load in loads:
        load.start()

    barrier = pltpu.get_barrier_semaphore()
    partners = to_t + to_y + [at_band(far), at_band(cross), at_band(sib)]
    for device in partners:
        pl.semaphore_signal(barrier, inc=1, device_id=device, device_id_type=MESH)

    def remote(src, dst, send, recv, device):
        return pltpu.make_async_remote_copy(
            src_ref=src, dst_ref=dst, send_sem=send, recv_sem=recv, device_id=device, device_id_type=MESH)

    sent = []

    loads[0].wait()
    for b in range(4):
        w[:, 512 + 64 * b : 512 + 64 * b + REM] = lon[:, COLS * b + 128 : COLS * b + COLS]
        w[:, 512 + 64 * b + REM : 576 + 64 * b] = jnp.zeros((LON, 64 - REM), BF16)
        w[:, 128 * b : 128 * b + 128] = lon[:, COLS * b : COLS * b + 128]

    forward = []
    loads[1].wait()
    for c in range(CHUNKS):
        v = dot(alpha[...].reshape(MEMB * S * ROWS, LON), w[:, lanes[c]])
        v = v.reshape(MEMB, S, ROWS, 128 * TILES[c])
        for m in range(MEMB):
            for b in range(4):
                if c == 0:
                    tile = 128 * (b // 2)
                    join = joined if b % 2 == 0 else joined_high
                    for h in range(2):
                        pair = join(v[m, 2 * h][:, tile : tile + 128], v[m, 2 * h + 1][:, tile : tile + 128])
                        fs[c][b, m, :, 128 * h : 128 * h + 128] = pair.astype(BF16)
                else:
                    for s in range(S):
                        fs[c][b, m, :, 128 * s : 128 * s + 128] = v[m, s][:, 128 * b : 128 * b + 128].astype(BF16)
        copies = [
            remote(fs[c].at[far], xr[c].at[band], f_send.at[c, 0], f_recv.at[c, 0], at_band(far)),
            remote(fs[c].at[cross], rl[c], f_send.at[c, 1], f_recv.at[c, 1], at_band(sib)),
            remote(fs[c].at[sib], xr[c].at[band], f_send.at[c, 2], f_recv.at[c, 2], at_band(sib)),
            remote(rl[c], xr[c].at[sib], f_send.at[c, 3], f_recv.at[c, 3], at_band(far)),
        ]
        forward.append(copies)
        xr[c][band] = fs[c][band]

    loads[2].wait()
    loads[3].wait()
    v = dot(static[...].reshape(S * ROWS, LON), w[...]).astype(BF16)
    own_rows = dot(one_hot(16, LAT, lambda k: jnp.where(k < OWN, OWN * mem + k, -1)), lat[...]).astype(BF16)
    here = jnp.where(iota((LAT, ROWS), 0) == ROWS * band + iota((LAT, ROWS), 1), 1.0, 0.0).astype(BF16)
    own_part = dot(own_rows, here).astype(BF16)
    parts = [dot(own_part, v[ROWS * s : ROWS * s + ROWS])[0:8] for s in range(S)]
    for b in range(4):
        tile = 512 + 128 * (b // 2)
        join = joined if b % 2 == 0 else joined_high
        for s in range(S):
            ss[b, :, 128 * s : 128 * s + 128] = parts[s][:, 128 * b : 128 * b + 128]
        for h in range(2):
            ss[b, :, 512 + 128 * h : 640 + 128 * h] = join(
                parts[2 * h][:, tile : tile + 128], parts[2 * h + 1][:, tile : tile + 128])
    others = (far, cross, sib)
    static_copies = [remote(ss.at[b], sr.at[band], t_send.at[k], t_recv.at[k], at_band(b)) for k, b in enumerate(others)]
    sr[band] = ss[band]
    order[...] = one_hot(LAT, LAT, grid_row)
    latp[...] = dot(order[...], lat[...]).astype(BF16)
    pl.semaphore_wait(barrier, len(partners))
    for copy in forward[1][:3] + [forward[0][1]] + static_copies:
        copy.start()
    forward[1][1].wait_recv()
    forward[1][3].start()
    forward[0][0].start()
    forward[0][1].wait_recv()
    forward[0][3].start()
    forward[0][2].start()

    spreader[...] = one_hot(S * COLS, WIDE, packed_lane)
    loads[9].wait()
    weights = weight_row[...].astype(F32)
    coef = weights / jnp.sqrt(jnp.sum(weights * weights, axis=1, keepdims=True))
    loads[4].wait()
    for m in range(MEMB):
        factor = 0.8 * jnp.sum(jnp.where(iota(coef.shape, 1) == MEMB * mem + m, coef, 0.0), axis=1, keepdims=True)
        ordered = dot(order[...], pert[m], (1, 1)).astype(BF16)
        spread[m, 0:LAT] = factor * dot(ordered, spreader[...])
    for c in range(CHUNKS):
        rows, height = TN * PIECE[c], ROWS * TILES[c]
        to_piece[c][...] = one_hot(rows, height, lambda a: piece_row(c, a))

    def sum_first(c):
        for k in (0, 2, 3):
            forward[c][k].wait_recv()
        total = None
        for m in range(MEMB):
            field = dot(latp[...], xr[c][:, m].reshape(LAT, 128 * TILES[c]))
            term = spread[m, 0:LAT, lanes[c]] * field
            total = term if total is None else total + term
        rs[c][...] = total.astype(BF16).reshape(YN, ROWS, 128 * TILES[c])
        copies = [
            remote(rs[c].at[ys[k]], r1[c].at[k], a_send.at[c, k], a_recv.at[c, k], to_y[k]) for k in range(YN - 1)]
        for copy in copies:
            copy.start()
        sent.extend(forward[c])
        return copies

    def sum_second(c, first):
        for copy in first:
            copy.wait_recv()
        total = rs[c][y].astype(F32)
        for k in range(YN - 1):
            total = total + r1[c][k].astype(F32)
        total = total.astype(BF16)
        tall = jnp.concatenate([total[:, 128 * l : 128 * l + 128] for l in range(TILES[c])], axis=0)
        s2[c][...] = dot(to_piece[c][...], tall).astype(BF16).reshape(TN, PIECE[c], 128)
        copies = [
            remote(s2[c].at[ts[k]], r2[c].at[k], b_send.at[c, k], b_recv.at[c, k], to_t[k]) for k in range(TN - 1)]
        for copy in copies:
            copy.start()
        sent.extend(first)
        return copies

    def pixels(c, second):
        for copy in second:
            copy.wait_recv()
        sent.extend(second)
        total = terms[c][...] + s2[c][t].astype(F32)
        for k in range(TN - 1):
            total = total + r2[c][k].astype(F32)
        lo, hi = SPAN[c]
        turned = pltpu.roll(total, 64, 1) if c == 0 else None
        for i in range(OWN):
            for s in range(S):
                row = OWN * s + i if c else OWN * (s // 2) + i
                source = total if c or s % 2 == 0 else turned
                incs[i, s : s + 1, :] = source[row : row + 1, :]
        inc = [incs[i, 0:S, 0 : hi - lo] for i in range(OWN)]
        counts = count[:, lo:hi].astype(F32)

        def channels(step, grads):
            base = pl.multiple_of(8 * step, 8)
            square = squares[pl.ds(base, 8), 0:1]
            grads = list(grads)
            for i in range(OWN):
                weight = mask[i, pl.ds(base, 8), lo:hi].astype(F32) * counts[i : i + 1, :] / square
                for n in range(8):
                    jac_n = jac[base + n, i, :, lo:hi].astype(F32)
                    radiance = jnp.sum(jac_n * inc[i], axis=0, keepdims=True)
                    grads[i] = grads[i] + jac_n * (weight[n : n + 1, :] * radiance)
            return tuple(grads)

        grads = lax.fori_loop(0, CH // 8, channels, tuple(jnp.zeros((S, hi - lo), F32) for _ in range(OWN)))
        gr[...] = jnp.zeros_like(gr)
        for i in range(OWN):
            for s in range(S):
                row = OWN * s + i if c else OWN * (s // 2) + i
                half = 0 if c else s % 2
                gr[half, row : row + 1, 0 : hi - lo] = grads[i][s : s + 1, :].astype(BF16).astype(F32)
        gp[c][...] = (gr[0] if c else joined(gr[0, 0 : PIECE[0]], gr[1, 0 : PIECE[0]])).astype(BF16)
        copies = [remote(gp[c], gz[c].at[t], c_send.at[c, k], c_recv.at[c, k], to_t[k]) for k in range(TN - 1)]
        for copy in copies:
            copy.start()
        gz[c][t] = gp[c][...]
        return copies

    def gather(c, third):
        for copy in third:
            copy.wait_recv()
        sent.extend(third)
        tall = dot(from_piece[c][...], gz[c][...].reshape(TN * PIECE[c], 128)).astype(BF16)
        for l in range(TILES[c]):
            ag[c][y, :, 128 * l : 128 * l + 128] = tall[ROWS * l : ROWS * l + ROWS]
        copies = [remote(ag[c].at[y], ag[c].at[y], d_send.at[c, k], d_recv.at[c, k], to_y[k]) for k in range(YN - 1)]
        for copy in copies:
            copy.start()
        return copies

    source, half = far + (cross - far) * (y // 2), y % 2

    def adjoint(c, fourth):
        for copy in fourth:
            copy.wait_recv()
        sent.extend(fourth)
        gradient = ag[c][...].reshape(LAT, 128 * TILES[c]).astype(F32)
        width = 64 * TILES[c]
        back = dot(latpt[...], (spread[MEMB, 0:LAT, lanes[c]] * gradient).astype(BF16)).astype(BF16)
        back = back.reshape(4, ROWS, 128 * TILES[c])
        for h in range(2):
            bss[c][h] = back[:, :, width * h : width * h + width]
        fixed = [
            remote(bss[c].at[half, source], brs[c].at[half, band], g_send.at[c, 0], g_recv.at[c, 0], at_band(source)),
            remote(bss[c].at[:, sib], brs[c].at[:, band], g_send.at[c, 1], g_recv.at[c, 1], at_band(sib)),
        ] + [
            remote(brs[c].at[half, source], brs[c].at[half, source], g_send.at[c, 2 + k], g_recv.at[c, 2 + k], to_y[k])
            for k in range(YN - 1)]
        for copy in fixed[:2]:
            copy.start()
        for m in range(MEMB):
            back = dot(latpt[...], (spread[m, 0:LAT, lanes[c]] * gradient).astype(BF16)).astype(BF16)
            bs[c][:, m] = back.reshape(4, ROWS, 128 * TILES[c])
        copies = [
            remote(bs[c].at[far], br[c].at[band], e_send.at[c, 0], e_recv.at[c, 0], at_band(far)),
            remote(bs[c].at[cross], bl[c], e_send.at[c, 1], e_recv.at[c, 1], at_band(sib)),
            remote(bs[c].at[sib], br[c].at[band], e_send.at[c, 2], e_recv.at[c, 2], at_band(sib)),
            remote(bl[c], br[c].at[sib], e_send.at[c, 3], e_recv.at[c, 3], at_band(far)),
        ]
        for copy in copies[:3]:
            copy.start()
        br[c][band] = bs[c][band]
        for h in range(2):
            brs[c][h, band] = bss[c][h, band]
        return copies, fixed

    first = {1: sum_first(1)}

    for load in loads[10:]:
        load.wait()
    rem[...] = jnp.zeros_like(rem)
    for h in range(2):
        for s in range(2):
            value = std[2 * h + s]
            ordered = None
            for _ in range(3):
                top = value.astype(BF16)
                term = dot(order[...], top, (1, 1))
                ordered = term if ordered is None else ordered + term
                value = value - top.astype(F32)
            ordered = 0.6 * ordered
            spread[MEMB, 0:LAT, 128 * (2 * h + s) : 128 * (2 * h + s) + 128] = ordered[:, 0:128]
            rem[s, :, 0:REM] = ordered[:, 128:COLS]
        spread[MEMB, 0:LAT, 512 + 128 * h : 640 + 128 * h] = joined(rem[0], rem[1])

    spread[:, LAT:] = jnp.zeros((FIELDS, 8, WIDE), F32)
    first_row = ROWS * y + OWN * t
    shift = first_row % 8
    own_std = spread[MEMB, pl.ds(pl.multiple_of(first_row - shift, 8), 16), :]
    own_std = pltpu.roll(own_std, (16 - shift) % 16, 0)[0:8]
    for copy in static_copies:
        copy.wait_recv()
    sent.extend(static_copies)
    static_term = own_std * (sr[0] + sr[1] + sr[2] + sr[3])
    for c in range(CHUNKS):
        terms[c][...] = jnp.zeros_like(terms[c])
        for l in range(TILES[c]):
            terms[c][OWN * l : OWN * l + OWN] = static_term[0:OWN, BASE[c] + 128 * l : BASE[c] + 128 * l + 128]
    for load in loads[5:9]:
        load.wait()
    error = jnp.sum(jnp.where(iota((CH, CH), 0) == iota((CH, CH), 1), error_row[...], 0.0), axis=1, keepdims=True)
    squares[...] = jnp.broadcast_to(error * error, squares.shape)

    second = {1: sum_second(1, first[1])}

    first[0] = sum_first(0)
    latpt[...] = dot(jnp.transpose(lat[...].astype(F32)).astype(BF16), order[...], (1, 1)).astype(BF16)
    for c in range(CHUNKS):
        rows, height = TN * PIECE[c], ROWS * TILES[c]
        hot = iota((height, rows), 0) == piece_row(c, iota((height, rows), 1))
        from_piece[c][...] = jnp.where(hot, 1.0, 0.0).astype(BF16)

    second[0] = sum_second(0, first[0])

    third = {1: pixels(1, second[1])}

    third[0] = pixels(0, second[0])

    fourth = {1: gather(1, third[1])}

    fourth[0] = gather(0, third[0])

    copies, fixed = adjoint(1, fourth[1])
    copies[1].wait_recv()
    copies[3].start()

    last, last_fixed = adjoint(0, fourth[0])
    fixed[0].wait_recv()
    for copy in fixed[2:]:
        copy.start()
    last[1].wait_recv()
    last[3].start()

    def result(f):
        return ga.at[f] if f < MEMB else gs

    for copy in copies[:1] + copies[2:]:
        copy.wait_recv()
    for f in range(FIELDS):
        if f == MEMB:
            last_fixed[0].wait_recv()
            for copy in last_fixed[2:]:
                copy.start()
            for copy in fixed[1:]:
                copy.wait_recv()
        for s in range(S):
            for b in range(4):
                if f < MEMB:
                    tile = br[1][b, f, :, 128 * s : 128 * s + 128]
                else:
                    tile = brs[1][s // 2, b, :, 128 * (s % 2) : 128 * (s % 2) + 128]
                lhs[1][ROWS * s : ROWS * s + ROWS, 128 * b : 128 * b + 128] = tile
        base = alpha[f] if f < MEMB else static[...]
        result(f)[...] = base.astype(F32) + dot(lhs[1][...], w[:, lanes[1]], (1, 1)).reshape(S, ROWS, LON)

    for copy in last[:1] + last[2:]:
        copy.wait_recv()
    for f in range(FIELDS):
        if f == MEMB:
            for copy in last_fixed[1:]:
                copy.wait_recv()
        for h in range(2):
            if f < MEMB:
                tiles = [br[0][b, f, :, 128 * h : 128 * h + 128].astype(F32) for b in range(4)]
            else:
                tiles = [brs[0][h, b].astype(F32) for b in range(4)]
            for s in range(2):
                join = joined if s == 0 else joined_high
                for g in range(2):
                    pair = join(tiles[2 * g], tiles[2 * g + 1]).astype(BF16)
                    lhs[0][pl.ds((2 * h + s) * ROWS, ROWS), 128 * g : 128 * g + 128] = pair
        result(f)[...] = result(f)[...] + dot(lhs[0][...], w[:, lanes[0]], (1, 1)).reshape(S, ROWS, LON)
    for copy in sent + copies + fixed + last + last_fixed:
        copy.wait_send()


def shards(alpha, static_ctl, perturbations, static_std, lon_root, lat_root, jacobian, obs_count, channel_mask,
           channel_error, member_weight):
    inputs = [alpha, static_ctl, jnp.transpose(perturbations, (0, 3, 1, 2)), jnp.transpose(static_std, (2, 0, 1)),
              lon_root, lat_root, jnp.transpose(jacobian, (0, 2, 1, 3)), obs_count, jnp.transpose(channel_mask, (1, 0, 2)),
              channel_error.reshape(1, CH), member_weight.reshape(1, MEM)]
    dma, vmem = pltpu.SemaphoreType.DMA, pltpu.VMEM
    scratch = [
        vmem((MEMB, S, ROWS, LON), BF16),
        vmem((S, ROWS, LON), BF16),
        vmem((MEMB, S * COLS, LAT), BF16),
        vmem((S, COLS, LAT), F32),
        vmem((LON, LON), BF16),
        vmem((LAT, LAT), BF16),
        vmem((CH, OWN, S, COLS), BF16),
        vmem((OWN, COLS), I32),
        vmem((OWN, CH, COLS), I32),
        vmem((1, CH), F32),
        vmem((1, MEM), I32),
        vmem((LON, WIDE), BF16),
        vmem((4, 8, WIDE), F32),
        vmem((4, 8, WIDE), F32),
        vmem((FIELDS, LAT + 8, WIDE), F32),
        vmem((2, LAT, 128), F32),
        vmem((LAT, LAT), BF16),
        vmem((LAT, LAT), BF16),
        vmem((LAT, LAT), BF16),
        vmem((S * COLS, WIDE), BF16),
        vmem((CH, 128), F32),
        vmem((OWN, 8, 128), F32),
        vmem((2, 32, 128), F32),
    ]

    def both(shape, kind):
        return [vmem(shape(128 * TILES[c], PIECE[c], ROWS * TILES[c]), kind) for c in range(CHUNKS)]

    scratch += both(lambda n, r, h: (4, MEMB, ROWS, n), BF16)
    scratch += both(lambda n, r, h: (MEMB, ROWS, n), BF16)
    scratch += both(lambda n, r, h: (4, MEMB, ROWS, n), BF16)
    scratch += both(lambda n, r, h: (YN, ROWS, n), BF16)
    scratch += both(lambda n, r, h: (YN - 1, ROWS, n), BF16)
    scratch += both(lambda n, r, h: (TN, r, 128), BF16)
    scratch += both(lambda n, r, h: (TN - 1, r, 128), BF16)
    scratch += both(lambda n, r, h: (r, 128), F32)
    scratch += both(lambda n, r, h: (r, 128), BF16)
    scratch += both(lambda n, r, h: (TN, r, 128), BF16)
    scratch += both(lambda n, r, h: (YN, ROWS, n), BF16)
    scratch += both(lambda n, r, h: (4, MEMB, ROWS, n), BF16)
    scratch += both(lambda n, r, h: (MEMB, ROWS, n), BF16)
    scratch += both(lambda n, r, h: (4, MEMB, ROWS, n), BF16)
    scratch += both(lambda n, r, h: (2, 4, ROWS, n // 2), BF16)
    scratch += both(lambda n, r, h: (2, 4, ROWS, n // 2), BF16)
    scratch += both(lambda n, r, h: (TN * r, h), BF16)
    scratch += both(lambda n, r, h: (h, TN * r), BF16)
    scratch += both(lambda n, r, h: (S * ROWS, n), BF16)
    scratch += [
        dma((10,)), dma((S,)),
        dma((2, 4)), dma((2, 4)), dma((3,)), dma((3,)),
        dma((2, YN - 1)), dma((2, YN - 1)), dma((2, TN - 1)), dma((2, TN - 1)),
        dma((2, TN - 1)), dma((2, TN - 1)), dma((2, YN - 1)), dma((2, YN - 1)),
        dma((2, 4)), dma((2, 4)), dma((2, YN + 1)), dma((2, YN + 1)),
    ]
    return pl.pallas_call(
        kernel,
        out_shape=(jax.ShapeDtypeStruct((MEMB, S, ROWS, LON), F32), jax.ShapeDtypeStruct((S, ROWS, LON), F32)),
        in_specs=[pl.BlockSpec(memory_space=pltpu.HBM)] * len(inputs),
        out_specs=(pl.BlockSpec(memory_space=pltpu.VMEM),) * 2,
        scratch_shapes=scratch,
        compiler_params=pltpu.CompilerParams(collective_id=0, has_side_effects=True, vmem_limit_bytes=40 << 20),
        name="hessian",
    )(*[pltpu.with_memory_space_constraint(v, pltpu.HBM) for v in inputs])


def solution(mesh):
    in_specs = (
        P("mem", None, "band", None),
        P(None, "band", None),
        P("mem", None, None, "band"),
        P(None, None, "band"),
        P(),
        P(),
        P(None, None, "mem", "band"),
        P("mem", "band"),
        P(None, "mem", "band"),
        P(),
        P(),
    )
    out_specs = (P("mem", None, "band", None), P(None, "band", None))
    return jax.shard_map(shards, mesh=mesh, in_specs=in_specs, out_specs=out_specs, check_vma=False)
```

```python
import functools

import jax
import jax.numpy as jnp
from jax import lax
from jax.experimental import pallas as pl
from jax.experimental.pallas import tpu as pltpu
from jax.sharding import PartitionSpec as P

MESH = pl.DeviceIdType.MESH
F32, BF16, I32 = jnp.float32, jnp.bfloat16, jnp.int32

S, CH, MEM, MEMB, FIELDS = 4, 32, 128, 2, 3
ROWS, LAT, LON, COLS = 80, 320, 720, 180
REM = COLS - 128
YN, TN, OWN = 4, 16, 5
WIDE = 768
NEXT_Y, NEXT_T = (2, 1, 3), (8, 7, 9, 6, 10, 5, 11, 4, 12, 3, 13, 2, 14, 1, 15)
CHUNKS = 2
TILES = (2, 4)
BASE = (512, 0)
PIECE = (16, 32)
SPAN = ((128, COLS), (0, 128))


def iota(shape, dim):
    return lax.broadcasted_iota(I32, shape, dim)


def one_hot(rows, columns, column_of_row):
    return jnp.where(iota((rows, columns), 1) == column_of_row(iota((rows, columns), 0)), 1.0, 0.0).astype(BF16)


def fifth(x):
    return (x * 205) // 1024


def grid_row(p):
    y = p // ROWS
    t = fifth(p - ROWS * y)
    return OWN * (8 * (t // 2) + 4 * (t % 2) + y) + p - ROWS * y - OWN * t


def packed_lane(row):
    j, s = row // 4, row % 4
    return jnp.where(j < 128, 128 * s + j, 512 + 128 * (s // 2) + 64 * (s % 2) + j - 128)


def piece_row(c, a):
    t, r = a // PIECE[c], a % PIECE[c]
    tile = fifth(r)
    return jnp.where(r < TILES[c] * OWN, ROWS * tile + OWN * t + r - OWN * tile, -1)


def low_half(shape):
    return iota(shape, len(shape) - 1) < 64


def joined(even, odd):
    return jnp.where(low_half(even.shape), even, pltpu.roll(odd, 64, 1))


def joined_high(even, odd):
    return jnp.where(low_half(even.shape), pltpu.roll(even, 64, 1), odd)


def dot(a, b, contract=(1, 0)):
    return lax.dot_general(a, b, (((contract[0],), (contract[1],)), ((), ())), preferred_element_type=F32)


def kernel(
    alpha_hbm, static_hbm, pert_hbm, std_hbm, lon_hbm, lat_hbm, jac_hbm, count_hbm, mask_hbm, error_hbm, weight_hbm,
    ga, gs,
    alpha, static, pert, std, lon, lat, jac, count, mask, error_row, weight_row,
    w, ss, sr, spread, rem, order, latp, latpt, spreader, squares, incs, gr,
    fs0, fs1, rl0, rl1, xr0, xr1, rs0, rs1, r10, r11, s20, s21, r20, r21, terms0, terms1, gp0, gp1, gz0, gz1, ag0, ag1,
    bs0, bs1, bl0, bl1, br0, br1, bss0, bss1, brs0, brs1, to0, to1, from0, from1, lhs0, lhs1,
    load_sem, std_sem, f_send, f_recv, t_send, t_recv, a_send, a_recv, b_send, b_recv, c_send, c_recv,
    d_send, d_recv, e_send, e_recv, g_send, g_recv,
):
    fs, rl, xr, rs, r1, s2, r2 = (fs0, fs1), (rl0, rl1), (xr0, xr1), (rs0, rs1), (r10, r11), (s20, s21), (r20, r21)
    terms, gp, gz, ag, bs, bl, br = (terms0, terms1), (gp0, gp1), (gz0, gz1), (ag0, ag1), (bs0, bs1), (bl0, bl1), (br0, br1)
    bss, brs, to_piece, from_piece, lhs = (bss0, bss1), (brs0, brs1), (to0, to1), (from0, from1), (lhs0, lhs1)
    lanes = [slice(BASE[c], BASE[c] + 128 * TILES[c]) for c in range(CHUNKS)]

    mem, band = lax.axis_index("mem"), lax.axis_index("band")
    z, x, y = mem // 8, (mem // 4) % 2, mem % 4
    t = 2 * z + x
    chip, core = band // 2, band % 2
    sib, far, cross = 2 * chip + 1 - core, 2 * (1 - chip) + core, 3 - band

    def at_band(b):
        return {"mem": mem, "band": b}

    ys = [lax.rem(y + k, YN) for k in NEXT_Y]
    to_y = [{"mem": 8 * z + 4 * x + v, "band": band} for v in ys]
    ts = [lax.rem(t + k, TN) for k in NEXT_T]
    to_t = [{"mem": 8 * (v // 2) + 4 * (v % 2) + y, "band": band} for v in ts]

    staged = [(lon_hbm, lon), (alpha_hbm, alpha), (static_hbm, static), (lat_hbm, lat),
              (pert_hbm.reshape(MEMB, S * COLS, LAT), pert), (jac_hbm, jac), (count_hbm, count), (mask_hbm, mask),
              (error_hbm, error_row), (weight_hbm, weight_row)]
    loads = [pltpu.make_async_copy(src, dst, load_sem.at[i]) for i, (src, dst) in enumerate(staged)]
    loads += [pltpu.make_async_copy(std_hbm.at[:, s, :], std.at[s], std_sem.at[s]) for s in range(S)]
    for load in loads:
        load.start()

    barrier = pltpu.get_barrier_semaphore()
    partners = to_t + to_y + [at_band(far), at_band(cross), at_band(sib)]
    for device in partners:
        pl.semaphore_signal(barrier, inc=1, device_id=device, device_id_type=MESH)

    def remote(src, dst, send, recv, device):
        return pltpu.make_async_remote_copy(
            src_ref=src, dst_ref=dst, send_sem=send, recv_sem=recv, device_id=device, device_id_type=MESH)

    sent = []

    loads[0].wait()
    for b in range(4):
        w[:, 512 + 64 * b : 512 + 64 * b + REM] = lon[:, COLS * b + 128 : COLS * b + COLS]
        w[:, 512 + 64 * b + REM : 576 + 64 * b] = jnp.zeros((LON, 64 - REM), BF16)
        w[:, 128 * b : 128 * b + 128] = lon[:, COLS * b : COLS * b + 128]

    forward = []
    loads[1].wait()
    for c in range(CHUNKS):
        v = dot(alpha[...].reshape(MEMB * S * ROWS, LON), w[:, lanes[c]])
        v = v.reshape(MEMB, S, ROWS, 128 * TILES[c])
        for m in range(MEMB):
            for b in range(4):
                if c == 0:
                    tile = 128 * (b // 2)
                    join = joined if b % 2 == 0 else joined_high
                    for h in range(2):
                        pair = join(v[m, 2 * h][:, tile : tile + 128], v[m, 2 * h + 1][:, tile : tile + 128])
                        fs[c][b, m, :, 128 * h : 128 * h + 128] = pair.astype(BF16)
                else:
                    for s in range(S):
                        fs[c][b, m, :, 128 * s : 128 * s + 128] = v[m, s][:, 128 * b : 128 * b + 128].astype(BF16)
        copies = [
            remote(fs[c].at[far], xr[c].at[band], f_send.at[c, 0], f_recv.at[c, 0], at_band(far)),
            remote(fs[c].at[cross], rl[c], f_send.at[c, 1], f_recv.at[c, 1], at_band(sib)),
            remote(fs[c].at[sib], xr[c].at[band], f_send.at[c, 2], f_recv.at[c, 2], at_band(sib)),
            remote(rl[c], xr[c].at[sib], f_send.at[c, 3], f_recv.at[c, 3], at_band(far)),
        ]
        forward.append(copies)
        xr[c][band] = fs[c][band]

    loads[2].wait()
    loads[3].wait()
    v = dot(static[...].reshape(S * ROWS, LON), w[...]).astype(BF16)
    own_rows = dot(one_hot(16, LAT, lambda k: jnp.where(k < OWN, OWN * mem + k, -1)), lat[...]).astype(BF16)
    here = jnp.where(iota((LAT, ROWS), 0) == ROWS * band + iota((LAT, ROWS), 1), 1.0, 0.0).astype(BF16)
    own_part = dot(own_rows, here).astype(BF16)
    parts = [dot(own_part, v[ROWS * s : ROWS * s + ROWS])[0:8] for s in range(S)]
    for b in range(4):
        tile = 512 + 128 * (b // 2)
        join = joined if b % 2 == 0 else joined_high
        for s in range(S):
            ss[b, :, 128 * s : 128 * s + 128] = parts[s][:, 128 * b : 128 * b + 128]
        for h in range(2):
            ss[b, :, 512 + 128 * h : 640 + 128 * h] = join(
                parts[2 * h][:, tile : tile + 128], parts[2 * h + 1][:, tile : tile + 128])
    others = (far, cross, sib)
    static_copies = [remote(ss.at[b], sr.at[band], t_send.at[k], t_recv.at[k], at_band(b)) for k, b in enumerate(others)]
    sr[band] = ss[band]
    order[...] = one_hot(LAT, LAT, grid_row)
    latp[...] = dot(order[...], lat[...]).astype(BF16)
    pl.semaphore_wait(barrier, len(partners))
    for copy in forward[0][:3] + [forward[1][1]] + static_copies:
        copy.start()
    forward[0][1].wait_recv()
    forward[0][3].start()
    forward[1][0].start()
    forward[1][1].wait_recv()
    forward[1][3].start()
    forward[1][2].start()

    spreader[...] = one_hot(S * COLS, WIDE, packed_lane)
    loads[9].wait()
    weights = weight_row[...].astype(F32)
    coef = weights / jnp.sqrt(jnp.sum(weights * weights, axis=1, keepdims=True))
    loads[4].wait()
    for m in range(MEMB):
        factor = 0.8 * jnp.sum(jnp.where(iota(coef.shape, 1) == MEMB * mem + m, coef, 0.0), axis=1, keepdims=True)
        ordered = dot(order[...], pert[m], (1, 1)).astype(BF16)
        spread[m, 0:LAT] = factor * dot(ordered, spreader[...])
    for c in range(CHUNKS):
        rows, height = TN * PIECE[c], ROWS * TILES[c]
        to_piece[c][...] = one_hot(rows, height, lambda a: piece_row(c, a))

    def sum_first(c):
        for k in (0, 2, 3):
            forward[c][k].wait_recv()
        total = None
        for m in range(MEMB):
            field = dot(latp[...], xr[c][:, m].reshape(LAT, 128 * TILES[c]))
            term = spread[m, 0:LAT, lanes[c]] * field
            total = term if total is None else total + term
        rs[c][...] = total.astype(BF16).reshape(YN, ROWS, 128 * TILES[c])
        copies = [
            remote(rs[c].at[ys[k]], r1[c].at[k], a_send.at[c, k], a_recv.at[c, k], to_y[k]) for k in range(YN - 1)]
        for copy in copies:
            copy.start()
        sent.extend(forward[c])
        return copies

    def sum_second(c, first):
        for copy in first:
            copy.wait_recv()
        total = rs[c][y].astype(F32)
        for k in range(YN - 1):
            total = total + r1[c][k].astype(F32)
        total = total.astype(BF16)
        tall = jnp.concatenate([total[:, 128 * l : 128 * l + 128] for l in range(TILES[c])], axis=0)
        s2[c][...] = dot(to_piece[c][...], tall).astype(BF16).reshape(TN, PIECE[c], 128)
        copies = [
            remote(s2[c].at[ts[k]], r2[c].at[k], b_send.at[c, k], b_recv.at[c, k], to_t[k]) for k in range(TN - 1)]
        for copy in copies:
            copy.start()
        sent.extend(first)
        return copies

    def pixels(c, second):
        for copy in second:
            copy.wait_recv()
        sent.extend(second)
        total = terms[c][...] + s2[c][t].astype(F32)
        for k in range(TN - 1):
            total = total + r2[c][k].astype(F32)
        lo, hi = SPAN[c]
        turned = pltpu.roll(total, 64, 1) if c == 0 else None
        for i in range(OWN):
            for s in range(S):
                row = OWN * s + i if c else OWN * (s // 2) + i
                source = total if c or s % 2 == 0 else turned
                incs[i, s : s + 1, :] = source[row : row + 1, :]
        inc = [incs[i, 0:S, 0 : hi - lo] for i in range(OWN)]
        counts = count[:, lo:hi].astype(F32)

        def channels(step, grads):
            base = pl.multiple_of(8 * step, 8)
            square = squares[pl.ds(base, 8), 0:1]
            grads = list(grads)
            for i in range(OWN):
                weight = mask[i, pl.ds(base, 8), lo:hi].astype(F32) * counts[i : i + 1, :] / square
                for n in range(8):
                    jac_n = jac[base + n, i, :, lo:hi].astype(F32)
                    radiance = jnp.sum(jac_n * inc[i], axis=0, keepdims=True)
                    grads[i] = grads[i] + jac_n * (weight[n : n + 1, :] * radiance)
            return tuple(grads)

        grads = lax.fori_loop(0, CH // 8, channels, tuple(jnp.zeros((S, hi - lo), F32) for _ in range(OWN)))
        gr[...] = jnp.zeros_like(gr)
        for i in range(OWN):
            for s in range(S):
                row = OWN * s + i if c else OWN * (s // 2) + i
                half = 0 if c else s % 2
                gr[half, row : row + 1, 0 : hi - lo] = grads[i][s : s + 1, :].astype(BF16).astype(F32)
        gp[c][...] = (gr[0] if c else joined(gr[0, 0 : PIECE[0]], gr[1, 0 : PIECE[0]])).astype(BF16)
        copies = [remote(gp[c], gz[c].at[t], c_send.at[c, k], c_recv.at[c, k], to_t[k]) for k in range(TN - 1)]
        for copy in copies:
            copy.start()
        gz[c][t] = gp[c][...]
        return copies

    def gather(c, third):
        for copy in third:
            copy.wait_recv()
        sent.extend(third)
        tall = dot(from_piece[c][...], gz[c][...].reshape(TN * PIECE[c], 128)).astype(BF16)
        for l in range(TILES[c]):
            ag[c][y, :, 128 * l : 128 * l + 128] = tall[ROWS * l : ROWS * l + ROWS]
        copies = [remote(ag[c].at[y], ag[c].at[y], d_send.at[c, k], d_recv.at[c, k], to_y[k]) for k in range(YN - 1)]
        for copy in copies:
            copy.start()
        return copies

    source, half = far + (cross - far) * (y // 2), y % 2

    def adjoint(c, fourth):
        for copy in fourth:
            copy.wait_recv()
        sent.extend(fourth)
        gradient = ag[c][...].reshape(LAT, 128 * TILES[c]).astype(F32)
        width = 64 * TILES[c]
        back = dot(latpt[...], (spread[MEMB, 0:LAT, lanes[c]] * gradient).astype(BF16)).astype(BF16)
        back = back.reshape(4, ROWS, 128 * TILES[c])
        for h in range(2):
            bss[c][h] = back[:, :, width * h : width * h + width]
        fixed = [
            remote(bss[c].at[half, source], brs[c].at[half, band], g_send.at[c, 0], g_recv.at[c, 0], at_band(source)),
            remote(bss[c].at[:, sib], brs[c].at[:, band], g_send.at[c, 1], g_recv.at[c, 1], at_band(sib)),
        ] + [
            remote(brs[c].at[half, source], brs[c].at[half, source], g_send.at[c, 2 + k], g_recv.at[c, 2 + k], to_y[k])
            for k in range(YN - 1)]
        for copy in fixed[:2]:
            copy.start()
        for m in range(MEMB):
            back = dot(latpt[...], (spread[m, 0:LAT, lanes[c]] * gradient).astype(BF16)).astype(BF16)
            bs[c][:, m] = back.reshape(4, ROWS, 128 * TILES[c])
        copies = [
            remote(bs[c].at[far], br[c].at[band], e_send.at[c, 0], e_recv.at[c, 0], at_band(far)),
            remote(bs[c].at[cross], bl[c], e_send.at[c, 1], e_recv.at[c, 1], at_band(sib)),
            remote(bs[c].at[sib], br[c].at[band], e_send.at[c, 2], e_recv.at[c, 2], at_band(sib)),
            remote(bl[c], br[c].at[sib], e_send.at[c, 3], e_recv.at[c, 3], at_band(far)),
        ]
        for copy in copies[:3]:
            copy.start()
        br[c][band] = bs[c][band]
        for h in range(2):
            brs[c][h, band] = bss[c][h, band]
        return copies, fixed

    first = [sum_first(0)]

    for load in loads[10:]:
        load.wait()
    rem[...] = jnp.zeros_like(rem)
    for h in range(2):
        for s in range(2):
            value = std[2 * h + s]
            ordered = None
            for _ in range(3):
                top = value.astype(BF16)
                term = dot(order[...], top, (1, 1))
                ordered = term if ordered is None else ordered + term
                value = value - top.astype(F32)
            ordered = 0.6 * ordered
            spread[MEMB, 0:LAT, 128 * (2 * h + s) : 128 * (2 * h + s) + 128] = ordered[:, 0:128]
            rem[s, :, 0:REM] = ordered[:, 128:COLS]
        spread[MEMB, 0:LAT, 512 + 128 * h : 640 + 128 * h] = joined(rem[0], rem[1])

    spread[:, LAT:] = jnp.zeros((FIELDS, 8, WIDE), F32)
    first_row = ROWS * y + OWN * t
    shift = first_row % 8
    own_std = spread[MEMB, pl.ds(pl.multiple_of(first_row - shift, 8), 16), :]
    own_std = pltpu.roll(own_std, (16 - shift) % 16, 0)[0:8]
    for copy in static_copies:
        copy.wait_recv()
    sent.extend(static_copies)
    static_term = own_std * (sr[0] + sr[1] + sr[2] + sr[3])
    for c in range(CHUNKS):
        terms[c][...] = jnp.zeros_like(terms[c])
        for l in range(TILES[c]):
            terms[c][OWN * l : OWN * l + OWN] = static_term[0:OWN, BASE[c] + 128 * l : BASE[c] + 128 * l + 128]
    for load in loads[5:9]:
        load.wait()
    error = jnp.sum(jnp.where(iota((CH, CH), 0) == iota((CH, CH), 1), error_row[...], 0.0), axis=1, keepdims=True)
    squares[...] = jnp.broadcast_to(error * error, squares.shape)

    second = [sum_second(0, first[0])]

    first.append(sum_first(1))
    latpt[...] = dot(jnp.transpose(lat[...].astype(F32)).astype(BF16), order[...], (1, 1)).astype(BF16)
    for c in range(CHUNKS):
        rows, height = TN * PIECE[c], ROWS * TILES[c]
        hot = iota((height, rows), 0) == piece_row(c, iota((height, rows), 1))
        from_piece[c][...] = jnp.where(hot, 1.0, 0.0).astype(BF16)

    third = [pixels(0, second[0])]

    second.append(sum_second(1, first[1]))

    fourth = [gather(0, third[0])]

    third.append(pixels(1, second[1]))

    ways = [adjoint(0, fourth[0])]
    ways[0][0][1].wait_recv()
    ways[0][0][3].start()

    fourth.append(gather(1, third[1]))
    ways[0][1][0].wait_recv()
    for copy in ways[0][1][2:]:
        copy.start()

    ways.append(adjoint(1, fourth[1]))
    ways[1][0][1].wait_recv()
    ways[1][0][3].start()

    result = [ga.at[0], ga.at[1], gs]
    copies, fixed = ways[0]
    for copy in copies[:1] + copies[2:]:
        copy.wait_recv()
    for f in range(FIELDS):
        if f == MEMB:
            for copy in fixed[1:]:
                copy.wait_recv()
        for h in range(2):
            if f < MEMB:
                tiles = [br[0][b, f, :, 128 * h : 128 * h + 128].astype(F32) for b in range(4)]
            else:
                tiles = [brs[0][h, b].astype(F32) for b in range(4)]
            for s in range(2):
                join = joined if s == 0 else joined_high
                for g in range(2):
                    pair = join(tiles[2 * g], tiles[2 * g + 1]).astype(BF16)
                    lhs[0][pl.ds((2 * h + s) * ROWS, ROWS), 128 * g : 128 * g + 128] = pair
        base = alpha[f] if f < MEMB else static[...]
        result[f][...] = base.astype(F32) + dot(lhs[0][...], w[:, lanes[0]], (1, 1)).reshape(S, ROWS, LON)
        if f == MEMB - 1:
            ways[1][1][0].wait_recv()
            for copy in ways[1][1][2:]:
                copy.start()

    copies, fixed = ways[1]
    for f in range(FIELDS):
        if f == 0:
            for copy in copies[:1] + copies[2:]:
                copy.wait_recv()
        if f == MEMB:
            for copy in fixed[1:]:
                copy.wait_recv()
        for s in range(S):
            for b in range(4):
                if f < MEMB:
                    tile = br[1][b, f, :, 128 * s : 128 * s + 128]
                else:
                    tile = brs[1][s // 2, b, :, 128 * (s % 2) : 128 * (s % 2) + 128]
                lhs[1][ROWS * s : ROWS * s + ROWS, 128 * b : 128 * b + 128] = tile
        result[f][...] = result[f][...] + dot(lhs[1][...], w[:, lanes[1]], (1, 1)).reshape(S, ROWS, LON)
    for copies, fixed in ways:
        sent.extend(copies)
        sent.extend(fixed)
    for copy in sent:
        copy.wait_send()


def shards(alpha, static_ctl, perturbations, static_std, lon_root, lat_root, jacobian, obs_count, channel_mask,
           channel_error, member_weight):
    inputs = [alpha, static_ctl, jnp.transpose(perturbations, (0, 3, 1, 2)), jnp.transpose(static_std, (2, 0, 1)),
              lon_root, lat_root, jnp.transpose(jacobian, (0, 2, 1, 3)), obs_count, jnp.transpose(channel_mask, (1, 0, 2)),
              channel_error.reshape(1, CH), member_weight.reshape(1, MEM)]
    dma, vmem = pltpu.SemaphoreType.DMA, pltpu.VMEM
    scratch = [
        vmem((MEMB, S, ROWS, LON), BF16),
        vmem((S, ROWS, LON), BF16),
        vmem((MEMB, S * COLS, LAT), BF16),
        vmem((S, COLS, LAT), F32),
        vmem((LON, LON), BF16),
        vmem((LAT, LAT), BF16),
        vmem((CH, OWN, S, COLS), BF16),
        vmem((OWN, COLS), I32),
        vmem((OWN, CH, COLS), I32),
        vmem((1, CH), F32),
        vmem((1, MEM), I32),
        vmem((LON, WIDE), BF16),
        vmem((4, 8, WIDE), F32),
        vmem((4, 8, WIDE), F32),
        vmem((FIELDS, LAT + 8, WIDE), F32),
        vmem((2, LAT, 128), F32),
        vmem((LAT, LAT), BF16),
        vmem((LAT, LAT), BF16),
        vmem((LAT, LAT), BF16),
        vmem((S * COLS, WIDE), BF16),
        vmem((CH, 128), F32),
        vmem((OWN, 8, 128), F32),
        vmem((2, 32, 128), F32),
    ]

    def both(shape, kind):
        return [vmem(shape(128 * TILES[c], PIECE[c], ROWS * TILES[c]), kind) for c in range(CHUNKS)]

    scratch += both(lambda n, r, h: (4, MEMB, ROWS, n), BF16)
    scratch += both(lambda n, r, h: (MEMB, ROWS, n), BF16)
    scratch += both(lambda n, r, h: (4, MEMB, ROWS, n), BF16)
    scratch += both(lambda n, r, h: (YN, ROWS, n), BF16)
    scratch += both(lambda n, r, h: (YN - 1, ROWS, n), BF16)
    scratch += both(lambda n, r, h: (TN, r, 128), BF16)
    scratch += both(lambda n, r, h: (TN - 1, r, 128), BF16)
    scratch += both(lambda n, r, h: (r, 128), F32)
    scratch += both(lambda n, r, h: (r, 128), BF16)
    scratch += both(lambda n, r, h: (TN, r, 128), BF16)
    scratch += both(lambda n, r, h: (YN, ROWS, n), BF16)
    scratch += both(lambda n, r, h: (4, MEMB, ROWS, n), BF16)
    scratch += both(lambda n, r, h: (MEMB, ROWS, n), BF16)
    scratch += both(lambda n, r, h: (4, MEMB, ROWS, n), BF16)
    scratch += both(lambda n, r, h: (2, 4, ROWS, n // 2), BF16)
    scratch += both(lambda n, r, h: (2, 4, ROWS, n // 2), BF16)
    scratch += both(lambda n, r, h: (TN * r, h), BF16)
    scratch += both(lambda n, r, h: (h, TN * r), BF16)
    scratch += both(lambda n, r, h: (S * ROWS, n), BF16)
    scratch += [
        dma((10,)), dma((S,)),
        dma((2, 4)), dma((2, 4)), dma((3,)), dma((3,)),
        dma((2, YN - 1)), dma((2, YN - 1)), dma((2, TN - 1)), dma((2, TN - 1)),
        dma((2, TN - 1)), dma((2, TN - 1)), dma((2, YN - 1)), dma((2, YN - 1)),
        dma((2, 4)), dma((2, 4)), dma((2, YN + 1)), dma((2, YN + 1)),
    ]
    return pl.pallas_call(
        kernel,
        out_shape=(jax.ShapeDtypeStruct((MEMB, S, ROWS, LON), F32), jax.ShapeDtypeStruct((S, ROWS, LON), F32)),
        in_specs=[pl.BlockSpec(memory_space=pltpu.HBM)] * len(inputs),
        out_specs=(pl.BlockSpec(memory_space=pltpu.VMEM),) * 2,
        scratch_shapes=scratch,
        compiler_params=pltpu.CompilerParams(collective_id=0, has_side_effects=True, vmem_limit_bytes=40 << 20),
        name="hessian",
    )(*[pltpu.with_memory_space_constraint(v, pltpu.HBM) for v in inputs])


def solution(mesh):
    in_specs = (
        P("mem", None, "band", None),
        P(None, "band", None),
        P("mem", None, None, "band"),
        P(None, None, "band"),
        P(),
        P(),
        P(None, None, "mem", "band"),
        P("mem", "band"),
        P(None, "mem", "band"),
        P(),
        P(),
    )
    out_specs = (P("mem", None, "band", None), P(None, "band", None))
    return jax.shard_map(shards, mesh=mesh, in_specs=in_specs, out_specs=out_specs, check_vma=False)
```

```python
import functools

import jax
import jax.numpy as jnp
from jax import lax
from jax.experimental import pallas as pl
from jax.experimental.pallas import tpu as pltpu
from jax.sharding import PartitionSpec as P

MESH = pl.DeviceIdType.MESH
F32, BF16, I32 = jnp.float32, jnp.bfloat16, jnp.int32

S, CH, MEM, MEMB, FIELDS = 4, 32, 128, 2, 3
ROWS, LAT, LON, COLS = 80, 320, 720, 180
REM = COLS - 128
YN, TN, OWN = 4, 16, 5
WIDE = 768
NEXT_Y, NEXT_T = (2, 1, 3), (8, 7, 9, 6, 10, 5, 11, 4, 12, 3, 13, 2, 14, 1, 15)
CHUNKS = 2
TILES = (2, 4)
BASE = (512, 0)
PIECE = (16, 32)
SPAN = ((128, COLS), (0, 128))


def iota(shape, dim):
    return lax.broadcasted_iota(I32, shape, dim)


def one_hot(rows, columns, column_of_row):
    return jnp.where(iota((rows, columns), 1) == column_of_row(iota((rows, columns), 0)), 1.0, 0.0).astype(BF16)


def fifth(x):
    return (x * 205) // 1024


def grid_row(p):
    y = p // ROWS
    t = fifth(p - ROWS * y)
    return OWN * (8 * (t // 2) + 4 * (t % 2) + y) + p - ROWS * y - OWN * t


def packed_lane(row):
    j, s = row // 4, row % 4
    return jnp.where(j < 128, 128 * s + j, 512 + 128 * (s // 2) + 64 * (s % 2) + j - 128)


def piece_row(c, a):
    t, r = a // PIECE[c], a % PIECE[c]
    tile = fifth(r)
    return jnp.where(r < TILES[c] * OWN, ROWS * tile + OWN * t + r - OWN * tile, -1)


def low_half(shape):
    return iota(shape, len(shape) - 1) < 64


def joined(even, odd):
    return jnp.where(low_half(even.shape), even, pltpu.roll(odd, 64, 1))


def joined_high(even, odd):
    return jnp.where(low_half(even.shape), pltpu.roll(even, 64, 1), odd)


def dot(a, b, contract=(1, 0)):
    return lax.dot_general(a, b, (((contract[0],), (contract[1],)), ((), ())), preferred_element_type=F32)


def kernel(
    alpha_hbm, static_hbm, pert_hbm, std_hbm, lon_hbm, lat_hbm, jac_hbm, count_hbm, mask_hbm, error_hbm, weight_hbm,
    ga, gs,
    alpha, static, pert, std, lon, lat, jac, count, mask, error_row, weight_row,
    w, ss, sr, spread, rem, order, latp, latpt, spreader, squares, incs, gr,
    fs0, fs1, rl0, rl1, xr0, xr1, rs0, rs1, r10, r11, s20, s21, r20, r21, terms0, terms1, gp0, gp1, gz0, gz1, ag0, ag1,
    bs0, bs1, bl0, bl1, br0, br1, bss0, bss1, brs0, brs1, to0, to1, from0, from1, lhs0, lhs1,
    load_sem, std_sem, f_send, f_recv, t_send, t_recv, a_send, a_recv, b_send, b_recv, c_send, c_recv,
    d_send, d_recv, e_send, e_recv, g_send, g_recv,
):
    fs, rl, xr, rs, r1, s2, r2 = (fs0, fs1), (rl0, rl1), (xr0, xr1), (rs0, rs1), (r10, r11), (s20, s21), (r20, r21)
    terms, gp, gz, ag, bs, bl, br = (terms0, terms1), (gp0, gp1), (gz0, gz1), (ag0, ag1), (bs0, bs1), (bl0, bl1), (br0, br1)
    bss, brs, to_piece, from_piece, lhs = (bss0, bss1), (brs0, brs1), (to0, to1), (from0, from1), (lhs0, lhs1)
    lanes = [slice(BASE[c], BASE[c] + 128 * TILES[c]) for c in range(CHUNKS)]

    mem, band = lax.axis_index("mem"), lax.axis_index("band")
    z, x, y = mem // 8, (mem // 4) % 2, mem % 4
    t = 2 * z + x
    chip, core = band // 2, band % 2
    sib, far, cross = 2 * chip + 1 - core, 2 * (1 - chip) + core, 3 - band

    def at_band(b):
        return {"mem": mem, "band": b}

    ys = [lax.rem(y + k, YN) for k in NEXT_Y]
    to_y = [{"mem": 8 * z + 4 * x + v, "band": band} for v in ys]
    ts = [lax.rem(t + k, TN) for k in NEXT_T]
    to_t = [{"mem": 8 * (v // 2) + 4 * (v % 2) + y, "band": band} for v in ts]

    staged = [(lon_hbm, lon), (alpha_hbm, alpha), (static_hbm, static), (lat_hbm, lat),
              (pert_hbm.reshape(MEMB, S * COLS, LAT), pert), (jac_hbm, jac), (count_hbm, count), (mask_hbm, mask),
              (error_hbm, error_row), (weight_hbm, weight_row)]
    loads = [pltpu.make_async_copy(src, dst, load_sem.at[i]) for i, (src, dst) in enumerate(staged)]
    loads += [pltpu.make_async_copy(std_hbm.at[:, s, :], std.at[s], std_sem.at[s]) for s in range(S)]
    barrier = pltpu.get_barrier_semaphore()
    partners = to_t + to_y + [at_band(far), at_band(cross), at_band(sib)]
    for device in partners:
        pl.semaphore_signal(barrier, inc=1, device_id=device, device_id_type=MESH)
    for load in loads:
        load.start()

    def remote(src, dst, send, recv, device):
        return pltpu.make_async_remote_copy(
            src_ref=src, dst_ref=dst, send_sem=send, recv_sem=recv, device_id=device, device_id_type=MESH)

    sent = []

    loads[0].wait()
    for b in range(4):
        w[:, 512 + 64 * b : 512 + 64 * b + REM] = lon[:, COLS * b + 128 : COLS * b + COLS]
        w[:, 512 + 64 * b + REM : 576 + 64 * b] = jnp.zeros((LON, 64 - REM), BF16)
        w[:, 128 * b : 128 * b + 128] = lon[:, COLS * b : COLS * b + 128]

    forward = []
    loads[1].wait()
    for c in range(CHUNKS):
        v = dot(alpha[...].reshape(MEMB * S * ROWS, LON), w[:, lanes[c]])
        v = v.reshape(MEMB, S, ROWS, 128 * TILES[c])
        for m in range(MEMB):
            for b in range(4):
                if c == 0:
                    tile = 128 * (b // 2)
                    join = joined if b % 2 == 0 else joined_high
                    for h in range(2):
                        pair = join(v[m, 2 * h][:, tile : tile + 128], v[m, 2 * h + 1][:, tile : tile + 128])
                        fs[c][b, m, :, 128 * h : 128 * h + 128] = pair.astype(BF16)
                else:
                    for s in range(S):
                        fs[c][b, m, :, 128 * s : 128 * s + 128] = v[m, s][:, 128 * b : 128 * b + 128].astype(BF16)
        copies = [
            remote(fs[c].at[far], xr[c].at[band], f_send.at[c, 0], f_recv.at[c, 0], at_band(far)),
            remote(fs[c].at[cross], rl[c], f_send.at[c, 1], f_recv.at[c, 1], at_band(sib)),
            remote(fs[c].at[sib], xr[c].at[band], f_send.at[c, 2], f_recv.at[c, 2], at_band(sib)),
            remote(rl[c], xr[c].at[sib], f_send.at[c, 3], f_recv.at[c, 3], at_band(far)),
        ]
        forward.append(copies)
        xr[c][band] = fs[c][band]

    loads[2].wait()
    loads[3].wait()
    v = dot(static[...].reshape(S * ROWS, LON), w[...]).astype(BF16)
    own_rows = dot(one_hot(16, LAT, lambda k: jnp.where(k < OWN, OWN * mem + k, -1)), lat[...]).astype(BF16)
    here = jnp.where(iota((LAT, ROWS), 0) == ROWS * band + iota((LAT, ROWS), 1), 1.0, 0.0).astype(BF16)
    own_part = dot(own_rows, here).astype(BF16)
    parts = [dot(own_part, v[ROWS * s : ROWS * s + ROWS])[0:8] for s in range(S)]
    for b in range(4):
        tile = 512 + 128 * (b // 2)
        join = joined if b % 2 == 0 else joined_high
        for s in range(S):
            ss[b, :, 128 * s : 128 * s + 128] = parts[s][:, 128 * b : 128 * b + 128]
        for h in range(2):
            ss[b, :, 512 + 128 * h : 640 + 128 * h] = join(
                parts[2 * h][:, tile : tile + 128], parts[2 * h + 1][:, tile : tile + 128])
    others = (far, cross, sib)
    static_copies = [remote(ss.at[b], sr.at[band], t_send.at[k], t_recv.at[k], at_band(b)) for k, b in enumerate(others)]
    sr[band] = ss[band]
    order[...] = one_hot(LAT, LAT, grid_row)
    latp[...] = dot(order[...], lat[...]).astype(BF16)
    pl.semaphore_wait(barrier, len(partners))
    for copy in forward[0][:3] + [forward[1][1]] + static_copies:
        copy.start()
    forward[0][1].wait_recv()
    forward[0][3].start()
    forward[1][0].start()
    forward[1][1].wait_recv()
    forward[1][3].start()
    forward[1][2].start()

    spreader[...] = one_hot(S * COLS, WIDE, packed_lane)
    loads[9].wait()
    weights = weight_row[...].astype(F32)
    coef = weights / jnp.sqrt(jnp.sum(weights * weights, axis=1, keepdims=True))
    loads[4].wait()
    for m in range(MEMB):
        factor = 0.8 * jnp.sum(jnp.where(iota(coef.shape, 1) == MEMB * mem + m, coef, 0.0), axis=1, keepdims=True)
        ordered = dot(order[...], pert[m], (1, 1)).astype(BF16)
        spread[m, 0:LAT] = factor * dot(ordered, spreader[...])
    for c in range(CHUNKS):
        rows, height = TN * PIECE[c], ROWS * TILES[c]
        to_piece[c][...] = one_hot(rows, height, lambda a: piece_row(c, a))

    def sum_first(c):
        for k in (0, 2, 3):
            forward[c][k].wait_recv()
        total = None
        for m in range(MEMB):
            field = dot(latp[...], xr[c][:, m].reshape(LAT, 128 * TILES[c]))
            term = spread[m, 0:LAT, lanes[c]] * field
            total = term if total is None else total + term
        rs[c][...] = total.astype(BF16).reshape(YN, ROWS, 128 * TILES[c])
        copies = [
            remote(rs[c].at[ys[k]], r1[c].at[k], a_send.at[c, k], a_recv.at[c, k], to_y[k]) for k in range(YN - 1)]
        for copy in copies:
            copy.start()
        sent.extend(forward[c])
        return copies

    def sum_second(c, first):
        for copy in first:
            copy.wait_recv()
        total = rs[c][y].astype(F32)
        for k in range(YN - 1):
            total = total + r1[c][k].astype(F32)
        total = total.astype(BF16)
        tall = jnp.concatenate([total[:, 128 * l : 128 * l + 128] for l in range(TILES[c])], axis=0)
        s2[c][...] = dot(to_piece[c][...], tall).astype(BF16).reshape(TN, PIECE[c], 128)
        copies = [
            remote(s2[c].at[ts[k]], r2[c].at[k], b_send.at[c, k], b_recv.at[c, k], to_t[k]) for k in range(TN - 1)]
        for copy in copies:
            copy.start()
        sent.extend(first)
        return copies

    def pixels(c, second):
        for copy in second:
            copy.wait_recv()
        sent.extend(second)
        total = terms[c][...] + s2[c][t].astype(F32)
        for k in range(TN - 1):
            total = total + r2[c][k].astype(F32)
        lo, hi = SPAN[c]
        turned = pltpu.roll(total, 64, 1) if c == 0 else None
        for i in range(OWN):
            for s in range(S):
                row = OWN * s + i if c else OWN * (s // 2) + i
                source = total if c or s % 2 == 0 else turned
                incs[i, s : s + 1, :] = source[row : row + 1, :]
        inc = [incs[i, 0:S, 0 : hi - lo] for i in range(OWN)]
        counts = count[:, lo:hi].astype(F32)

        def channels(step, grads):
            base = pl.multiple_of(8 * step, 8)
            square = squares[pl.ds(base, 8), 0:1]
            grads = list(grads)
            for i in range(OWN):
                weight = mask[i, pl.ds(base, 8), lo:hi].astype(F32) * counts[i : i + 1, :] / square
                for n in range(8):
                    jac_n = jac[base + n, i, :, lo:hi].astype(F32)
                    radiance = jnp.sum(jac_n * inc[i], axis=0, keepdims=True)
                    grads[i] = grads[i] + jac_n * (weight[n : n + 1, :] * radiance)
            return tuple(grads)

        grads = lax.fori_loop(0, CH // 8, channels, tuple(jnp.zeros((S, hi - lo), F32) for _ in range(OWN)))
        gr[...] = jnp.zeros_like(gr)
        for i in range(OWN):
            for s in range(S):
                row = OWN * s + i if c else OWN * (s // 2) + i
                half = 0 if c else s % 2
                gr[half, row : row + 1, 0 : hi - lo] = grads[i][s : s + 1, :].astype(BF16).astype(F32)
        gp[c][...] = (gr[0] if c else joined(gr[0, 0 : PIECE[0]], gr[1, 0 : PIECE[0]])).astype(BF16)
        copies = [remote(gp[c], gz[c].at[t], c_send.at[c, k], c_recv.at[c, k], to_t[k]) for k in range(TN - 1)]
        for copy in copies:
            copy.start()
        gz[c][t] = gp[c][...]
        return copies

    def gather(c, third):
        for copy in third:
            copy.wait_recv()
        sent.extend(third)
        tall = dot(from_piece[c][...], gz[c][...].reshape(TN * PIECE[c], 128)).astype(BF16)
        for l in range(TILES[c]):
            ag[c][y, :, 128 * l : 128 * l + 128] = tall[ROWS * l : ROWS * l + ROWS]
        copies = [remote(ag[c].at[y], ag[c].at[y], d_send.at[c, k], d_recv.at[c, k], to_y[k]) for k in range(YN - 1)]
        for copy in copies:
            copy.start()
        return copies

    source, half = far + (cross - far) * (y // 2), y % 2

    def adjoint(c, fourth):
        for copy in fourth:
            copy.wait_recv()
        sent.extend(fourth)
        gradient = ag[c][...].reshape(LAT, 128 * TILES[c]).astype(F32)
        width = 64 * TILES[c]
        back = dot(latpt[...], (spread[MEMB, 0:LAT, lanes[c]] * gradient).astype(BF16)).astype(BF16)
        back = back.reshape(4, ROWS, 128 * TILES[c])
        for h in range(2):
            bss[c][h] = back[:, :, width * h : width * h + width]
        fixed = [
            remote(bss[c].at[half, source], brs[c].at[half, band], g_send.at[c, 0], g_recv.at[c, 0], at_band(source)),
            remote(bss[c].at[:, sib], brs[c].at[:, band], g_send.at[c, 1], g_recv.at[c, 1], at_band(sib)),
        ] + [
            remote(brs[c].at[half, source], brs[c].at[half, source], g_send.at[c, 2 + k], g_recv.at[c, 2 + k], to_y[k])
            for k in range(YN - 1)]
        for copy in fixed[:2]:
            copy.start()
        for m in range(MEMB):
            back = dot(latpt[...], (spread[m, 0:LAT, lanes[c]] * gradient).astype(BF16)).astype(BF16)
            bs[c][:, m] = back.reshape(4, ROWS, 128 * TILES[c])
        copies = [
            remote(bs[c].at[far], br[c].at[band], e_send.at[c, 0], e_recv.at[c, 0], at_band(far)),
            remote(bs[c].at[cross], bl[c], e_send.at[c, 1], e_recv.at[c, 1], at_band(sib)),
            remote(bs[c].at[sib], br[c].at[band], e_send.at[c, 2], e_recv.at[c, 2], at_band(sib)),
            remote(bl[c], br[c].at[sib], e_send.at[c, 3], e_recv.at[c, 3], at_band(far)),
        ]
        for copy in copies[:3]:
            copy.start()
        br[c][band] = bs[c][band]
        for h in range(2):
            brs[c][h, band] = bss[c][h, band]
        return copies, fixed

    first = [sum_first(0)]

    for load in loads[10:]:
        load.wait()
    rem[...] = jnp.zeros_like(rem)
    for h in range(2):
        for s in range(2):
            value = std[2 * h + s]
            ordered = None
            for _ in range(3):
                top = value.astype(BF16)
                term = dot(order[...], top, (1, 1))
                ordered = term if ordered is None else ordered + term
                value = value - top.astype(F32)
            ordered = 0.6 * ordered
            spread[MEMB, 0:LAT, 128 * (2 * h + s) : 128 * (2 * h + s) + 128] = ordered[:, 0:128]
            rem[s, :, 0:REM] = ordered[:, 128:COLS]
        spread[MEMB, 0:LAT, 512 + 128 * h : 640 + 128 * h] = joined(rem[0], rem[1])

    spread[:, LAT:] = jnp.zeros((FIELDS, 8, WIDE), F32)
    first_row = ROWS * y + OWN * t
    shift = first_row % 8
    own_std = spread[MEMB, pl.ds(pl.multiple_of(first_row - shift, 8), 16), :]
    own_std = pltpu.roll(own_std, (16 - shift) % 16, 0)[0:8]
    for copy in static_copies:
        copy.wait_recv()
    sent.extend(static_copies)
    static_term = own_std * (sr[0] + sr[1] + sr[2] + sr[3])
    for c in range(CHUNKS):
        terms[c][...] = jnp.zeros_like(terms[c])
        for l in range(TILES[c]):
            terms[c][OWN * l : OWN * l + OWN] = static_term[0:OWN, BASE[c] + 128 * l : BASE[c] + 128 * l + 128]
    for load in loads[5:9]:
        load.wait()
    error = jnp.sum(jnp.where(iota((CH, CH), 0) == iota((CH, CH), 1), error_row[...], 0.0), axis=1, keepdims=True)
    squares[...] = jnp.broadcast_to(error * error, squares.shape)

    second = [sum_second(0, first[0])]

    first.append(sum_first(1))
    latpt[...] = dot(jnp.transpose(lat[...].astype(F32)).astype(BF16), order[...], (1, 1)).astype(BF16)
    for c in range(CHUNKS):
        rows, height = TN * PIECE[c], ROWS * TILES[c]
        hot = iota((height, rows), 0) == piece_row(c, iota((height, rows), 1))
        from_piece[c][...] = jnp.where(hot, 1.0, 0.0).astype(BF16)

    third = [pixels(0, second[0])]

    second.append(sum_second(1, first[1]))

    fourth = [gather(0, third[0])]

    third.append(pixels(1, second[1]))

    ways = [adjoint(0, fourth[0])]
    ways[0][0][1].wait_recv()
    ways[0][0][3].start()

    fourth.append(gather(1, third[1]))
    ways[0][1][0].wait_recv()
    for copy in ways[0][1][2:]:
        copy.start()

    ways.append(adjoint(1, fourth[1]))
    ways[1][0][1].wait_recv()
    ways[1][0][3].start()

    result = [ga.at[0], ga.at[1], gs]
    copies, fixed = ways[0]
    for copy in copies[:1] + copies[2:]:
        copy.wait_recv()
    for f in range(FIELDS):
        if f == MEMB:
            for copy in fixed[1:]:
                copy.wait_recv()
        for h in range(2):
            if f < MEMB:
                tiles = [br[0][b, f, :, 128 * h : 128 * h + 128].astype(F32) for b in range(4)]
            else:
                tiles = [brs[0][h, b].astype(F32) for b in range(4)]
            for s in range(2):
                join = joined if s == 0 else joined_high
                for g in range(2):
                    pair = join(tiles[2 * g], tiles[2 * g + 1]).astype(BF16)
                    lhs[0][pl.ds((2 * h + s) * ROWS, ROWS), 128 * g : 128 * g + 128] = pair
        base = alpha[f] if f < MEMB else static[...]
        result[f][...] = base.astype(F32) + dot(lhs[0][...], w[:, lanes[0]], (1, 1)).reshape(S, ROWS, LON)
        if f == MEMB - 1:
            ways[1][1][0].wait_recv()
            for copy in ways[1][1][2:]:
                copy.start()

    copies, fixed = ways[1]
    for f in range(FIELDS):
        if f == 0:
            for copy in copies[:1] + copies[2:]:
                copy.wait_recv()
        if f == MEMB:
            for copy in fixed[1:]:
                copy.wait_recv()
        for s in range(S):
            for b in range(4):
                if f < MEMB:
                    tile = br[1][b, f, :, 128 * s : 128 * s + 128]
                else:
                    tile = brs[1][s // 2, b, :, 128 * (s % 2) : 128 * (s % 2) + 128]
                lhs[1][ROWS * s : ROWS * s + ROWS, 128 * b : 128 * b + 128] = tile
        result[f][...] = result[f][...] + dot(lhs[1][...], w[:, lanes[1]], (1, 1)).reshape(S, ROWS, LON)
    for copies, fixed in ways:
        sent.extend(copies)
        sent.extend(fixed)
    for copy in sent:
        copy.wait_send()


def shards(alpha, static_ctl, perturbations, static_std, lon_root, lat_root, jacobian, obs_count, channel_mask,
           channel_error, member_weight):
    inputs = [alpha, static_ctl, jnp.transpose(perturbations, (0, 3, 1, 2)), jnp.transpose(static_std, (2, 0, 1)),
              lon_root, lat_root, jnp.transpose(jacobian, (0, 2, 1, 3)), obs_count, jnp.transpose(channel_mask, (1, 0, 2)),
              channel_error.reshape(1, CH), member_weight.reshape(1, MEM)]
    dma, vmem = pltpu.SemaphoreType.DMA, pltpu.VMEM
    scratch = [
        vmem((MEMB, S, ROWS, LON), BF16),
        vmem((S, ROWS, LON), BF16),
        vmem((MEMB, S * COLS, LAT), BF16),
        vmem((S, COLS, LAT), F32),
        vmem((LON, LON), BF16),
        vmem((LAT, LAT), BF16),
        vmem((CH, OWN, S, COLS), BF16),
        vmem((OWN, COLS), I32),
        vmem((OWN, CH, COLS), I32),
        vmem((1, CH), F32),
        vmem((1, MEM), I32),
        vmem((LON, WIDE), BF16),
        vmem((4, 8, WIDE), F32),
        vmem((4, 8, WIDE), F32),
        vmem((FIELDS, LAT + 8, WIDE), F32),
        vmem((2, LAT, 128), F32),
        vmem((LAT, LAT), BF16),
        vmem((LAT, LAT), BF16),
        vmem((LAT, LAT), BF16),
        vmem((S * COLS, WIDE), BF16),
        vmem((CH, 128), F32),
        vmem((OWN, 8, 128), F32),
        vmem((2, 32, 128), F32),
    ]

    def both(shape, kind):
        return [vmem(shape(128 * TILES[c], PIECE[c], ROWS * TILES[c]), kind) for c in range(CHUNKS)]

    scratch += both(lambda n, r, h: (4, MEMB, ROWS, n), BF16)
    scratch += both(lambda n, r, h: (MEMB, ROWS, n), BF16)
    scratch += both(lambda n, r, h: (4, MEMB, ROWS, n), BF16)
    scratch += both(lambda n, r, h: (YN, ROWS, n), BF16)
    scratch += both(lambda n, r, h: (YN - 1, ROWS, n), BF16)
    scratch += both(lambda n, r, h: (TN, r, 128), BF16)
    scratch += both(lambda n, r, h: (TN - 1, r, 128), BF16)
    scratch += both(lambda n, r, h: (r, 128), F32)
    scratch += both(lambda n, r, h: (r, 128), BF16)
    scratch += both(lambda n, r, h: (TN, r, 128), BF16)
    scratch += both(lambda n, r, h: (YN, ROWS, n), BF16)
    scratch += both(lambda n, r, h: (4, MEMB, ROWS, n), BF16)
    scratch += both(lambda n, r, h: (MEMB, ROWS, n), BF16)
    scratch += both(lambda n, r, h: (4, MEMB, ROWS, n), BF16)
    scratch += both(lambda n, r, h: (2, 4, ROWS, n // 2), BF16)
    scratch += both(lambda n, r, h: (2, 4, ROWS, n // 2), BF16)
    scratch += both(lambda n, r, h: (TN * r, h), BF16)
    scratch += both(lambda n, r, h: (h, TN * r), BF16)
    scratch += both(lambda n, r, h: (S * ROWS, n), BF16)
    scratch += [
        dma((10,)), dma((S,)),
        dma((2, 4)), dma((2, 4)), dma((3,)), dma((3,)),
        dma((2, YN - 1)), dma((2, YN - 1)), dma((2, TN - 1)), dma((2, TN - 1)),
        dma((2, TN - 1)), dma((2, TN - 1)), dma((2, YN - 1)), dma((2, YN - 1)),
        dma((2, 4)), dma((2, 4)), dma((2, YN + 1)), dma((2, YN + 1)),
    ]
    return pl.pallas_call(
        kernel,
        out_shape=(jax.ShapeDtypeStruct((MEMB, S, ROWS, LON), F32), jax.ShapeDtypeStruct((S, ROWS, LON), F32)),
        in_specs=[pl.BlockSpec(memory_space=pltpu.HBM)] * len(inputs),
        out_specs=(pl.BlockSpec(memory_space=pltpu.VMEM),) * 2,
        scratch_shapes=scratch,
        compiler_params=pltpu.CompilerParams(collective_id=0, has_side_effects=True, vmem_limit_bytes=40 << 20),
        name="hessian",
    )(*[pltpu.with_memory_space_constraint(v, pltpu.HBM) for v in inputs])


def solution(mesh):
    in_specs = (
        P("mem", None, "band", None),
        P(None, "band", None),
        P("mem", None, None, "band"),
        P(None, None, "band"),
        P(),
        P(),
        P(None, None, "mem", "band"),
        P("mem", "band"),
        P(None, "mem", "band"),
        P(),
        P(),
    )
    out_specs = (P("mem", None, "band", None), P(None, "band", None))
    return jax.shard_map(shards, mesh=mesh, in_specs=in_specs, out_specs=out_specs, check_vma=False)
```
